32 devices in a mesh: dp: 2 (over core), blk: 4 (over y, x), head: 4 (over z).
Axes of the slice: x: 2, y: 2, z: 4, core: 2. Of those that a mesh axis runs over, the one named last changes fastest.
Arguments:
- activations: bfloat16 [2, 2, 2048, 1536], P(None, 'dp', ('blk', 'head')), may hold values from -6 to 6
- segments: int32 [2, 2, 2048], P(None, 'dp', 'blk'), may hold values from 0 to 15, never falling along the last dimension, each value on 1 to 1024 neighbouring positions
- cotangent: bfloat16 [2, 2, 2048, 1536], P(None, 'dp', ('blk', 'head')), may hold values from -6 to 6
- norm_gain_one: bfloat16 [1536], P(('dp', 'blk')), may hold values from 0.5 to 1.5
- query_weight: bfloat16 [1536, 1536], P(('dp', 'blk')), may hold values from -0.15625 to 0.15625
- key_weight: bfloat16 [1536, 768], P(('dp', 'blk')), may hold values from -0.15625 to 0.15625
- value_weight: bfloat16 [1536, 768], P(('dp', 'blk')), may hold values from -0.15625 to 0.15625
- output_weight: bfloat16 [1536, 1536], P(('dp', 'blk')), may hold values from -1.25 to 1.25
- norm_gain_two: bfloat16 [1536], P(('dp', 'blk')), may hold values from 0.5 to 1.5
- gate_weight: bfloat16 [1536, 4096], P(('dp', 'blk')), may hold values from -0.15625 to 0.15625
- up_weight: bfloat16 [1536, 4096], P(('dp', 'blk')), may hold values from -0.15625 to 0.15625
- down_weight: bfloat16 [4096, 1536], P(('dp', 'blk')), may hold values from -0.09375 to 0.09375
Outputs:
- block_out: bfloat16 [2, 2, 2048, 1536], P(None, 'dp', ('blk', 'head'))
- grad_input: bfloat16 [2, 2, 2048, 1536], P(None, 'dp', ('blk', 'head'))
- grad_gain_one: float32 [1536], P(('dp', 'blk'))
- grad_query: float32 [1536, 1536], P(('dp', 'blk'))
- grad_key: float32 [1536, 768], P(('dp', 'blk'))
- grad_value: float32 [1536, 768], P(('dp', 'blk'))
- grad_output: float32 [1536, 1536], P(('dp', 'blk'))
- grad_gain_two: float32 [1536], P(('dp', 'blk'))
- grad_gate: float32 [1536, 4096], P(('dp', 'blk'))
- grad_up: float32 [1536, 4096], P(('dp', 'blk'))
- grad_down: float32 [4096, 1536], P(('dp', 'blk'))
The draws below stay inside these ranges and needn't reach their ends.
Inputs may be any that keep to these rules, and one draw needn't show every extreme that they name: `segments`: along each sequence the segment numbers never fall and every number is used; a document has at most 1024 tokens, and in every sequence one has exactly that many.
All inputs are finite; a program needn't handle non-finite values.
Results may differ from the reference program's by a relative error of at most 0.023.
Values may be sent and summed in bfloat16 or wider, within the bound.
No kernel may reach another device: no remote copies, remote signals or barrier semaphores. Data moves between devices by JAX's collectives and lax.ppermute only.
A program may use at most 320 MiB of HBM per device.

```python
import math
import jax
import jax.numpy as jnp
import numpy as np
from jax import lax

D = 1536
QH = 16
KVH = 8
HD = 96
FF = 4096
MB = 2
DOCS = 16
SEQS = 2
SPAN = 512
SEQ = 2048


def shard_levels(rng, extent, split, smallest, top_value):
    def one(axis_at, blocks):
        heights = jax.random.uniform(jax.random.fold_in(jax.random.fold_in(rng, 6), axis_at), (blocks,), jnp.float32, smallest / len(split), top_value / len(split))
        return jnp.repeat(jnp.exp(heights), extent[axis_at] // blocks).reshape((-1,) + (1,) * (len(extent) - axis_at - 1))

    level = one(*split[0])
    for cut in split[1:]:
        level = level * one(*cut)
    return level


def length_profile(number_of, total, bound, slope):
    portions = [(1 << 20) // math.isqrt(standing ** slope) + 1 for standing in range(2, number_of + 1)]
    spare, holding = total - bound - (number_of - 1), [1] * (number_of - 1)
    while spare > 0:
        free = [i for i in range(number_of - 1) if holding[i] < bound]
        mass, remaining = sum([portions[i] for i in free]), spare
        for i in free:
            addition = min(bound - holding[i], max(1, remaining * portions[i] // mass), spare)
            holding[i] = holding[i] + addition
            spare = spare - addition
    return np.array([bound] + holding)


def uneven_parts(own_key, number_of, total, bound, skew):
    if number_of == 2:
        one = jax.random.randint(own_key, (), max(1, total - bound), min(bound, total - 1) + 1)
        return jnp.stack([one, total - one])
    tallies = jnp.asarray(length_profile(number_of, total, bound, skew), jnp.int32)
    couples = (number_of - 1) // 2
    donor, taker = tallies[1:1 + 2 * couples:2], tallies[2:2 + 2 * couples:2]
    room = jnp.minimum(donor - 1, bound - taker)
    moved = jax.random.randint(jax.random.fold_in(own_key, 1), (couples,), 0, 1 << 20) % (room + 1)
    tallies = tallies.at[1:1 + 2 * couples:2].set(donor - moved).at[2:2 + 2 * couples:2].set(taker + moved)
    return tallies[jax.random.permutation(jax.random.fold_in(own_key, 2), number_of)]


def bell_draw(own_key, dims, scale, limit, split=(), kind=jnp.bfloat16):
    values = scale * jax.random.normal(own_key, dims, jnp.float32)
    if split:
        values = values * shard_levels(own_key, dims, split, -0.22, 0.18)
    return jnp.clip(values, -limit, limit).astype(kind)


def setup_inputs(seed: int = 0) -> dict:
    key_of = jax.random.split(jax.random.key(seed), 13)
    return {
        "activations": bell_draw(key_of[0], (MB, SEQS, SEQ, D), 1.0, 6.0, ((1, 2), (2, 16))),
        "segments": jax.vmap(lambda own: jnp.searchsorted(jnp.cumsum(uneven_parts(own, DOCS, SEQ, SEQ // 2, 2)), jnp.arange(SEQ), side="right"))(jax.random.split(key_of[1], MB * SEQS)).reshape((MB, SEQS, SEQ)).astype(jnp.int32),
        "cotangent": bell_draw(key_of[2], (MB, SEQS, SEQ, D), 1.0, 6.0, ((1, 2), (2, 16))),
        "norm_gain_one": jnp.clip(1.0 + 0.1 * jax.random.normal(key_of[3], (D,), jnp.float32), 0.5, 1.5).astype(jnp.bfloat16),
        "query_weight": bell_draw(key_of[4], (D, QH * HD), D ** -0.5, 0.15625, ((0, 8),)),
        "key_weight": bell_draw(key_of[5], (D, KVH * HD), D ** -0.5, 0.15625, ((0, 8),)),
        "value_weight": bell_draw(key_of[6], (D, KVH * HD), D ** -0.5, 0.15625, ((0, 8),)),
        "output_weight": bell_draw(key_of[7], (QH * HD, D), (QH * HD // 64) ** -0.5, 1.25, ((0, 8),)),
        "norm_gain_two": jnp.clip(1.0 + 0.1 * jax.random.normal(key_of[8], (D,), jnp.float32), 0.5, 1.5).astype(jnp.bfloat16),
        "gate_weight": bell_draw(key_of[9], (D, FF), D ** -0.5, 0.15625, ((0, 8),)),
        "up_weight": bell_draw(key_of[10], (D, FF), D ** -0.5, 0.15625, ((0, 8),)),
        "down_weight": bell_draw(key_of[11], (FF, D), FF ** -0.5, 0.09375, ((0, 8),)),
    }


@jax.custom_vjp
def low(v):
    return lax.optimization_barrier(v.astype(jnp.bfloat16)).astype(jnp.float32)

@jax.custom_vjp
def low_back(v):
    return v

def low_keep(v):
    return (low(v), None)

def low_pass(kept, grad):
    return (grad,)

def back_keep(v):
    return (v, None)

def back_low(kept, grad):
    return (low(grad),)
low.defvjp(low_keep, low_pass)
low_back.defvjp(back_keep, back_low)
EPS = 1e-05
NEG = -1e+30

def high_dot(left, right):
    return jnp.dot(left, right, precision=lax.Precision.HIGHEST)

def rms_apply(values, gain):
    return values * lax.rsqrt(lax.optimization_barrier(jnp.mean(values * values, -1, keepdims=True)) + EPS) * gain

def attend(queries, keys, values, seg_ids):
    length = queries.shape[0]
    share = QH // KVH
    keys_wide = jnp.repeat(keys, share, axis=1)
    values_wide = jnp.repeat(values, share, axis=1)
    block_rows = min(SPAN, 1024)
    count_blocks = length // block_rows
    positions = jnp.arange(length, dtype=jnp.int32)
    scale = 1.0 / HD ** 0.5

    def one_block(inputs):
        query_blk, query_pos, query_seg = inputs
        scores = jnp.einsum('qhd,khd->hqk', query_blk, keys_wide, precision=lax.Precision.HIGHEST) * scale
        scores = low_back(scores)
        allowed = (positions[None, :] <= query_pos[:, None]) & (seg_ids[None, :] == query_seg[:, None])
        scores = jnp.where(allowed[None], scores, NEG)
        probs = low(jax.nn.softmax(scores, axis=-1))
        return jnp.einsum('hqk,khd->qhd', probs, values_wide, precision=lax.Precision.HIGHEST)
    result = lax.map(jax.checkpoint(one_block), (queries.reshape(count_blocks, block_rows, QH, HD), positions.reshape(count_blocks, block_rows), seg_ids.reshape(count_blocks, block_rows)))
    return result.reshape(length, QH, HD)

def layer(x_seq, seg_ids, params):
    gain_one, query_w, key_w, value_w, out_w, gain_two, gate_w, up_w, down_w = params
    length = x_seq.shape[0]
    input_one = low(rms_apply(x_seq, gain_one))
    queries = low(low_back(high_dot(input_one, query_w))).reshape(length, QH, HD)
    keys = low(low_back(high_dot(input_one, key_w))).reshape(length, KVH, HD)
    values = low(low_back(high_dot(input_one, value_w))).reshape(length, KVH, HD)
    attn = attend(queries, keys, values, seg_ids)
    attn = low(low_back(attn)).reshape(length, QH * HD)
    x_mid = x_seq + low_back(high_dot(attn, out_w))
    input_two = low(rms_apply(x_mid, gain_two))
    gate_val = low_back(high_dot(input_two, gate_w))
    up_val = low_back(high_dot(input_two, up_w))
    hidden = low(jax.nn.silu(gate_val) * up_val)
    return x_mid + low_back(high_dot(hidden, down_w))

def reference(activations, segments, cotangent, norm_gain_one, query_weight, key_weight, value_weight, output_weight, norm_gain_two, gate_weight, up_weight, down_weight):
    params = tuple((item.astype(jnp.float32) for item in (norm_gain_one, query_weight, key_weight, value_weight, output_weight, norm_gain_two, gate_weight, up_weight, down_weight)))
    count_seqs = MB * SEQS
    x_all = activations.reshape(count_seqs, SEQ, D)
    seg_all = segments.reshape(count_seqs, SEQ)
    cot_all = cotangent.reshape(count_seqs, SEQ, D)

    def one_seq(totals, item):
        x_seq, seg_ids, cot_seq = item
        result, pull = jax.vjp(lambda x_val, p_val: layer(x_val, seg_ids, p_val), x_seq.astype(jnp.float32), params)
        grad_x, grad_params = pull(cot_seq.astype(jnp.float32))
        totals = jax.tree.map(lambda left, right: left + right, totals, grad_params)
        return (totals, (result.astype(jnp.bfloat16), grad_x.astype(jnp.bfloat16)))
    zeros = jax.tree.map(jnp.zeros_like, params)
    totals, (results, grads_x) = lax.scan(one_seq, zeros, (x_all, seg_all, cot_all))
    block_out = results.reshape(MB, SEQS, SEQ, D)
    grad_input = grads_x.reshape(MB, SEQS, SEQ, D)
    return (block_out, grad_input, totals[0], totals[1], totals[2], totals[3], totals[4], totals[5], totals[6], totals[7], totals[8])
```

```python
import functools
import math

import jax
import jax.numpy as jnp
from jax import lax
from jax.experimental import pallas as pl
from jax.experimental.pallas import tpu as pltpu
from jax.sharding import PartitionSpec as P

D = 1536
QH = 16
KVH = 8
HD = 96
HP = 128
FF = 4096
EPS = 1e-05
NEG = -1e30
BLK = 256
BF = jnp.bfloat16
F32 = jnp.float32


def dot(left, right, dims=((1,), (0,))):
    return lax.dot_general(left, right, (dims, ((), ())), preferred_element_type=F32)


def normalize(values):
    factor = lax.rsqrt(jnp.mean(values * values, -1, keepdims=True) + EPS)
    return values * factor, factor


def norm_back(grad_norm, gain, normed, factor):
    scaled = grad_norm * gain
    return factor * (scaled - normed * jnp.mean(scaled * normed, -1, keepdims=True))


def rows_of(index):
    return pl.ds(pl.multiple_of(index * BLK, BLK), BLK)


def allowed_pairs(qpos, qseg, kpos, kseg):
    return (kpos <= qpos) & (kseg == qseg)


def attn_fwd_kernel(need, q_ref, kv_ref, qp_ref, qs_ref, kp_ref, ks_ref, o_ref, lse_ref, m_sc, l_sc, acc_sc):
    scale = 1.0 / math.sqrt(HD)
    n_q, n_k = q_ref.shape[0] // BLK, kv_ref.shape[0] // BLK

    def one_query(i, _):
        qr = rows_of(i)
        m_sc[...] = jnp.full_like(m_sc, NEG)
        l_sc[...] = jnp.zeros_like(l_sc)
        acc_sc[...] = jnp.zeros_like(acc_sc)
        qpos, qseg = qp_ref[qr, :], qs_ref[qr, :]

        def one_key(j, _):
            @pl.when(need[i, j] != 0)
            def _():
                kr = rows_of(j)
                ok = allowed_pairs(qpos, qseg, kp_ref[j], ks_ref[j])
                k, v = kv_ref[kr, 0:HP], kv_ref[kr, HP : 2 * HP]
                for g in range(2):
                    q = q_ref[qr, g * HP : (g + 1) * HP]
                    s = jnp.where(ok, dot(q, k, ((1,), (1,))) * scale, NEG)
                    m_old = m_sc[g]
                    m_new = jnp.maximum(m_old, jnp.max(s, -1, keepdims=True))
                    p = jnp.where(ok, jnp.exp(s - m_new), 0.0)
                    decay = jnp.exp(m_old - m_new)
                    l_sc[g] = l_sc[g] * decay + jnp.sum(p, -1, keepdims=True)
                    acc_sc[g] = acc_sc[g] * decay + dot(p.astype(BF), v)
                    m_sc[g] = m_new

            return 0

        lax.fori_loop(0, n_k, one_key, 0)
        for g in range(2):
            o_ref[qr, g * HP : (g + 1) * HP] = (acc_sc[g] / l_sc[g]).astype(BF)
            lse_ref[qr, g : g + 1] = m_sc[g] + jnp.log(l_sc[g])
        return 0

    lax.fori_loop(0, n_q, one_query, 0)


def attn_bwd_kernel(
    need, q_ref, kv_ref, qp_ref, qs_ref, kp_ref, ks_ref, o_ref, lse_ref, do_ref, dq_ref, dkv_ref, dq_sc, dk_sc, dv_sc
):
    scale = 1.0 / math.sqrt(HD)
    n_q, n_k = q_ref.shape[0] // BLK, kv_ref.shape[0] // BLK
    dk_sc[...] = jnp.zeros_like(dk_sc)
    dv_sc[...] = jnp.zeros_like(dv_sc)

    def as_row(col):
        return jnp.broadcast_to(col, (BLK, HP)).T[0:1, :]

    def one_query(i, _):
        qr = rows_of(i)
        dq_sc[...] = jnp.zeros_like(dq_sc)
        qpos, qseg = qp_ref[i], qs_ref[i]
        lse, delta = [], []
        for g in range(2):
            cols = slice(g * HP, (g + 1) * HP)
            lse.append(as_row(lse_ref[qr, g : g + 1]))
            prod = do_ref[qr, cols].astype(F32) * o_ref[qr, cols].astype(F32)
            delta.append(as_row(jnp.sum(prod, -1, keepdims=True)))

        def one_key(j, _):
            @pl.when(need[i, j] != 0)
            def _():
                kr = rows_of(j)
                ok = allowed_pairs(qpos, qseg, kp_ref[kr, :], ks_ref[kr, :])
                k, v = kv_ref[kr, 0:HP], kv_ref[kr, HP : 2 * HP]
                for g in range(2):
                    cols = slice(g * HP, (g + 1) * HP)
                    q, do = q_ref[qr, cols], do_ref[qr, cols]
                    s = dot(k, q, ((1,), (1,))) * scale
                    p = jnp.where(ok, jnp.exp(s - lse[g]), 0.0)
                    dp = dot(v, do, ((1,), (1,)))
                    ds = (p * (dp - delta[g])).astype(BF)
                    dv_sc[kr, :] += dot(p.astype(BF), do)
                    dk_sc[kr, :] += dot(ds, q)
                    dq_sc[g] += dot(ds, k, ((0,), (0,)))

            return 0

        lax.fori_loop(0, n_k, one_key, 0)
        for g in range(2):
            dq_ref[qr, g * HP : (g + 1) * HP] = (dq_sc[g] * scale).astype(BF)
        return 0

    lax.fori_loop(0, n_q, one_query, 0)
    dkv_ref[:, 0:HP] = (dk_sc[...] * scale).astype(BF)
    dkv_ref[:, HP : 2 * HP] = dv_sc[...].astype(BF)


def in_vmem(count):
    return [pl.BlockSpec(memory_space=pltpu.SMEM)] + [pl.BlockSpec(memory_space=pltpu.VMEM)] * count


def attn_cost(n_q, n_k, products):
    return pl.CostEstimate(
        flops=products * n_q * n_k * 2 * HP * 2 // 2, transcendentals=n_q * n_k, bytes_accessed=(n_q + n_k) * HP * 16
    )


def attend(need, q, kv, qpos, qseg, kpos, kseg):
    n_q, n_k = q.shape[0], kv.shape[0]
    return pl.pallas_call(
        attn_fwd_kernel,
        out_shape=(jax.ShapeDtypeStruct((n_q, 2 * HP), BF), jax.ShapeDtypeStruct((n_q, 2), F32)),
        in_specs=in_vmem(6),
        out_specs=(pl.BlockSpec(memory_space=pltpu.VMEM),) * 2,
        scratch_shapes=[pltpu.VMEM((2, BLK, 1), F32), pltpu.VMEM((2, BLK, 1), F32), pltpu.VMEM((2, BLK, HP), F32)],
        compiler_params=pltpu.CompilerParams(vmem_limit_bytes=40 << 20),
        cost_estimate=attn_cost(n_q, n_k, 2),
        name="attn_fwd",
    )(need, q, kv, qpos[:, None], qseg[:, None], kpos.reshape(-1, 1, BLK), kseg.reshape(-1, 1, BLK))


def attend_back(need, q, kv, qpos, qseg, kpos, kseg, o, lse, do):
    n_q, n_k = q.shape[0], kv.shape[0]
    return pl.pallas_call(
        attn_bwd_kernel,
        out_shape=(jax.ShapeDtypeStruct((n_q, 2 * HP), BF), jax.ShapeDtypeStruct((n_k, 2 * HP), BF)),
        in_specs=in_vmem(9),
        out_specs=(pl.BlockSpec(memory_space=pltpu.VMEM),) * 2,
        scratch_shapes=[pltpu.VMEM((2, BLK, HP), F32), pltpu.VMEM((n_k, HP), F32), pltpu.VMEM((n_k, HP), F32)],
        compiler_params=pltpu.CompilerParams(vmem_limit_bytes=48 << 20),
        cost_estimate=attn_cost(n_q, n_k, 5),
        name="attn_bwd",
    )(need, q, kv, qpos.reshape(-1, 1, BLK), qseg.reshape(-1, 1, BLK), kpos[:, None], kseg[:, None], o, lse, do)


def swap(value, axis, mask):
    return lax.ppermute(value, axis, [(i, i ^ mask) for i in range(lax.axis_size(axis))])


def gather_rel(value):
    n_blk = lax.axis_size("blk")
    mine = jnp.stack([value] + [swap(value, "blk", k) for k in range(1, n_blk)])
    return jnp.stack([mine, swap(mine, "dp", 1)])


def scatter_rel(parts):
    n_blk = lax.axis_size("blk")
    local = parts[0] + swap(parts[1].astype(BF), "dp", 1).astype(F32)
    total = local[0]
    for k in range(1, n_blk):
        total = total + swap(local[k].astype(BF), "blk", k).astype(F32)
    return total


def exchange_rel(parts):
    n_blk = lax.axis_size("blk")
    both = jnp.stack([parts[0], swap(parts[1], "dp", 1)], 1)
    return jnp.stack([both[0]] + [swap(both[k], "blk", k) for k in range(1, n_blk)], 1)


def rel_to_abs(value, reverse=False):
    n_blk = lax.axis_size("blk")
    mine = lax.axis_index("dp") * n_blk + lax.axis_index("blk")
    flat = value.reshape((2 * n_blk,) + value.shape[(1 if reverse else 2) :])
    out = jnp.stack([lax.dynamic_index_in_dim(flat, i ^ mine, 0, keepdims=False) for i in range(2 * n_blk)])
    return out.reshape((2, n_blk) + out.shape[1:]) if reverse else out


def per_device(
    activations,
    segments,
    cotangent,
    norm_gain_one,
    query_weight,
    key_weight,
    value_weight,
    output_weight,
    norm_gain_two,
    gate_weight,
    up_weight,
    down_weight,
):
    n_blk, n_head = lax.axis_size("blk"), lax.axis_size("head")
    n_plane = 2 * n_blk
    assert lax.axis_size("dp") == 2 and activations.shape[0] == 2 and n_plane == KVH
    sub = n_head // 4
    tok = activations.shape[2]
    span = tok * n_head
    own = 2 * tok
    rows = n_plane * own
    my_dp, my_blk, my_head = (lax.axis_index(name) for name in ("dp", "blk", "head"))
    my_seq, my_sub = my_head // sub, my_head % sub

    def routes(k):
        pairs = []
        for core in range(2):
            for head in range(n_head):
                seq_part, sub_part = head // sub, head % sub
                target = 2 * (k ^ (seq_part & 1)) + core
                pairs.append((core * n_head + head, (seq_part >> 1) * n_head + target * sub + sub_part))
        return pairs

    def to_plane(value):
        parts = []
        for k in range(2):
            piece = lax.dynamic_index_in_dim(value, k ^ (my_seq & 1), 0, keepdims=False)
            parts.append(lax.ppermute(piece, ("dp", "head"), routes(k)))
        return jnp.concatenate(parts, 0)

    def from_plane(value):
        parts = []
        for k in range(2):
            back = [(b, a) for a, b in routes(k)]
            parts.append(lax.ppermute(value[k * tok : (k + 1) * tok], ("dp", "head"), back))
        odd = (my_seq & 1) == 1
        return jnp.stack([jnp.where(odd, parts[1], parts[0]), jnp.where(odd, parts[0], parts[1])])

    x = to_plane(activations[:, 0]).astype(F32)
    cot = to_plane(cotangent[:, 0])

    small = jnp.concatenate([norm_gain_one, norm_gain_two, segments[:, 0].reshape(-1).astype(BF)])[None]
    small = rel_to_abs(gather_rel(small))[:, 0]
    n_gain = D // n_plane
    gain_one = small[:, :n_gain].reshape(D).astype(F32)
    gain_two = small[:, n_gain : 2 * n_gain].reshape(D).astype(F32)
    seg_all = small[:, 2 * n_gain :].reshape(2, n_blk, 2, span)
    seg_seq = lax.dynamic_index_in_dim(seg_all, my_seq & 1, 0, keepdims=False)
    seg_seq = lax.dynamic_index_in_dim(seg_seq, my_seq >> 1, 1, keepdims=False)
    chunks = seg_seq.astype(jnp.int32).reshape(n_blk * n_head, tok)

    def chunk_ids(sub_index):
        ids = []
        for core in range(2):
            for blk in range(n_blk):
                for k in range(2):
                    seq_part = 2 * (my_dp ^ core) + ((my_seq >> 1) ^ k)
                    ids.append((my_blk ^ blk) * n_head + seq_part * sub + sub_index)
        return ids

    def pos_seg(sub_index):
        ids = chunk_ids(sub_index)
        lane = jnp.arange(tok, dtype=jnp.int32)
        pos = jnp.concatenate([i * tok + lane for i in ids])
        seg = jnp.concatenate([lax.dynamic_index_in_dim(chunks, i, 0, keepdims=False) for i in ids])
        return pos, seg

    qpos, qseg = pos_seg(my_sub)
    if sub == 1:
        kpos, kseg = qpos, qseg
    else:
        every = [pos_seg(i) for i in range(sub)]
        kpos, kseg = (jnp.concatenate([e[i] for e in every]) for i in range(2))
    blocked = lambda v: v.reshape(-1, BLK)
    qb, qsb, kb, ksb = blocked(qpos), blocked(qseg), blocked(kpos), blocked(kseg)
    need = (
        (jnp.min(kb, 1)[None, :] <= jnp.max(qb, 1)[:, None])
        & (jnp.min(ksb, 1)[None, :] <= jnp.max(qsb, 1)[:, None])
        & (jnp.max(ksb, 1)[None, :] >= jnp.min(qsb, 1)[:, None])
    ).astype(jnp.int32)

    def column_parts(weight):
        width = weight.shape[1] // n_plane
        return weight.reshape(weight.shape[0], n_plane, width).transpose(1, 0, 2)

    qkv_parts = jnp.concatenate([column_parts(w) for w in (query_weight, key_weight, value_weight)], -1)
    qkv_w = rel_to_abs(exchange_rel(rel_to_abs(qkv_parts, True))).reshape(D, 4 * HD)
    pad_heads = lambda v: jnp.pad(v.reshape(v.shape[0], -1, HD), ((0, 0), (0, 0), (0, HP - HD))).reshape(v.shape[0], -1)
    qkv_w = pad_heads(qkv_w)
    out_pad = jnp.pad(output_weight.reshape(2, HD, D), ((0, 0), (0, HP - HD), (0, 0))).reshape(2 * HP, D)
    out_w = gather_rel(out_pad).reshape(n_plane * 2 * HP, D)
    ff_parts = jnp.concatenate([column_parts(w) for w in (gate_weight, up_weight)], -1)
    ff_w = rel_to_abs(exchange_rel(rel_to_abs(ff_parts, True))).reshape(D, 2 * FF // n_plane)
    ff_here = FF // n_plane
    gate_w, up_w = ff_w[:, :ff_here], ff_w[:, ff_here:]

    normed_one, factor_one = normalize(x)
    input_one = (normed_one * gain_one).astype(BF)
    all_one = gather_rel(input_one).reshape(rows, D)
    qkv = dot(all_one, qkv_w).astype(BF)
    q, kv = qkv[:, : 2 * HP], qkv[:, 2 * HP :]
    if sub > 1:
        groups = [[s * sub + i for i in range(sub)] for s in range(4)]
        kv = lax.all_gather(kv, "head", axis=0, tiled=True, axis_index_groups=groups)
    o, lse = attend(need, q, kv, qpos, qseg, kpos, kseg)
    o_tok = exchange_rel(o.reshape(2, n_blk, own, 2 * HP))
    o_tok = o_tok.reshape(n_plane, own, 2 * HP).transpose(1, 0, 2).reshape(own, n_plane * 2 * HP)
    x_mid = x + dot(o_tok, out_w)
    normed_two, factor_two = normalize(x_mid)
    input_two = (normed_two * gain_two).astype(BF)
    all_two = gather_rel(input_two).reshape(rows, D)
    all_cot = gather_rel(cot).reshape(rows, D)
    gate_val = dot(all_two, gate_w)
    up_val = dot(all_two, up_w)
    sigma = jax.nn.sigmoid(gate_val)
    silu_val = gate_val * sigma
    hidden = (silu_val * up_val).astype(BF)
    in_plane = lambda v: v.reshape(2, n_blk, own, D)
    block_out = (x_mid + scatter_rel(in_plane(dot(hidden, down_weight)))).astype(BF)

    grad_hidden = dot(all_cot, down_weight, ((1,), (1,)))
    grad_gate = (grad_hidden * up_val * sigma * (1.0 + gate_val * (1.0 - sigma))).astype(BF)
    grad_up = (grad_hidden * silu_val).astype(BF)
    grad_in_two = scatter_rel(in_plane(dot(grad_gate, gate_w, ((1,), (1,))) + dot(grad_up, up_w, ((1,), (1,)))))
    grad_mid = cot.astype(F32) + norm_back(grad_in_two, gain_two, normed_two, factor_two)
    grad_branch = grad_mid.astype(BF)
    grad_o = dot(grad_branch, out_w, ((1,), (1,))).astype(BF)
    grad_o = exchange_rel(grad_o.reshape(own, 2, n_blk, 2 * HP).transpose(1, 2, 0, 3)).reshape(rows, 2 * HP)
    all_branch = gather_rel(grad_branch).reshape(rows, D)
    dq, dkv = attend_back(need, q, kv, qpos, qseg, kpos, kseg, o, lse, grad_o)
    if sub > 1:
        dkv = lax.psum_scatter(dkv, "head", scatter_dimension=0, tiled=True, axis_index_groups=groups)
    dqkv = jnp.concatenate([dq, dkv], 1)
    grad_in_one = scatter_rel(in_plane(dot(dqkv, qkv_w, ((1,), (1,)))))
    grad_input = grad_mid + norm_back(grad_in_one, gain_one, normed_one, factor_one)

    contract = ((0,), (0,))

    def owned_rows(grad):
        return lax.all_gather(
            lax.psum_scatter(grad.astype(BF), "head", scatter_dimension=0, tiled=True), "head", axis=0, tiled=True
        ).astype(F32)

    def owned_columns(grad):
        width = grad.shape[1]
        part = D // n_plane // n_head
        sent = grad.astype(BF).reshape(n_plane, n_head, part, width).transpose(1, 0, 2, 3)
        mine = lax.psum_scatter(sent.reshape(D, width), "head", scatter_dimension=0, tiled=True)
        moved = exchange_rel(rel_to_abs(mine.reshape(n_plane, part, width), True))
        full = lax.all_gather(moved, "head", axis=0)
        full = rel_to_abs(jnp.moveaxis(full, 0, 2))
        return full.reshape(n_plane, D // n_plane, width).transpose(1, 0, 2).astype(F32)

    grad_down = owned_rows(dot(hidden, all_cot, contract))
    grad_ff = owned_columns(jnp.concatenate([dot(all_two, grad_gate, contract), dot(all_two, grad_up, contract)], 1))
    grad_out = dot(o, all_branch, contract).reshape(2, HP, D)[:, :HD].reshape(2 * HD, D)
    grad_out = owned_rows(grad_out)
    grad_qkv = dot(all_one, dqkv, contract).reshape(D, 4, HP)[:, :, :HD].reshape(D, 4 * HD)
    grad_qkv = owned_columns(grad_qkv)
    flat = lambda v: v.reshape(v.shape[0], -1)
    grad_query = flat(grad_qkv[:, :, : 2 * HD])
    grad_key = flat(grad_qkv[:, :, 2 * HD : 3 * HD])
    grad_value = flat(grad_qkv[:, :, 3 * HD :])
    grad_gate_w = flat(grad_ff[:, :, :ff_here])
    grad_up_w = flat(grad_ff[:, :, ff_here:])

    def gain_grad(gain, *pairs):
        return sum(jnp.sum(w.astype(F32) * g, -1) for w, g in pairs) / gain.astype(F32)

    grad_gain_one = gain_grad(
        norm_gain_one, (query_weight, grad_query), (key_weight, grad_key), (value_weight, grad_value)
    )
    grad_gain_two = gain_grad(norm_gain_two, (gate_weight, grad_gate_w), (up_weight, grad_up_w))
    return (
        from_plane(block_out)[:, None],
        from_plane(grad_input.astype(BF))[:, None],
        grad_gain_one,
        grad_query,
        grad_key,
        grad_value,
        grad_out,
        grad_gain_two,
        grad_gate_w,
        grad_up_w,
        grad_down,
    )


def solution(mesh):
    tokens = P(None, "dp", ("blk", "head"), None)
    vector = P(("dp", "blk"))
    matrix = P(("dp", "blk"), None)
    return jax.shard_map(
        per_device,
        mesh=mesh,
        in_specs=(
            tokens,
            P(None, "dp", "blk"),
            tokens,
            vector,
            matrix,
            matrix,
            matrix,
            matrix,
            vector,
            matrix,
            matrix,
            matrix,
        ),
        out_specs=(tokens, tokens, vector, matrix, matrix, matrix, matrix, vector, matrix, matrix, matrix),
        check_vma=False,
    )
```

```python
import functools
import math

import jax
import jax.numpy as jnp
from jax import lax
from jax.experimental import pallas as pl
from jax.experimental.pallas import tpu as pltpu
from jax.sharding import PartitionSpec as P

D = 1536
QH = 16
KVH = 8
HD = 96
HP = 128
FF = 4096
EPS = 1e-05
NEG = -1e30
BLK = 256
BF = jnp.bfloat16
F32 = jnp.float32


def dot(left, right, dims=((1,), (0,))):
    return lax.dot_general(left, right, (dims, ((), ())), preferred_element_type=F32)


def normalize(values):
    factor = lax.rsqrt(jnp.mean(values * values, -1, keepdims=True) + EPS)
    return values * factor, factor


def norm_back(grad_norm, gain, normed, factor):
    scaled = grad_norm * gain
    return factor * (scaled - normed * jnp.mean(scaled * normed, -1, keepdims=True))


def rows_of(index):
    return pl.ds(pl.multiple_of(index * BLK, BLK), BLK)


def as_column(row):
    return jnp.broadcast_to(row, (HP, BLK)).T[:, 0:1]


def as_row(col):
    return jnp.broadcast_to(col, (BLK, HP)).T[0:1, :]


def keys_to_columns(kp_ref, ks_ref, pos_sc, seg_sc):
    def one(j, _):
        pos_sc[rows_of(j), :] = as_column(kp_ref[j])
        seg_sc[rows_of(j), :] = as_column(ks_ref[j])
        return 0

    lax.fori_loop(0, kp_ref.shape[0], one, 0)


def attn_fwd_kernel(first, need, q_ref, kv_ref, qp_ref, qs_ref, kp_ref, ks_ref, o_ref, lse_ref, m_sc, l_sc, acc_sc, pos_sc, seg_sc):
    scale = 1.0 / math.sqrt(HD)
    n_q, n_k = q_ref.shape[0] // BLK, kv_ref.shape[0] // BLK
    k_cols, v_cols = slice(first, first + HP), slice(first + HP, first + 2 * HP)
    keys_to_columns(kp_ref, ks_ref, pos_sc, seg_sc)

    def one_query(i, _):
        qr = rows_of(i)
        m_sc[...] = jnp.full_like(m_sc, NEG)
        l_sc[...] = jnp.zeros_like(l_sc)
        acc_sc[...] = jnp.zeros_like(acc_sc)
        qpos, qseg = qp_ref[i], qs_ref[i]

        def one_key(j, _):
            @pl.when(need[i, j] != 0)
            def _():
                kr = rows_of(j)
                ok = (pos_sc[kr, :] <= qpos) & (seg_sc[kr, :] == qseg)
                k, v = kv_ref[kr, k_cols], kv_ref[kr, v_cols]
                state = [(m_sc[g], l_sc[g], acc_sc[g], q_ref[qr, g * HP : (g + 1) * HP]) for g in range(2)]
                scores = [jnp.where(ok, dot(k, q, ((1,), (1,))) * scale, NEG) for _, _, _, q in state]
                new = []
                for (m_old, l_old, acc_old, _), s in zip(state, scores):
                    m_new = jnp.maximum(m_old, jnp.max(s, 0, keepdims=True))
                    p = jnp.where(ok, jnp.exp(s - m_new), 0.0)
                    decay = jnp.exp(m_old - m_new)
                    total = l_old * decay + jnp.sum(p, 0, keepdims=True)
                    new.append((m_new, total, acc_old * decay + dot(v, p.astype(BF), ((0,), (0,)))))
                for g in range(2):
                    m_sc[g], l_sc[g], acc_sc[g] = new[g]

            return 0

        lax.fori_loop(0, n_k, one_key, 0)
        for g in range(2):
            o_ref[qr, g * HP : (g + 1) * HP] = (acc_sc[g] / l_sc[g]).T.astype(BF)
            lse_ref[i, g : g + 1, :] = m_sc[g] + jnp.log(l_sc[g])
        return 0

    lax.fori_loop(0, n_q, one_query, 0)


def attn_bwd_kernel(first, need, q_ref, kv_ref, qp_ref, qs_ref, kp_ref, ks_ref, o_ref, lse_ref, do_ref, *rest):
    dq_ref, dkv_ref = rest[0], rest[-6]
    dq_sc, dk_sc, dv_sc, pos_sc, seg_sc = rest[-5:]
    scale = 1.0 / math.sqrt(HD)
    n_q, n_k = q_ref.shape[0] // BLK, kv_ref.shape[0] // BLK
    k_cols, v_cols = slice(first, first + HP), slice(first + HP, first + 2 * HP)
    dk_sc[...] = jnp.zeros_like(dk_sc)
    dv_sc[...] = jnp.zeros_like(dv_sc)
    keys_to_columns(kp_ref, ks_ref, pos_sc, seg_sc)

    def one_query(i, _):
        qr = rows_of(i)
        dq_sc[...] = jnp.zeros_like(dq_sc)
        qpos, qseg = qp_ref[i], qs_ref[i]
        lse, delta = [], []
        for g in range(2):
            cols = slice(g * HP, (g + 1) * HP)
            lse.append(lse_ref[i, g : g + 1, :])
            prod = do_ref[qr, cols].astype(F32) * o_ref[qr, cols].astype(F32)
            delta.append(as_row(jnp.sum(prod, -1, keepdims=True)))

        def one_key(j, _):
            @pl.when(need[i, j] != 0)
            def _():
                kr = rows_of(j)
                ok = (pos_sc[kr, :] <= qpos) & (seg_sc[kr, :] == qseg)
                k, v = kv_ref[kr, k_cols], kv_ref[kr, v_cols]
                qs = [q_ref[qr, g * HP : (g + 1) * HP] for g in range(2)]
                dos = [do_ref[qr, g * HP : (g + 1) * HP] for g in range(2)]
                scores = [dot(k, q, ((1,), (1,))) * scale for q in qs]
                dps = [dot(v, do, ((1,), (1,))) for do in dos]
                dv, dk = dv_sc[kr, :], dk_sc[kr, :]
                dqs = []
                for g in range(2):
                    p = jnp.where(ok, jnp.exp(scores[g] - lse[g]), 0.0)
                    ds = (p * (dps[g] - delta[g])).astype(BF)
                    dv = dv + dot(p.astype(BF), dos[g])
                    dk = dk + dot(ds, qs[g])
                    dqs.append(dot(ds, k, ((0,), (0,))))
                dv_sc[kr, :], dk_sc[kr, :] = dv, dk
                for g in range(2):
                    dq_sc[g] += dqs[g]

            return 0

        lax.fori_loop(0, n_k, one_key, 0)
        for g in range(2):
            dq_ref[qr, g * HP : (g + 1) * HP] = (dq_sc[g] * scale).astype(BF)
        return 0

    lax.fori_loop(0, n_q, one_query, 0)
    dkv_ref[:, k_cols] = (dk_sc[...] * scale).astype(BF)
    dkv_ref[:, v_cols] = dv_sc[...].astype(BF)


def in_vmem(count):
    return [pl.BlockSpec(memory_space=pltpu.SMEM)] + [pl.BlockSpec(memory_space=pltpu.VMEM)] * count


def attn_cost(n_q, n_k, products):
    return pl.CostEstimate(
        flops=6 * products * n_q * n_k * 2 * HP, transcendentals=n_q * n_k * 2, bytes_accessed=(n_q + n_k) * HP * 16
    )


def attend(need, q, kv, qpos, qseg, kpos, kseg):
    first, kv = (2 * HP, q) if kv is None else (0, kv)
    n_q, n_k = q.shape[0], kv.shape[0]
    return pl.pallas_call(
        functools.partial(attn_fwd_kernel, first),
        out_shape=(jax.ShapeDtypeStruct((n_q, 2 * HP), BF), jax.ShapeDtypeStruct((n_q // BLK, 2, BLK), F32)),
        in_specs=in_vmem(6),
        out_specs=(pl.BlockSpec(memory_space=pltpu.VMEM),) * 2,
        scratch_shapes=[pltpu.VMEM((2, 1, BLK), F32)] * 2 + [pltpu.VMEM((2, HP, BLK), F32)] + [pltpu.VMEM((n_k, 1), F32)] * 2,
        compiler_params=pltpu.CompilerParams(vmem_limit_bytes=40 << 20),
        cost_estimate=attn_cost(n_q, n_k, 2),
        name="attn_fwd",
    )(need, q, kv, qpos, qseg, kpos, kseg)


def attend_back(need, q, kv, qpos, qseg, kpos, kseg, o, lse, do):
    joint = kv is None
    first, kv = (2 * HP, q) if joint else (0, kv)
    n_q, n_k = q.shape[0], kv.shape[0]
    shapes = [jax.ShapeDtypeStruct((n_q, 4 * HP), BF)] if joint else [jax.ShapeDtypeStruct((n, 2 * HP), BF) for n in (n_q, n_k)]
    return pl.pallas_call(
        functools.partial(attn_bwd_kernel, first),
        out_shape=shapes,
        in_specs=in_vmem(9),
        out_specs=[pl.BlockSpec(memory_space=pltpu.VMEM)] * len(shapes),
        scratch_shapes=[pltpu.VMEM((2, BLK, HP), F32)] + [pltpu.VMEM((n_k, HP), F32)] * 2 + [pltpu.VMEM((n_k, 1), F32)] * 2,
        compiler_params=pltpu.CompilerParams(vmem_limit_bytes=48 << 20),
        cost_estimate=attn_cost(n_q, n_k, 5),
        name="attn_bwd",
    )(need, q, kv, qpos, qseg, kpos, kseg, o, lse, do)


def whole(count):
    return [pl.BlockSpec(memory_space=pltpu.VMEM)] * count


def place_call(kernel, out_shape, ids, *values, name, scratch=()):
    moved = sum(v.size * v.dtype.itemsize for v in values)
    return pl.pallas_call(
        kernel,
        out_shape=out_shape,
        in_specs=[pl.BlockSpec(memory_space=pltpu.SMEM)] + whole(len(values)),
        out_specs=jax.tree.map(lambda _: pl.BlockSpec(memory_space=pltpu.VMEM), out_shape),
        scratch_shapes=scratch,
        compiler_params=pltpu.CompilerParams(vmem_limit_bytes=40 << 20),
        cost_estimate=pl.CostEstimate(flops=0, transcendentals=0, bytes_accessed=2 * moved),
        name=name,
    )(ids, *values)


def pack_qkv_kernel(ids, q_ref, k_ref, v_ref, small_ref, out_ref):
    rows = q_ref.shape[0]
    zero = jnp.zeros((rows, HP - HD), BF)
    for dev in range(KVH):
        slot = ids[0] ^ dev
        heads = [(q_ref, 2 * dev), (q_ref, 2 * dev + 1), (k_ref, dev), (v_ref, dev)]
        for i, (ref, head) in enumerate(heads):
            piece = ref[:, head * HD : (head + 1) * HD]
            out_ref[slot, :rows, i * HP : (i + 1) * HP] = jnp.concatenate([piece, zero], 1)
        out_ref[slot, rows:, :] = small_ref[...]


def pack_ff_kernel(ids, gate_ref, up_ref, out_ref):
    width = gate_ref.shape[1] // KVH
    for dev in range(KVH):
        slot = ids[0] ^ dev
        for i, ref in enumerate((gate_ref, up_ref)):
            out_ref[slot, :, i * width : (i + 1) * width] = ref[:, dev * width : (dev + 1) * width]


def head_kernel(n_blk, ids, *refs):
    got, x_refs = refs[:n_blk], refs[n_blk : n_blk + 2]
    w_ref, seg_ref, gain_ref, x_ref, n_ref, small_sc = refs[n_blk + 2 :]
    n_rows = w_ref.shape[0] // (2 * n_blk)
    for k, ref in enumerate(got):
        for core in range(2):
            at = pl.multiple_of((ids[0] ^ (core * n_blk + k)) * n_rows, 16)
            w_ref[pl.ds(at, n_rows), :] = ref[core, :n_rows, :]
            small_sc[core * n_blk + k] = ref[core, n_rows:, :]
    gains = [[], []]
    for dev in range(2 * n_blk):
        small = small_sc[ids[0] ^ dev]
        seg_ref[dev] = small
        small = small.astype(F32)
        for i in range(2):
            gains[i].append(small[i : i + 1, :n_rows])
    for i in range(2):
        gain_ref[i] = jnp.concatenate(gains[i], 1)
    tok = x_refs[0].shape[0]
    for i, ref in enumerate(x_refs):
        x = ref[...]
        x_ref[i * tok : (i + 1) * tok, :] = x
        x = x.astype(F32)
        factor = lax.rsqrt(jnp.mean(x * x, -1, keepdims=True) + EPS)
        n_ref[i * tok : (i + 1) * tok, :] = (x * factor * gain_ref[0]).astype(BF)


def unpack_ff_kernel(ids, in_ref, gate_ref, up_ref):
    n_head, n_slot, part, width = in_ref.shape
    for head in range(n_head):
        for slot in range(n_slot):
            at = pl.ds(pl.multiple_of(((ids[0] ^ slot) * n_head + head) * part, 16), part)
            gate_ref[at, :] = in_ref[head, slot, :, : width // 2]
            up_ref[at, :] = in_ref[head, slot, :, width // 2 :]


def chunk_heads(ids, count):
    if count == 7:
        return [(ids[1] + (i - 3), (ids[1] + (i - 3) >= 0) & (ids[1] + (i - 3) < 4)) for i in range(7)]
    return [(i, None) for i in range(count)]


def place_chunk(ok, body):
    if ok is None:
        body()
    else:
        pl.when(ok)(body)


def place_rows_kernel(ids, *refs):
    out_ref = refs[-1]
    part = refs[0].shape[0]
    for ref, (head, ok) in zip(refs[:-1], chunk_heads(ids, len(refs) - 1)):

        def body():
            out_ref[pl.ds(pl.multiple_of(head * part, 16), part), :] = ref[...].astype(F32)

        place_chunk(ok, body)


def place_columns_kernel(widths, count, ids, *refs):
    chunks, outs = refs[:count], refs[count:]
    n_slot, part = chunks[0].shape[:2]
    for ref, (head, ok) in zip(chunks, chunk_heads(ids, count)):

        def body():
            at = pl.ds(pl.multiple_of(head * part, 16), part)
            first = 0
            for out_ref, width in zip(outs, widths):
                for pair in range(0, n_slot, 2):
                    both = [ref[ids[0] ^ dev][:, first : first + width] for dev in (pair, pair + 1)]
                    out_ref[at, pair * width : (pair + 2) * width] = jnp.concatenate(both, 1).astype(F32)
                first += width

        place_chunk(ok, body)


def ff_kernel(n0, n1, c0, c1, gate_ref, up_ref, down_ref, hid_ref, dgu_ref, own_ref, other_ref):
    width = gate_ref.shape[1]
    for i, (n_ref, c_ref) in ((1, (n1, c1)), (0, (n0, c0))):
        n = n_ref[...]
        gate = dot(n, gate_ref[...])
        up = dot(n, up_ref[...])
        grad = dot(c_ref[...], down_ref[...], ((1,), (1,)))
        sigma = jax.nn.sigmoid(gate)
        silu = gate * sigma
        hid_ref[i] = (silu * up).astype(BF)
        grad_gate = (grad * up * sigma * (1.0 + gate * (1.0 - sigma))).astype(BF)
        grad_up = (grad * silu).astype(BF)
        dgu_ref[i, :, :width] = grad_gate
        dgu_ref[i, :, width:] = grad_up
        total = dot(grad_gate, gate_ref[...], ((1,), (1,))) + dot(grad_up, up_ref[...], ((1,), (1,)))
        if i == 0:
            own_ref[...] = total
        else:
            other_ref[...] = total.astype(BF)


def ff_call(n0, n1, c0, c1, gate_w, up_w, down_w):
    rows, width = n0.shape[0], gate_w.shape[1]
    return pl.pallas_call(
        ff_kernel,
        out_shape=(
            jax.ShapeDtypeStruct((2, rows, width), BF),
            jax.ShapeDtypeStruct((2, rows, 2 * width), BF),
            jax.ShapeDtypeStruct((rows, D), F32),
            jax.ShapeDtypeStruct((rows, D), BF),
        ),
        in_specs=whole(7),
        out_specs=tuple(whole(4)),
        compiler_params=pltpu.CompilerParams(vmem_limit_bytes=40 << 20),
        cost_estimate=pl.CostEstimate(
            flops=2 * 2 * rows * D * width * 5, transcendentals=2 * rows * width, bytes_accessed=12 << 20
        ),
        name="ff",
    )(n0, n1, c0, c1, gate_w, up_w, down_w)


def ff_weight_kernel(n_pairs, *refs):
    n_refs, c_refs = refs[: 2 * n_pairs], refs[2 * n_pairs : 4 * n_pairs]
    dgu_refs, hid_refs = refs[4 * n_pairs : 5 * n_pairs], refs[5 * n_pairs : 6 * n_pairs]
    ff_ref, down_ref = refs[6 * n_pairs :]
    over = ((0,), (0,))
    total_ff = total_down = None
    for i in range(2 * n_pairs):
        core, k = i // n_pairs, i % n_pairs
        one = dot(n_refs[i][...], dgu_refs[k][core], over)
        two = dot(hid_refs[k][core], c_refs[i][...], over)
        total_ff = one if total_ff is None else total_ff + one
        total_down = two if total_down is None else total_down + two
    n_head, n_dev, part, width = ff_ref.shape
    for dev in range(n_dev):
        for head in range(n_head):
            first = (dev * n_head + head) * part
            ff_ref[head, dev] = total_ff[first : first + part].astype(BF)
    down_ref[...] = total_down.astype(BF)


def ff_weight_call(n_list, c_list, dgu_list, hid_list, n_head, n_plane):
    n_pairs = len(dgu_list)
    rows, width2 = n_list[0].shape[0], dgu_list[0].shape[2]
    part = D // n_plane // n_head
    cols = 384
    steps = D // cols
    lanes = pl.BlockSpec((rows, cols), lambda j: (0, j))
    fixed = lambda v: pl.BlockSpec(v.shape, lambda j: (0, 0, 0), pipeline_mode=pl.Buffered(1))
    per_step = n_plane // steps
    return pl.pallas_call(
        functools.partial(ff_weight_kernel, n_pairs),
        grid=(steps,),
        out_shape=(
            jax.ShapeDtypeStruct((n_head, n_plane, part, width2), BF),
            jax.ShapeDtypeStruct((width2 // 2, D), BF),
        ),
        in_specs=[lanes] * (4 * n_pairs) + [fixed(v) for v in dgu_list] + [fixed(v) for v in hid_list],
        out_specs=(
            pl.BlockSpec((n_head, per_step, part, width2), lambda j: (0, j, 0, 0)),
            pl.BlockSpec((width2 // 2, cols), lambda j: (0, j)),
        ),
        compiler_params=pltpu.CompilerParams(vmem_limit_bytes=56 << 20),
        cost_estimate=pl.CostEstimate(
            flops=2 * 2 * n_pairs * rows * D * width2 * 3 // 2, transcendentals=0, bytes_accessed=24 << 20
        ),
        name="ff_weight",
    )(*n_list, *c_list, *dgu_list, *hid_list)


def simple_call(kernel, out_shape, values, name, flops):
    leaves = jax.tree.leaves(out_shape)
    moved = sum(v.size * v.dtype.itemsize for v in list(values) + leaves)
    return pl.pallas_call(
        kernel,
        out_shape=out_shape,
        in_specs=whole(len(values)),
        out_specs=jax.tree.map(lambda _: pl.BlockSpec(memory_space=pltpu.VMEM), out_shape),
        compiler_params=pltpu.CompilerParams(vmem_limit_bytes=52 << 20),
        cost_estimate=pl.CostEstimate(flops=flops, transcendentals=0, bytes_accessed=moved),
        name=name,
    )(*values)


def stack_project_kernel(*refs):
    weight, out_ref = refs[-2], refs[-1]
    rows = refs[0].shape[0]
    for i, ref in enumerate(refs[:-2]):
        out_ref[i * rows : (i + 1) * rows, :] = dot(ref[...], weight[...]).astype(BF)


def out_project_kernel(n_blk, *refs):
    o_refs, w_refs = refs[:n_blk], refs[n_blk : 3 * n_blk]
    x_ref, gain_ref, mid_ref, n_ref = refs[3 * n_blk :]
    total = x_ref[...].astype(F32)
    for core in range(2):
        for k in range(n_blk):
            o = o_refs[k][core]
            o = jnp.concatenate([o[:, :HD], o[:, HP : HP + HD]], 1)
            total = total + dot(o, w_refs[core * n_blk + k][...])
    mid_ref[...] = total
    factor = lax.rsqrt(jnp.mean(total * total, -1, keepdims=True) + EPS)
    n_ref[...] = (total * factor * gain_ref[...]).astype(BF)


def branch_kernel(n_blk, *refs):
    w_refs = refs[: 2 * n_blk]
    local_ref, got_refs = refs[2 * n_blk], refs[2 * n_blk + 1 : 3 * n_blk]
    mid_ref, cot_ref, gain_ref, grad_ref, branch_ref, do_ref = refs[3 * n_blk :]
    total = local_ref[...]
    for ref in got_refs:
        total = total + ref[...].astype(F32)
    mid = mid_ref[...]
    factor = lax.rsqrt(jnp.mean(mid * mid, -1, keepdims=True) + EPS)
    grad = cot_ref[...].astype(F32) + norm_back(total, gain_ref[...], mid * factor, factor)
    grad_ref[...] = grad
    branch = grad.astype(BF)
    branch_ref[...] = branch
    zero = jnp.zeros((branch.shape[0], HP - HD), BF)
    for core in range(2):
        for k in range(n_blk):
            do = dot(branch, w_refs[core * n_blk + k][...], ((1,), (1,))).astype(BF)
            do_ref[core, k] = jnp.concatenate([do[:, :HD], zero, do[:, HD:], zero], 1)


def back_project_kernel(transposed, *refs):
    weight, own_ref, other_ref = refs[-3], refs[-2], refs[-1]
    dims = ((1,), (1,)) if transposed else ((1,), (0,))
    n_blk, rows = own_ref.shape[:2]
    for core in (1, 0):
        for k in range(n_blk):
            at = (core * n_blk + k) * rows
            value = refs[0][at : at + rows, :] if len(refs) == 4 else refs[k][core]
            part = dot(value, weight[...], dims)
            if core:
                other_ref[k] = part.astype(BF)
            else:
                own_ref[k] = part


def out_weight_kernel(count, *refs):
    o_ref, b_refs, out_ref = refs[0], refs[1 : 1 + count], refs[-1]
    rows = b_refs[0].shape[0]
    total = None
    for i, ref in enumerate(b_refs):
        one = dot(o_ref[i * rows : (i + 1) * rows, :], ref[...], ((0,), (0,)))
        total = one if total is None else total + one
    out_ref[:HD, :] = total[:HD].astype(BF)
    out_ref[HD:, :] = total[HP : HP + HD].astype(BF)


def qkv_weight_kernel(n_refs_count, *refs):
    n_refs, grad_ref, out_ref = refs[:n_refs_count], refs[-2], refs[-1]
    rows = n_refs[0].shape[0]
    total = None
    for i, ref in enumerate(n_refs):
        one = dot(ref[...], grad_ref[i * rows : (i + 1) * rows, :], ((0,), (0,)))
        total = one if total is None else total + one
    total = jnp.concatenate([total[:, g * HP : g * HP + HD] for g in range(4)], 1)
    n_head, n_dev, part, _ = out_ref.shape
    for dev in range(n_dev):
        for head in range(n_head):
            first = (dev * n_head + head) * part
            out_ref[head, dev] = total[first : first + part].astype(BF)


def qkv_weight_call(n_list, dqkv, n_head, n_plane):
    rows = n_list[0].shape[0]
    part = D // n_plane // n_head
    cols = 384
    steps = D // cols
    return pl.pallas_call(
        functools.partial(qkv_weight_kernel, len(n_list)),
        grid=(steps,),
        out_shape=jax.ShapeDtypeStruct((n_head, n_plane, part, 4 * HD), BF),
        in_specs=[pl.BlockSpec((rows, cols), lambda j: (0, j))] * len(n_list)
        + [pl.BlockSpec(dqkv.shape, lambda j: (0, 0), pipeline_mode=pl.Buffered(1))],
        out_specs=pl.BlockSpec((n_head, n_plane // steps, part, 4 * HD), lambda j: (0, j, 0, 0)),
        compiler_params=pltpu.CompilerParams(vmem_limit_bytes=48 << 20),
        cost_estimate=pl.CostEstimate(
            flops=2 * len(n_list) * rows * D * 4 * HP * 2, transcendentals=0, bytes_accessed=12 << 20
        ),
        name="qkv_weight",
    )(*n_list, dqkv)


def after(value, *first):
    return lax.optimization_barrier((value,) + first)[0]


def swap(value, axis, mask):
    return lax.ppermute(value, axis, [(i, i ^ mask) for i in range(lax.axis_size(axis))])


class Stages:
    def __init__(self):
        self.last = ()

    def __call__(self, *trees):
        leaves, tree = jax.tree.flatten(trees)
        tied = lax.optimization_barrier(tuple(leaves) + self.last)
        self.last = (tied[0],)
        return jax.tree.unflatten(tree, tied[: len(leaves)])


def near(value):
    return swap(value, "blk", 1), swap(value, "blk", 2)


def far(one, two):
    half = one.shape[0] // 2
    return swap(one[:half], "blk", 2), swap(two[half:], "blk", 1)


def across(*values):
    return tuple(swap(v, "dp", 1) for v in values)


def chips(both):
    return [both[0]] + [swap(both[k], "blk", k) for k in range(1, len(both))]


def pair_up(mine, other):
    return [jnp.stack([mine[k], other[k]]) for k in range(mine.shape[0])]


def add_cores(own, other):
    return own + swap(other, "dp", 1).astype(F32)


def line_step(left, right):
    up = [(i, i + 1) for i in range(3)]
    return lax.ppermute(left, "head", up), lax.ppermute(right, "head", [(b, a) for a, b in up])


def rel_to_abs(value, reverse=False):
    n_blk = lax.axis_size("blk")
    mine = lax.axis_index("dp") * n_blk + lax.axis_index("blk")
    flat = value.reshape((2 * n_blk,) + value.shape[(1 if reverse else 2) :])
    out = jnp.stack([lax.dynamic_index_in_dim(flat, i ^ mine, 0, keepdims=False) for i in range(2 * n_blk)])
    return out.reshape((2, n_blk) + out.shape[1:]) if reverse else out


def per_device(
    activations,
    segments,
    cotangent,
    norm_gain_one,
    query_weight,
    key_weight,
    value_weight,
    output_weight,
    norm_gain_two,
    gate_weight,
    up_weight,
    down_weight,
):
    n_blk, n_head = lax.axis_size("blk"), lax.axis_size("head")
    n_plane = 2 * n_blk
    assert lax.axis_size("dp") == 2 and activations.shape[0] == 2 and n_plane == KVH
    sub = n_head // 4
    tok = activations.shape[2]
    span = tok * n_head
    own = 2 * tok
    rows = n_plane * own
    my_dp, my_blk, my_head = (lax.axis_index(name) for name in ("dp", "blk", "head"))
    my_seq, my_sub = my_head // sub, my_head % sub

    def routes(k):
        pairs = []
        for core in range(2):
            for head in range(n_head):
                seq_part, sub_part = head // sub, head % sub
                target = 2 * (k ^ (seq_part & 1)) + core
                pairs.append((core * n_head + head, (seq_part >> 1) * n_head + target * sub + sub_part))
        return pairs

    def to_plane(value):
        parts = []
        for k in range(2):
            piece = lax.dynamic_index_in_dim(value, k ^ (my_seq & 1), 0, keepdims=False)
            parts.append(lax.ppermute(piece, ("dp", "head"), routes(k)))
        return parts

    def from_plane(value):
        parts = []
        for k in range(2):
            back = [(b, a) for a, b in routes(k)]
            parts.append(lax.ppermute(value[k * tok : (k + 1) * tok], ("dp", "head"), back))
        odd = (my_seq & 1) == 1
        return jnp.stack([jnp.where(odd, parts[1], parts[0]), jnp.where(odd, parts[0], parts[1])])

    me = my_dp * n_blk + my_blk
    ids = jnp.stack([me, my_head]).astype(jnp.int32)
    n_rows = D // n_plane
    part = n_rows // n_head
    ff_here = FF // n_plane
    width = 4 * HP
    assert span % width == 0
    seg_rows = span // width
    small_rows = -(-(2 + 2 * seg_rows) // 16) * 16
    gain_row = lambda v: jnp.pad(v, (0, width - n_rows))[None]
    small = [gain_row(norm_gain_one), gain_row(norm_gain_two), segments[:, 0].astype(BF).reshape(2 * seg_rows, width)]
    small.append(jnp.zeros((small_rows - 2 - 2 * seg_rows, width), BF))
    small = jnp.concatenate(small)
    fence = Stages()
    join = jnp.concatenate
    share = n_rows // 4

    def pack_qkv(*values):
        shape = jax.ShapeDtypeStruct((n_plane, n_rows + small_rows, 4 * HP), BF)
        packed = place_call(pack_qkv_kernel, shape, ids, *values, name="pack_qkv")
        return packed.reshape((2, n_blk) + packed.shape[1:])

    def pack_ff(gate, up):
        cut = [lax.dynamic_slice_in_dim(w, my_seq * share, share, 0) for w in (gate, up)]
        shape = jax.ShapeDtypeStruct((n_plane, share, 2 * ff_here), BF)
        packed = place_call(pack_ff_kernel, shape, ids, *cut, name="pack_ff")
        return packed.reshape((2, n_blk) + packed.shape[1:])

    packed, near_out, act_low, cot_low, gate_low, up_low = fence(
        pack_qkv(query_weight, key_weight, value_weight, small),
        near(output_weight),
        activations,
        cotangent,
        gate_weight,
        up_weight,
    )
    both, act_low, cot_low, gate_low, up_low = fence(
        pair_up(packed[0], swap(packed[1], "dp", 1)), act_low, cot_low, gate_low, up_low
    )
    ff_packed = pack_ff(gate_low, up_low)
    got, x_parts, ff_both, cot_low = fence(
        chips(both), to_plane(act_low[:, 0]), pair_up(ff_packed[0], swap(ff_packed[1], "dp", 1)), cot_low
    )
    qkv_w, seg_all, gains, x_low, input_one = place_call(
        functools.partial(head_kernel, n_blk),
        (
            jax.ShapeDtypeStruct((D, width), BF),
            jax.ShapeDtypeStruct((n_plane, small_rows, width), BF),
            jax.ShapeDtypeStruct((2, 1, D), F32),
            jax.ShapeDtypeStruct((own, D), BF),
            jax.ShapeDtypeStruct((own, D), BF),
        ),
        ids,
        *got,
        *x_parts,
        name="head",
        scratch=[pltpu.VMEM((n_plane, small_rows, width), BF)],
    )
    gain_one, gain_two = gains[0, 0], gains[1, 0]
    seg_all = seg_all[:, 2 : 2 + 2 * seg_rows].reshape(2, n_blk, 2, span)
    seg_seq = lax.dynamic_index_in_dim(seg_all, my_seq & 1, 0, keepdims=False)
    seg_seq = lax.dynamic_index_in_dim(seg_seq, my_seq >> 1, 1, keepdims=False)
    chunks = seg_seq.astype(jnp.int32).reshape(n_blk * n_head, tok)

    def chunk_ids(sub_index):
        ids = []
        for core in range(2):
            for blk in range(n_blk):
                for k in range(2):
                    seq_part = 2 * (my_dp ^ core) + ((my_seq >> 1) ^ k)
                    ids.append((my_blk ^ blk) * n_head + seq_part * sub + sub_index)
        return ids

    def pos_seg(sub_index):
        ids = chunk_ids(sub_index)
        lane = jnp.arange(tok, dtype=jnp.int32)
        pos = jnp.concatenate([i * tok + lane for i in ids])
        seg = jnp.concatenate([lax.dynamic_index_in_dim(chunks, i, 0, keepdims=False) for i in ids])
        return pos, seg

    qpos, qseg = pos_seg(my_sub)
    if sub == 1:
        kpos, kseg = qpos, qseg
    else:
        every = [pos_seg(i) for i in range(sub)]
        kpos, kseg = (jnp.concatenate([e[i] for e in every]) for i in range(2))
    blocked = lambda v: v.reshape(-1, BLK)
    qb, qsb, kb, ksb = blocked(qpos), blocked(qseg), blocked(kpos), blocked(kseg)
    need = (
        (jnp.min(kb, 1)[None, :] <= jnp.max(qb, 1)[:, None])
        & (jnp.min(ksb, 1)[None, :] <= jnp.max(qsb, 1)[:, None])
        & (jnp.max(ksb, 1)[None, :] >= jnp.min(qsb, 1)[:, None])
    ).astype(jnp.int32)

    input_one, qkv_w, ff_both, cot_low = fence(input_one, qkv_w, ff_both, cot_low)
    near_one, cot, side_one = fence(near(input_one), to_plane(cot_low[:, 0]), across(input_one))
    far_one, more_one, cot = fence(far(*near_one), across(*near_one), join(cot))
    far_one = join(far_one)
    mine_one = [input_one, *near_one, far_one]
    all_one = fence(*mine_one, *side_one, *more_one, *across(far_one))

    def project_qkv(*values):
        shape = jax.ShapeDtypeStruct((rows, 4 * HP), BF)
        return simple_call(stack_project_kernel, shape, values, "project_qkv", 2 * rows * D * 4 * HP)

    ff_both = [after(v, all_one[-1]) for v in ff_both]
    qkv, ff_got, cot, near_out = fence(project_qkv(*all_one, qkv_w), chips(ff_both), cot, near_out)
    kv = ()
    if sub > 1:
        groups = [[s * sub + i for i in range(sub)] for s in range(4)]
        kv = (lax.all_gather(qkv[:, 2 * HP :], "head", axis=0, tiled=True, axis_index_groups=groups),)
    q_args = tuple(v.astype(F32).reshape(-1, 1, BLK) for v in (qpos, qseg, kpos, kseg))
    sharing = None if sub == 1 else [[s * sub + i for s in range(4)] for i in range(sub)]
    ff_all = jnp.stack(ff_got, 1).reshape(-1, 2 * ff_here)
    ff_all = lax.all_gather(ff_all, "head", axis=0, tiled=True, axis_index_groups=sharing)
    ff_all = ff_all.reshape(4, n_plane, share, 2 * ff_here)
    (o, lse), near_cot, far_out = fence(attend(need, qkv, *(kv or (None,)), *q_args), near(cot), far(*near_out))
    o_parts = o.reshape(2, n_blk, own, 2 * HP)
    mine_out = [output_weight, *near_out, join(far_out)]
    o_both, near_cot = fence(pair_up(o_parts[0], swap(o_parts[1], "dp", 1)), near_cot)
    o_got, side_out, near_cot = fence(chips(o_both), across(*mine_out), near_cot)
    all_out = [*mine_out, *side_out]

    def out_project(*values):
        shapes = (jax.ShapeDtypeStruct((own, D), F32), jax.ShapeDtypeStruct((own, D), BF))
        kernel = functools.partial(out_project_kernel, n_blk)
        return simple_call(kernel, shapes, values, "out_project", 2 * own * D * D)

    (x_mid, input_two), side_cot = fence(
        out_project(*o_got, *all_out, x_low, gain_two[None]), across(cot, *near_cot)
    )

    def unpack_ff(value):
        shapes = (jax.ShapeDtypeStruct((D, ff_here), BF),) * 2
        return place_call(unpack_ff_kernel, shapes, ids, value, name="unpack_ff")

    def ff_part(n_mine, n_side, c_mine, c_side):
        return ff_call(n_mine, n_side, c_mine, c_side, gate_w, up_w, down_weight)

    gate_w, up_w = unpack_ff(after(ff_all, input_two))
    side_two = across(input_two)
    near_two, part_0, near_cot, gate_w, up_w = fence(
        near(input_two), ff_part(input_two, side_two[0], cot, side_cot[0]), near_cot, gate_w, up_w
    )
    more_two = across(*near_two)
    far_two, far_cot, part_1, part_2 = fence(
        far(*near_two),
        far(*near_cot),
        ff_part(near_two[0], more_two[0], near_cot[0], side_cot[1]),
        ff_part(near_two[1], more_two[1], near_cot[1], side_cot[2]),
    )
    far_two, far_cot = join(far_two), join(far_cot)
    last_two, last_cot = across(far_two, far_cot)
    side_parts = across(part_0[3], part_1[3], part_2[3])
    part_3, side_parts = fence(ff_part(far_two, last_two, far_cot, last_cot), side_parts)
    parts = [part_0, part_1, part_2, part_3]
    side_parts = [*side_parts, *across(part_3[3])]
    hidden, grad_gu = [p[0] for p in parts], [p[1] for p in parts]
    all_two = [input_two, *near_two, far_two, *side_two, *more_two, last_two]
    all_cot = [cot, *near_cot, far_cot, *side_cot, last_cot]
    local_two = [p[2] + v.astype(F32) for p, v in zip(parts, side_parts)]
    local_0, sent_two = fence(local_two[0], [v.astype(BF) for v in local_two])
    got_two = chips(sent_two)[1:]

    contract = ((0,), (0,))

    def rel_parts(mine):
        return rel_to_abs(mine, True)

    def head_sum(sent):
        return lax.psum_scatter(sent, "head", scatter_dimension=0, tiled=True)

    def owned_rows(chunks):
        if n_head != 4:
            return chunks[0].reshape(-1, chunks[0].shape[-1]).astype(F32)
        shape = jax.ShapeDtypeStruct((4 * chunks[0].shape[0], chunks[0].shape[1]), F32)
        return place_call(place_rows_kernel, shape, ids, *chunks, name="place_rows")

    def owned_columns(chunks, widths):
        if n_head != 4:
            full = rel_to_abs(jnp.moveaxis(chunks[0], 0, 1).reshape((2, n_blk, n_head) + chunks[0].shape[2:]))
            full = full.reshape(n_plane, n_rows, -1).transpose(1, 0, 2).astype(F32)
            ends = [sum(widths[: i + 1]) for i in range(len(widths))]
            return [full[:, :, e - w : e].reshape(n_rows, -1) for e, w in zip(ends, widths)]
        shapes = [jax.ShapeDtypeStruct((n_rows, n_plane * w), F32) for w in widths]
        kernel = functools.partial(place_columns_kernel, widths, len(chunks))
        return place_call(kernel, shapes, ids, *chunks, name="place_columns")

    ff_sent, down_sent = ff_weight_call(all_two, all_cot, grad_gu, hidden, n_head, n_plane)
    got_two, ff_sent, down_sent = fence(got_two, ff_sent, down_sent)
    down_mine = head_sum(down_sent)
    ff_mine = head_sum(ff_sent.reshape(D, 2 * ff_here)).reshape(n_plane, part, 2 * ff_here)

    def branch(*values):
        shapes = (
            jax.ShapeDtypeStruct((own, D), F32),
            jax.ShapeDtypeStruct((own, D), BF),
            jax.ShapeDtypeStruct((2, n_blk, own, 2 * HP), BF),
        )
        kernel = functools.partial(branch_kernel, n_blk)
        return simple_call(kernel, shapes, values, "branch", 2 * own * D * D)

    grad_mid, grad_branch, grad_o = fence(*branch(*all_out, local_0, *got_two, x_mid, cot, gain_two[None]))
    (do_both,) = fence(pair_up(grad_o[0], swap(grad_o[1], "dp", 1)))
    do_got, down_mine, grad_branch = fence(chips(do_both), down_mine, grad_branch)
    grad_o = jnp.stack(do_got, 1).reshape(rows, 2 * HP)
    line = n_head == 4
    no_step = lambda *v: ()
    step = line_step if line else no_step
    back = attend_back(need, qkv, *(kv or (None,)), *q_args, o, lse, grad_o)
    line_0 = step(down_mine, down_mine)
    dqkv, near_branch = fence(back, near(grad_branch))
    if sub > 1:
        dkv = lax.psum_scatter(dqkv[1], "head", scatter_dimension=0, tiled=True, axis_index_groups=groups)
        dqkv = [join([dqkv[0], dkv], 1)]
    dqkv = dqkv[0]

    def back_project(transposed, *values):
        shapes = tuple(jax.ShapeDtypeStruct((n_blk, own, D), t) for t in (F32, BF))
        kernel = functools.partial(back_project_kernel, transposed)
        return simple_call(kernel, shapes, values, "back_project", 2 * rows * D * values[-1].size // D)

    qkv_grad, far_branch, dqkv, line_0 = fence(
        qkv_weight_call(all_one, dqkv, n_head, n_plane), far(*near_branch), dqkv, line_0
    )
    qkv_mine = head_sum(qkv_grad.reshape(D, 4 * HD)).reshape(n_plane, part, 4 * HD)
    mine_branch = [grad_branch, *near_branch, join(far_branch)]
    (one_own, one_other), line_1, side_branch, ff_mine = fence(
        back_project(True, dqkv, qkv_w), step(*line_0), across(*mine_branch), ff_mine
    )

    def out_weights(*values):
        rows_per = values[1].shape[0]
        lanes = pl.BlockSpec((rows_per, 384), lambda j: (0, j))
        return pl.pallas_call(
            functools.partial(out_weight_kernel, n_plane),
            grid=(D // 384,),
            out_shape=jax.ShapeDtypeStruct((2 * HD, D), BF),
            in_specs=[pl.BlockSpec(values[0].shape, lambda j: (0, 0), pipeline_mode=pl.Buffered(1))] + [lanes] * n_plane,
            out_specs=pl.BlockSpec((2 * HD, 384), lambda j: (0, j)),
            compiler_params=pltpu.CompilerParams(vmem_limit_bytes=48 << 20),
            cost_estimate=pl.CostEstimate(flops=4 * rows * D * 2 * HP, transcendentals=0, bytes_accessed=9 << 20),
            name="out_weight",
        )(*values)

    ff_rel = rel_parts(ff_mine)
    one_side, out_grad, one_own, ff_both, line_1, hidden = fence(
        swap(one_other, "dp", 1),
        out_weights(o, *mine_branch, *side_branch),
        one_own,
        pair_up(ff_rel[0], swap(ff_rel[1], "dp", 1)),
        line_1,
        hidden,
    )
    out_mine = head_sum(out_grad)
    local_one = [one_own[k] + one_side[k].astype(F32) for k in range(n_blk)]
    ff_got, local_0, sent_one, line_2, qkv_mine = fence(
        chips(ff_both), local_one[0], [v.astype(BF) for v in local_one], step(*line_1), qkv_mine
    )
    ff_rows = jnp.stack(ff_got, 1).reshape(ff_mine.shape)
    qkv_rel = rel_parts(qkv_mine)
    qkv_both = pair_up(qkv_rel[0], swap(qkv_rel[1], "dp", 1))
    ff_0 = step(ff_rows, ff_rows)
    out_own, out_other = back_project(False, *hidden, down_weight)
    out_side = swap(out_other, "dp", 1)
    local_out = [out_own[k] + out_side[k].astype(F32) for k in range(n_blk)]
    ff_0, qkv_rows, local_out_0, sent_out, sent_one, local_0, out_mine = fence(
        ff_0, chips(qkv_both), local_out[0], [v.astype(BF) for v in local_out], sent_one, local_0, out_mine
    )
    got_one, ff_1 = fence(chips(sent_one)[1:], step(*ff_0))
    normed, factor = normalize(x_low.astype(F32))
    grad_in_one = local_0 + sum(g.astype(F32) for g in got_one)
    grad_input = (grad_mid + norm_back(grad_in_one, gain_one, normed, factor)).astype(BF)
    local_0 = local_out_0
    got_out = chips([after(v, *ff_1) if line else v for v in sent_out])[1:]
    late = join([jnp.stack(qkv_rows, 1).reshape(-1, 4 * HD), out_mine.reshape(-1, 4 * HD)])
    late = lax.all_gather(late, "head", axis=0)
    if line:
        down_chunks = [line_2[0], line_1[0], line_0[0], down_mine, line_0[1], line_1[1], line_2[1]]
        grad_down = owned_rows(down_chunks)
    else:
        grad_down = owned_rows([lax.all_gather(down_mine, "head", axis=0)])
    got_out, ff_2, grad_input = fence(got_out, step(*ff_1), grad_input)
    block_out = (x_mid + local_0 + sum(g.astype(F32) for g in got_out)).astype(BF)
    block_out, grad_input = from_plane(block_out), from_plane(grad_input)
    late_qkv = late[:, : n_plane * part].reshape(n_head, n_plane, part, 4 * HD)
    late_out = late[:, n_plane * part :].reshape(n_head, part, D)
    each = lambda v: [v[i] for i in range(4)] if line else [v]
    if line:
        ff_chunks = [ff_2[0], ff_1[0], ff_0[0], ff_rows, ff_0[1], ff_1[1], ff_2[1]]
    else:
        ff_chunks = [lax.all_gather(ff_rows, "head", axis=0)]
    grad_gate_w, grad_up_w = owned_columns(ff_chunks, (ff_here, ff_here))
    grad_query, grad_key, grad_value = owned_columns(each(late_qkv), (2 * HD, HD, HD))
    grad_out = owned_rows(each(late_out))

    def gain_grad(gain, *pairs):
        return sum(jnp.sum(w.astype(F32) * g, -1) for w, g in pairs) / gain.astype(F32)

    grad_gain_one = gain_grad(
        norm_gain_one, (query_weight, grad_query), (key_weight, grad_key), (value_weight, grad_value)
    )
    grad_gain_two = gain_grad(norm_gain_two, (gate_weight, grad_gate_w), (up_weight, grad_up_w))
    return (
        block_out[:, None],
        grad_input[:, None],
        grad_gain_one,
        grad_query,
        grad_key,
        grad_value,
        grad_out,
        grad_gain_two,
        grad_gate_w,
        grad_up_w,
        grad_down,
    )


def solution(mesh):
    tokens = P(None, "dp", ("blk", "head"), None)
    vector = P(("dp", "blk"))
    matrix = P(("dp", "blk"), None)
    return jax.shard_map(
        per_device,
        mesh=mesh,
        in_specs=(
            tokens,
            P(None, "dp", "blk"),
            tokens,
            vector,
            matrix,
            matrix,
            matrix,
            matrix,
            vector,
            matrix,
            matrix,
            matrix,
        ),
        out_specs=(tokens, tokens, vector, matrix, matrix, matrix, matrix, vector, matrix, matrix, matrix),
        check_vma=False,
    )
```

```python
import functools
import math

import jax
import jax.numpy as jnp
from jax import lax
from jax.experimental import pallas as pl
from jax.experimental.pallas import tpu as pltpu
from jax.sharding import PartitionSpec as P

D = 1536
QH = 16
KVH = 8
HD = 96
HP = 128
FF = 4096
EPS = 1e-05
NEG = -1e30
BLK = 256
BF = jnp.bfloat16
F32 = jnp.float32


def small_cost(flops, transcendentals, bytes_accessed):
    part = 64
    return pl.CostEstimate(
        flops=flops // part, transcendentals=transcendentals // part, bytes_accessed=bytes_accessed // part
    )


def dot(left, right, dims=((1,), (0,))):
    return lax.dot_general(left, right, (dims, ((), ())), preferred_element_type=F32)


def normalize(values):
    factor = lax.rsqrt(jnp.mean(values * values, -1, keepdims=True) + EPS)
    return values * factor, factor


def norm_back(grad_norm, gain, normed, factor):
    scaled = grad_norm * gain
    return factor * (scaled - normed * jnp.mean(scaled * normed, -1, keepdims=True))


def rows_of(index):
    return pl.ds(pl.multiple_of(index * BLK, BLK), BLK)


def as_column(row):
    return jnp.broadcast_to(row, (HP, BLK)).T[:, 0:1]


def as_row(col):
    return jnp.broadcast_to(col, (BLK, HP)).T[0:1, :]


def keys_to_columns(kp_ref, ks_ref, pos_sc, seg_sc):
    def one(j, _):
        pos_sc[rows_of(j), :] = as_column(kp_ref[j])
        seg_sc[rows_of(j), :] = as_column(ks_ref[j])
        return 0

    lax.fori_loop(0, kp_ref.shape[0], one, 0)


def attn_fwd_kernel(first, need, q_ref, kv_ref, qp_ref, qs_ref, kp_ref, ks_ref, o_ref, lse_ref, m_sc, l_sc, acc_sc, pos_sc, seg_sc):
    scale = 1.0 / math.sqrt(HD)
    n_q, n_k = q_ref.shape[0] // BLK, kv_ref.shape[0] // BLK
    k_cols, v_cols = slice(first, first + HP), slice(first + HP, first + 2 * HP)
    keys_to_columns(kp_ref, ks_ref, pos_sc, seg_sc)

    def one_query(i, _):
        qr = rows_of(i)
        m_sc[...] = jnp.full_like(m_sc, NEG)
        l_sc[...] = jnp.zeros_like(l_sc)
        acc_sc[...] = jnp.zeros_like(acc_sc)
        qpos, qseg = qp_ref[i], qs_ref[i]

        def one_key(j, _):
            @pl.when(need[i, j] != 0)
            def _():
                kr = rows_of(j)
                ok = (pos_sc[kr, :] <= qpos) & (seg_sc[kr, :] == qseg)
                k, v = kv_ref[kr, k_cols], kv_ref[kr, v_cols]
                state = [(m_sc[g], l_sc[g], acc_sc[g], q_ref[qr, g * HP : (g + 1) * HP]) for g in range(2)]
                scores = [jnp.where(ok, dot(k, q, ((1,), (1,))) * scale, NEG) for _, _, _, q in state]
                new = []
                for (m_old, l_old, acc_old, _), s in zip(state, scores):
                    m_new = jnp.maximum(m_old, jnp.max(s, 0, keepdims=True))
                    p = jnp.where(ok, jnp.exp(s - m_new), 0.0)
                    decay = jnp.exp(m_old - m_new)
                    total = l_old * decay + jnp.sum(p, 0, keepdims=True)
                    new.append((m_new, total, acc_old * decay + dot(v, p.astype(BF), ((0,), (0,)))))
                for g in range(2):
                    m_sc[g], l_sc[g], acc_sc[g] = new[g]

            return 0

        lax.fori_loop(0, n_k, one_key, 0)
        for g in range(2):
            o_ref[qr, g * HP : (g + 1) * HP] = (acc_sc[g] / l_sc[g]).T.astype(BF)
            lse_ref[i, g : g + 1, :] = m_sc[g] + jnp.log(l_sc[g])
        return 0

    lax.fori_loop(0, n_q, one_query, 0)


def attn_bwd_kernel(first, need, q_ref, kv_ref, qp_ref, qs_ref, kp_ref, ks_ref, o_ref, lse_ref, do_ref, *rest):
    dq_ref, dkv_ref = rest[0], rest[-6]
    dq_sc, dk_sc, dv_sc, pos_sc, seg_sc = rest[-5:]
    scale = 1.0 / math.sqrt(HD)
    n_q, n_k = q_ref.shape[0] // BLK, kv_ref.shape[0] // BLK
    k_cols, v_cols = slice(first, first + HP), slice(first + HP, first + 2 * HP)
    dk_sc[...] = jnp.zeros_like(dk_sc)
    dv_sc[...] = jnp.zeros_like(dv_sc)
    keys_to_columns(kp_ref, ks_ref, pos_sc, seg_sc)

    def one_query(i, _):
        qr = rows_of(i)
        dq_sc[...] = jnp.zeros_like(dq_sc)
        qpos, qseg = qp_ref[i], qs_ref[i]
        lse, delta = [], []
        for g in range(2):
            cols = slice(g * HP, (g + 1) * HP)
            lse.append(lse_ref[i, g : g + 1, :])
            prod = do_ref[qr, cols].astype(F32) * o_ref[qr, cols].astype(F32)
            delta.append(as_row(jnp.sum(prod, -1, keepdims=True)))

        def one_key(j, _):
            @pl.when(need[i, j] != 0)
            def _():
                kr = rows_of(j)
                ok = (pos_sc[kr, :] <= qpos) & (seg_sc[kr, :] == qseg)
                k, v = kv_ref[kr, k_cols], kv_ref[kr, v_cols]
                qs = [q_ref[qr, g * HP : (g + 1) * HP] for g in range(2)]
                dos = [do_ref[qr, g * HP : (g + 1) * HP] for g in range(2)]
                scores = [dot(k, q, ((1,), (1,))) * scale for q in qs]
                dps = [dot(v, do, ((1,), (1,))) for do in dos]
                dv, dk = dv_sc[kr, :], dk_sc[kr, :]
                dqs = []
                for g in range(2):
                    p = jnp.where(ok, jnp.exp(scores[g] - lse[g]), 0.0)
                    ds = (p * (dps[g] - delta[g])).astype(BF)
                    dv = dv + dot(p.astype(BF), dos[g])
                    dk = dk + dot(ds, qs[g])
                    dqs.append(dot(ds, k, ((0,), (0,))))
                dv_sc[kr, :], dk_sc[kr, :] = dv, dk
                for g in range(2):
                    dq_sc[g] += dqs[g]

            return 0

        lax.fori_loop(0, n_k, one_key, 0)
        for g in range(2):
            dq_ref[qr, g * HP : (g + 1) * HP] = (dq_sc[g] * scale).astype(BF)
        return 0

    lax.fori_loop(0, n_q, one_query, 0)
    dkv_ref[:, k_cols] = (dk_sc[...] * scale).astype(BF)
    dkv_ref[:, v_cols] = dv_sc[...].astype(BF)


def in_vmem(count):
    return [pl.BlockSpec(memory_space=pltpu.SMEM)] + [pl.BlockSpec(memory_space=pltpu.VMEM)] * count


def attn_cost(n_q, n_k, products):
    return small_cost(
        flops=2 * products * n_q * n_k * 2 * HP, transcendentals=n_q * n_k * 2, bytes_accessed=(n_q + n_k) * HP * 16
    )


def attend(need, q, kv, qpos, qseg, kpos, kseg):
    first, kv = (2 * HP, q) if kv is None else (0, kv)
    n_q, n_k = q.shape[0], kv.shape[0]
    return pl.pallas_call(
        functools.partial(attn_fwd_kernel, first),
        out_shape=(jax.ShapeDtypeStruct((n_q, 2 * HP), BF), jax.ShapeDtypeStruct((n_q // BLK, 2, BLK), F32)),
        in_specs=in_vmem(6),
        out_specs=(pl.BlockSpec(memory_space=pltpu.VMEM),) * 2,
        scratch_shapes=[pltpu.VMEM((2, 1, BLK), F32)] * 2 + [pltpu.VMEM((2, HP, BLK), F32)] + [pltpu.VMEM((n_k, 1), F32)] * 2,
        compiler_params=pltpu.CompilerParams(vmem_limit_bytes=40 << 20),
        cost_estimate=attn_cost(n_q, n_k, 2),
        name="attn_fwd",
    )(need, q, kv, qpos, qseg, kpos, kseg)


def attend_back(need, q, kv, qpos, qseg, kpos, kseg, o, lse, do):
    joint = kv is None
    first, kv = (2 * HP, q) if joint else (0, kv)
    n_q, n_k = q.shape[0], kv.shape[0]
    shapes = [jax.ShapeDtypeStruct((n_q, 4 * HP), BF)] if joint else [jax.ShapeDtypeStruct((n, 2 * HP), BF) for n in (n_q, n_k)]
    return pl.pallas_call(
        functools.partial(attn_bwd_kernel, first),
        out_shape=shapes,
        in_specs=in_vmem(9),
        out_specs=[pl.BlockSpec(memory_space=pltpu.VMEM)] * len(shapes),
        scratch_shapes=[pltpu.VMEM((2, BLK, HP), F32)] + [pltpu.VMEM((n_k, HP), F32)] * 2 + [pltpu.VMEM((n_k, 1), F32)] * 2,
        compiler_params=pltpu.CompilerParams(vmem_limit_bytes=48 << 20),
        cost_estimate=attn_cost(n_q, n_k, 5),
        name="attn_bwd",
    )(need, q, kv, qpos, qseg, kpos, kseg, o, lse, do)


def whole(count):
    return [pl.BlockSpec(memory_space=pltpu.VMEM)] * count


def place_call(kernel, out_shape, ids, *values, name, scratch=()):
    moved = sum(v.size * v.dtype.itemsize for v in values)
    return pl.pallas_call(
        kernel,
        out_shape=out_shape,
        in_specs=[pl.BlockSpec(memory_space=pltpu.SMEM)] + whole(len(values)),
        out_specs=jax.tree.map(lambda _: pl.BlockSpec(memory_space=pltpu.VMEM), out_shape),
        scratch_shapes=scratch,
        compiler_params=pltpu.CompilerParams(vmem_limit_bytes=40 << 20),
        cost_estimate=small_cost(flops=0, transcendentals=0, bytes_accessed=2 * moved),
        name=name,
    )(ids, *values)


def pack_qkv_kernel(ids, q_ref, k_ref, v_ref, small_ref, out_ref):
    rows = q_ref.shape[0]
    zero = jnp.zeros((rows, HP - HD), BF)
    for dev in range(KVH):
        slot = ids[0] ^ dev
        heads = [(q_ref, 2 * dev), (q_ref, 2 * dev + 1), (k_ref, dev), (v_ref, dev)]
        for i, (ref, head) in enumerate(heads):
            piece = ref[:, head * HD : (head + 1) * HD]
            out_ref[slot, :rows, i * HP : (i + 1) * HP] = jnp.concatenate([piece, zero], 1)
        out_ref[slot, rows:, :] = small_ref[...]


def pack_ff_kernel(ids, gate_ref, up_ref, out_ref):
    width = gate_ref.shape[1] // KVH
    for dev in range(KVH):
        slot = ids[0] ^ dev
        for i, ref in enumerate((gate_ref, up_ref)):
            out_ref[slot, :, i * width : (i + 1) * width] = ref[:, dev * width : (dev + 1) * width]


def head_kernel(n_blk, ids, *refs):
    got, x_refs = refs[:n_blk], refs[n_blk : n_blk + 2]
    w_ref, seg_ref, gain_ref, x_ref, c_ref, n_ref, small_sc = refs[n_blk + 2 :]
    n_rows = w_ref.shape[0] // (2 * n_blk)
    for k, ref in enumerate(got):
        for core in range(2):
            at = pl.multiple_of((ids[0] ^ (core * n_blk + k)) * n_rows, 16)
            w_ref[pl.ds(at, n_rows), :] = ref[core, :n_rows, :]
            small_sc[core * n_blk + k] = ref[core, n_rows:, :]
    gains = [[], []]
    for dev in range(2 * n_blk):
        small = small_sc[ids[0] ^ dev]
        seg_ref[dev] = small
        small = small.astype(F32)
        for i in range(2):
            gains[i].append(small[i : i + 1, :n_rows])
    for i in range(2):
        gain_ref[i] = jnp.concatenate(gains[i], 1)
    tok = x_refs[0].shape[0] // 2
    for i, ref in enumerate(x_refs):
        x = ref[:tok, :]
        x_ref[i * tok : (i + 1) * tok, :] = x
        c_ref[i * tok : (i + 1) * tok, :] = ref[tok:, :]
        x = x.astype(F32)
        factor = lax.rsqrt(jnp.mean(x * x, -1, keepdims=True) + EPS)
        n_ref[i * tok : (i + 1) * tok, :] = (x * factor * gain_ref[0]).astype(BF)


def unpack_ff_kernel(ids, in_ref, gate_ref, up_ref):
    n_head, n_slot, part, width = in_ref.shape
    for head in range(n_head):
        for slot in range(n_slot):
            at = pl.ds(pl.multiple_of(((ids[0] ^ slot) * n_head + head) * part, 16), part)
            gate_ref[at, :] = in_ref[head, slot, :, : width // 2]
            up_ref[at, :] = in_ref[head, slot, :, width // 2 :]


def chunk_heads(ids, count):
    if count == 7:
        return [(ids[1] + (i - 3), (ids[1] + (i - 3) >= 0) & (ids[1] + (i - 3) < 4)) for i in range(7)]
    return [(i, None) for i in range(count)]


def place_chunk(ok, body):
    if ok is None:
        body()
    else:
        pl.when(ok)(body)


def place_rows_kernel(ids, *refs):
    out_ref = refs[-1]
    part = refs[0].shape[0]
    for ref, (head, ok) in zip(refs[:-1], chunk_heads(ids, len(refs) - 1)):

        def body():
            out_ref[pl.ds(pl.multiple_of(head * part, 16), part), :] = ref[...].astype(F32)

        place_chunk(ok, body)


def place_columns_kernel(widths, count, ids, *refs):
    chunks, outs = refs[:count], refs[count:]
    n_slot, part = chunks[0].shape[:2]
    for ref, (head, ok) in zip(chunks, chunk_heads(ids, count)):

        def body():
            at = pl.ds(pl.multiple_of(head * part, 16), part)
            first = 0
            for out_ref, width in zip(outs, widths):
                for pair in range(0, n_slot, 2):
                    both = [ref[ids[0] ^ dev][:, first : first + width] for dev in (pair, pair + 1)]
                    out_ref[at, pair * width : (pair + 2) * width] = jnp.concatenate(both, 1).astype(F32)
                first += width

        place_chunk(ok, body)


def ff_kernel(n0, n1, c0, c1, gate_ref, up_ref, down_ref, hid_ref, dgu_ref, own_ref, other_ref):
    width = gate_ref.shape[1]
    for i, (n_ref, c_ref) in ((1, (n1, c1)), (0, (n0, c0))):
        n = n_ref[...]
        gate = dot(n, gate_ref[...])
        up = dot(n, up_ref[...])
        grad = dot(c_ref[...], down_ref[...], ((1,), (1,)))
        sigma = jax.nn.sigmoid(gate)
        silu = gate * sigma
        hid_ref[i] = (silu * up).astype(BF)
        grad_gate = (grad * up * sigma * (1.0 + gate * (1.0 - sigma))).astype(BF)
        grad_up = (grad * silu).astype(BF)
        dgu_ref[i, :, :width] = grad_gate
        dgu_ref[i, :, width:] = grad_up
        total = dot(grad_gate, gate_ref[...], ((1,), (1,))) + dot(grad_up, up_ref[...], ((1,), (1,)))
        if i == 0:
            own_ref[...] = total
        else:
            other_ref[...] = total.astype(BF)


def ff_call(n0, n1, c0, c1, gate_w, up_w, down_w):
    rows, width = n0.shape[0], gate_w.shape[1]
    return pl.pallas_call(
        ff_kernel,
        out_shape=(
            jax.ShapeDtypeStruct((2, rows, width), BF),
            jax.ShapeDtypeStruct((2, rows, 2 * width), BF),
            jax.ShapeDtypeStruct((rows, D), F32),
            jax.ShapeDtypeStruct((rows, D), BF),
        ),
        in_specs=whole(7),
        out_specs=tuple(whole(4)),
        compiler_params=pltpu.CompilerParams(vmem_limit_bytes=40 << 20),
        cost_estimate=small_cost(
            flops=2 * 2 * rows * D * width * 5, transcendentals=2 * rows * width, bytes_accessed=12 << 20
        ),
        name="ff",
    )(n0, n1, c0, c1, gate_w, up_w, down_w)


def ff_weight_kernel(n_pairs, *refs):
    n_refs, c_refs = refs[: 2 * n_pairs], refs[2 * n_pairs : 4 * n_pairs]
    dgu_refs, hid_refs = refs[4 * n_pairs : 5 * n_pairs], refs[5 * n_pairs : 6 * n_pairs]
    ff_ref, down_ref = refs[6 * n_pairs :]
    over = ((0,), (0,))
    total_ff = total_down = None
    for i in range(2 * n_pairs):
        core, k = i // n_pairs, i % n_pairs
        one = dot(n_refs[i][...], dgu_refs[k][core], over)
        two = dot(hid_refs[k][core], c_refs[i][...], over)
        total_ff = one if total_ff is None else total_ff + one
        total_down = two if total_down is None else total_down + two
    n_head, n_dev, part, width = ff_ref.shape
    for dev in range(n_dev):
        for head in range(n_head):
            first = (dev * n_head + head) * part
            ff_ref[head, dev] = total_ff[first : first + part].astype(BF)
    down_ref[...] = total_down.astype(BF)


def ff_weight_call(n_list, c_list, dgu_list, hid_list, n_head, n_plane):
    n_pairs = len(dgu_list)
    rows, width2 = n_list[0].shape[0], dgu_list[0].shape[2]
    part = D // n_plane // n_head
    cols = 384
    steps = D // cols
    lanes = pl.BlockSpec((rows, cols), lambda j: (0, j))
    fixed = lambda v: pl.BlockSpec(v.shape, lambda j: (0, 0, 0), pipeline_mode=pl.Buffered(1))
    per_step = n_plane // steps
    return pl.pallas_call(
        functools.partial(ff_weight_kernel, n_pairs),
        grid=(steps,),
        out_shape=(
            jax.ShapeDtypeStruct((n_head, n_plane, part, width2), BF),
            jax.ShapeDtypeStruct((width2 // 2, D), BF),
        ),
        in_specs=[lanes] * (4 * n_pairs) + [fixed(v) for v in dgu_list] + [fixed(v) for v in hid_list],
        out_specs=(
            pl.BlockSpec((n_head, per_step, part, width2), lambda j: (0, j, 0, 0)),
            pl.BlockSpec((width2 // 2, cols), lambda j: (0, j)),
        ),
        compiler_params=pltpu.CompilerParams(vmem_limit_bytes=56 << 20),
        cost_estimate=small_cost(
            flops=2 * 2 * n_pairs * rows * D * width2 * 3 // 2, transcendentals=0, bytes_accessed=24 << 20
        ),
        name="ff_weight",
    )(*n_list, *c_list, *dgu_list, *hid_list)


def simple_call(kernel, out_shape, values, name, flops):
    leaves = jax.tree.leaves(out_shape)
    moved = sum(v.size * v.dtype.itemsize for v in list(values) + leaves)
    return pl.pallas_call(
        kernel,
        out_shape=out_shape,
        in_specs=whole(len(values)),
        out_specs=jax.tree.map(lambda _: pl.BlockSpec(memory_space=pltpu.VMEM), out_shape),
        compiler_params=pltpu.CompilerParams(vmem_limit_bytes=52 << 20),
        cost_estimate=small_cost(flops=flops, transcendentals=0, bytes_accessed=moved),
        name=name,
    )(*values)


def stack_project_kernel(*refs):
    weight, out_ref = refs[-2], refs[-1]
    rows = refs[0].shape[0]
    for i, ref in enumerate(refs[:-2]):
        out_ref[i * rows : (i + 1) * rows, :] = dot(ref[...], weight[...]).astype(BF)


def out_project_kernel(n_blk, *refs):
    o_refs, w_refs = refs[:n_blk], refs[n_blk : 3 * n_blk]
    x_ref, gain_ref, mid_ref, n_ref = refs[3 * n_blk :]
    total = x_ref[...].astype(F32)
    for core in range(2):
        for k in range(n_blk):
            o = o_refs[k][core]
            o = jnp.concatenate([o[:, :HD], o[:, HP : HP + HD]], 1)
            total = total + dot(o, w_refs[core * n_blk + k][...])
    mid_ref[...] = total
    factor = lax.rsqrt(jnp.mean(total * total, -1, keepdims=True) + EPS)
    n_ref[...] = (total * factor * gain_ref[...]).astype(BF)


def branch_kernel(n_blk, *refs):
    w_refs = refs[: 2 * n_blk]
    local_ref, got_refs = refs[2 * n_blk], refs[2 * n_blk + 1 : 3 * n_blk]
    mid_ref, cot_ref, gain_ref, grad_ref, branch_ref, do_ref = refs[3 * n_blk :]
    total = local_ref[...]
    for ref in got_refs:
        total = total + ref[...].astype(F32)
    mid = mid_ref[...]
    factor = lax.rsqrt(jnp.mean(mid * mid, -1, keepdims=True) + EPS)
    grad = cot_ref[...].astype(F32) + norm_back(total, gain_ref[...], mid * factor, factor)
    grad_ref[...] = grad
    branch = grad.astype(BF)
    branch_ref[...] = branch
    zero = jnp.zeros((branch.shape[0], HP - HD), BF)
    for core in range(2):
        for k in range(n_blk):
            do = dot(branch, w_refs[core * n_blk + k][...], ((1,), (1,))).astype(BF)
            do_ref[core, k] = jnp.concatenate([do[:, :HD], zero, do[:, HD:], zero], 1)


def back_project_kernel(transposed, *refs):
    weight, own_ref, other_ref = refs[-3], refs[-2], refs[-1]
    dims = ((1,), (1,)) if transposed else ((1,), (0,))
    n_blk, rows = own_ref.shape[:2]
    for core in (1, 0):
        for k in range(n_blk):
            at = (core * n_blk + k) * rows
            value = refs[0][at : at + rows, :] if len(refs) == 4 else refs[k][core]
            part = dot(value, weight[...], dims)
            if core:
                other_ref[k] = part.astype(BF)
            else:
                own_ref[k] = part


def out_weight_kernel(count, *refs):
    o_ref, b_refs, out_ref = refs[0], refs[1 : 1 + count], refs[-1]
    rows = b_refs[0].shape[0]
    total = None
    for i, ref in enumerate(b_refs):
        one = dot(o_ref[i * rows : (i + 1) * rows, :], ref[...], ((0,), (0,)))
        total = one if total is None else total + one
    out_ref[:HD, :] = total[:HD].astype(BF)
    out_ref[HD:, :] = total[HP : HP + HD].astype(BF)


def qkv_weight_kernel(n_refs_count, *refs):
    n_refs, grad_ref, out_ref = refs[:n_refs_count], refs[-2], refs[-1]
    rows = n_refs[0].shape[0]
    total = None
    for i, ref in enumerate(n_refs):
        one = dot(ref[...], grad_ref[i * rows : (i + 1) * rows, :], ((0,), (0,)))
        total = one if total is None else total + one
    total = jnp.concatenate([total[:, g * HP : g * HP + HD] for g in range(4)], 1)
    n_head, n_dev, part, _ = out_ref.shape
    for dev in range(n_dev):
        for head in range(n_head):
            first = (dev * n_head + head) * part
            out_ref[head, dev] = total[first : first + part].astype(BF)


def qkv_weight_call(n_list, dqkv, n_head, n_plane):
    rows = n_list[0].shape[0]
    part = D // n_plane // n_head
    cols = 384
    steps = D // cols
    return pl.pallas_call(
        functools.partial(qkv_weight_kernel, len(n_list)),
        grid=(steps,),
        out_shape=jax.ShapeDtypeStruct((n_head, n_plane, part, 4 * HD), BF),
        in_specs=[pl.BlockSpec((rows, cols), lambda j: (0, j))] * len(n_list)
        + [pl.BlockSpec(dqkv.shape, lambda j: (0, 0), pipeline_mode=pl.Buffered(1))],
        out_specs=pl.BlockSpec((n_head, n_plane // steps, part, 4 * HD), lambda j: (0, j, 0, 0)),
        compiler_params=pltpu.CompilerParams(vmem_limit_bytes=48 << 20),
        cost_estimate=small_cost(
            flops=2 * len(n_list) * rows * D * 4 * HP * 2, transcendentals=0, bytes_accessed=12 << 20
        ),
        name="qkv_weight",
    )(*n_list, dqkv)


def after(value, *first):
    return lax.optimization_barrier((value,) + first)[0]


def swap(value, axis, mask):
    return lax.ppermute(value, axis, [(i, i ^ mask) for i in range(lax.axis_size(axis))])


class Stages:
    def __init__(self):
        self.last = ()

    def __call__(self, *trees):
        leaves, tree = jax.tree.flatten(trees)
        tied = lax.optimization_barrier(tuple(leaves) + self.last)
        self.last = (tied[0],)
        return jax.tree.unflatten(tree, tied[: len(leaves)])


def near(value):
    return swap(value, "blk", 1), swap(value, "blk", 2)


def far(one, two):
    half = one.shape[0] // 2
    return swap(one[:half], "blk", 2), swap(two[half:], "blk", 1)


def across(*values):
    return tuple(swap(v, "dp", 1) for v in values)


def chips(both):
    return [both[0]] + [swap(both[k], "blk", k) for k in range(1, len(both))]


def pair_up(mine, other):
    return [jnp.stack([mine[k], other[k]]) for k in range(mine.shape[0])]


def add_cores(own, other):
    return own + swap(other, "dp", 1).astype(F32)


def sum_far(parts):
    half = parts[3].shape[0] // 2
    return swap(parts[3][:half].astype(BF), "blk", 1), swap(parts[3][half:].astype(BF), "blk", 2)


def sum_near(parts, low, high):
    half = parts[3].shape[0] // 2
    one = jnp.concatenate([parts[1][:half], parts[1][half:] + high.astype(F32)])
    two = jnp.concatenate([parts[2][:half] + low.astype(F32), parts[2][half:]])
    return swap(one.astype(BF), "blk", 1), swap(two.astype(BF), "blk", 2)


def line_step(left, right):
    up = [(i, i + 1) for i in range(3)]
    return lax.ppermute(left, "head", up), lax.ppermute(right, "head", [(b, a) for a, b in up])


def rel_to_abs(value, reverse=False):
    n_blk = lax.axis_size("blk")
    mine = lax.axis_index("dp") * n_blk + lax.axis_index("blk")
    flat = value.reshape((2 * n_blk,) + value.shape[(1 if reverse else 2) :])
    out = jnp.stack([lax.dynamic_index_in_dim(flat, i ^ mine, 0, keepdims=False) for i in range(2 * n_blk)])
    return out.reshape((2, n_blk) + out.shape[1:]) if reverse else out


def per_device(
    activations,
    segments,
    cotangent,
    norm_gain_one,
    query_weight,
    key_weight,
    value_weight,
    output_weight,
    norm_gain_two,
    gate_weight,
    up_weight,
    down_weight,
):
    n_blk, n_head = lax.axis_size("blk"), lax.axis_size("head")
    n_plane = 2 * n_blk
    assert lax.axis_size("dp") == 2 and activations.shape[0] == 2 and n_plane == KVH
    sub = n_head // 4
    tok = activations.shape[2]
    span = tok * n_head
    own = 2 * tok
    rows = n_plane * own
    my_dp, my_blk, my_head = (lax.axis_index(name) for name in ("dp", "blk", "head"))
    my_seq, my_sub = my_head // sub, my_head % sub

    def routes(k):
        pairs = []
        for core in range(2):
            for head in range(n_head):
                seq_part, sub_part = head // sub, head % sub
                target = 2 * (k ^ (seq_part & 1)) + core
                pairs.append((core * n_head + head, (seq_part >> 1) * n_head + target * sub + sub_part))
        return pairs

    def to_plane(*values):
        parts = []
        for k in range(2):
            piece = [lax.dynamic_index_in_dim(v[:, 0], k ^ (my_seq & 1), 0, keepdims=False) for v in values]
            parts.append(lax.ppermute(jnp.concatenate(piece), ("dp", "head"), routes(k)))
        return parts

    def from_plane(value):
        parts = []
        for k in range(2):
            back = [(b, a) for a, b in routes(k)]
            parts.append(lax.ppermute(value[k * tok : (k + 1) * tok], ("dp", "head"), back))
        odd = (my_seq & 1) == 1
        return jnp.stack([jnp.where(odd, parts[1], parts[0]), jnp.where(odd, parts[0], parts[1])])

    me = my_dp * n_blk + my_blk
    ids = jnp.stack([me, my_head]).astype(jnp.int32)
    n_rows = D // n_plane
    part = n_rows // n_head
    ff_here = FF // n_plane
    width = 4 * HP
    assert span % width == 0
    seg_rows = span // width
    small_rows = -(-(2 + 2 * seg_rows) // 16) * 16
    gain_row = lambda v: jnp.pad(v, (0, width - n_rows))[None]
    small = [gain_row(norm_gain_one), gain_row(norm_gain_two), segments[:, 0].astype(BF).reshape(2 * seg_rows, width)]
    small.append(jnp.zeros((small_rows - 2 - 2 * seg_rows, width), BF))
    small = jnp.concatenate(small)
    fence = Stages()
    join = jnp.concatenate
    share = n_rows // 4

    def pack_qkv(*values):
        shape = jax.ShapeDtypeStruct((n_plane, n_rows + small_rows, 4 * HP), BF)
        packed = place_call(pack_qkv_kernel, shape, ids, *values, name="pack_qkv")
        return packed.reshape((2, n_blk) + packed.shape[1:])

    def pack_ff(gate, up):
        cut = [lax.dynamic_slice_in_dim(w, my_seq * share, share, 0) for w in (gate, up)]
        shape = jax.ShapeDtypeStruct((n_plane, share, 2 * ff_here), BF)
        packed = place_call(pack_ff_kernel, shape, ids, *cut, name="pack_ff")
        return packed.reshape((2, n_blk) + packed.shape[1:])

    near_out = near(output_weight)
    packed, act_low, cot_low, gate_low, up_low = fence(
        pack_qkv(query_weight, key_weight, value_weight, small), activations, cotangent, gate_weight, up_weight
    )
    both, near_out, act_low, cot_low, gate_low, up_low = fence(
        pair_up(packed[0], swap(packed[1], "dp", 1)), near_out, act_low, cot_low, gate_low, up_low
    )
    ff_packed = pack_ff(gate_low, up_low)
    got, x_parts, ff_both = fence(
        chips(both), to_plane(act_low, cot_low), pair_up(ff_packed[0], swap(ff_packed[1], "dp", 1))
    )
    qkv_w, seg_all, gains, x_low, cot, input_one = place_call(
        functools.partial(head_kernel, n_blk),
        (
            jax.ShapeDtypeStruct((D, width), BF),
            jax.ShapeDtypeStruct((n_plane, small_rows, width), BF),
            jax.ShapeDtypeStruct((2, 1, D), F32),
            jax.ShapeDtypeStruct((own, D), BF),
            jax.ShapeDtypeStruct((own, D), BF),
            jax.ShapeDtypeStruct((own, D), BF),
        ),
        ids,
        *got,
        *x_parts,
        name="head",
        scratch=[pltpu.VMEM((n_plane, small_rows, width), BF)],
    )
    gain_one, gain_two = gains[0, 0], gains[1, 0]
    seg_all = seg_all[:, 2 : 2 + 2 * seg_rows].reshape(2, n_blk, 2, span)
    seg_seq = lax.dynamic_index_in_dim(seg_all, my_seq & 1, 0, keepdims=False)
    seg_seq = lax.dynamic_index_in_dim(seg_seq, my_seq >> 1, 1, keepdims=False)
    chunks = seg_seq.astype(jnp.int32).reshape(n_blk * n_head, tok)

    def chunk_ids(sub_index):
        ids = []
        for core in range(2):
            for blk in range(n_blk):
                for k in range(2):
                    seq_part = 2 * (my_dp ^ core) + ((my_seq >> 1) ^ k)
                    ids.append((my_blk ^ blk) * n_head + seq_part * sub + sub_index)
        return ids

    def pos_seg(sub_index):
        ids = chunk_ids(sub_index)
        lane = jnp.arange(tok, dtype=jnp.int32)
        pos = jnp.concatenate([i * tok + lane for i in ids])
        seg = jnp.concatenate([lax.dynamic_index_in_dim(chunks, i, 0, keepdims=False) for i in ids])
        return pos, seg

    qpos, qseg = pos_seg(my_sub)
    if sub == 1:
        kpos, kseg = qpos, qseg
    else:
        every = [pos_seg(i) for i in range(sub)]
        kpos, kseg = (jnp.concatenate([e[i] for e in every]) for i in range(2))
    blocked = lambda v: v.reshape(-1, BLK)
    qb, qsb, kb, ksb = blocked(qpos), blocked(qseg), blocked(kpos), blocked(kseg)
    need = (
        (jnp.min(kb, 1)[None, :] <= jnp.max(qb, 1)[:, None])
        & (jnp.min(ksb, 1)[None, :] <= jnp.max(qsb, 1)[:, None])
        & (jnp.max(ksb, 1)[None, :] >= jnp.min(qsb, 1)[:, None])
    ).astype(jnp.int32)

    input_one, qkv_w, ff_both, cot = fence(input_one, qkv_w, ff_both, cot)
    near_one, side_one, ff_both = fence(near(input_one), across(input_one), ff_both)
    far_one, ff_got, near_one = fence(far(*near_one), chips(ff_both), near_one)
    far_one = join(far_one)
    more_one = across(*near_one)
    mine_one = [input_one, *near_one, far_one]
    all_one = fence(*mine_one, *side_one, *more_one, *across(far_one))

    def project_qkv(*values):
        shape = jax.ShapeDtypeStruct((rows, 4 * HP), BF)
        return simple_call(stack_project_kernel, shape, values, "project_qkv", 2 * rows * D * 4 * HP)

    qkv = project_qkv(*all_one, qkv_w)
    cot, *near_out = lax.optimization_barrier((cot, *near_out, all_one[-1]))[:-1]
    kv = ()
    if sub > 1:
        groups = [[s * sub + i for i in range(sub)] for s in range(4)]
        kv = (lax.all_gather(qkv[:, 2 * HP :], "head", axis=0, tiled=True, axis_index_groups=groups),)
    q_args = tuple(v.astype(F32).reshape(-1, 1, BLK) for v in (qpos, qseg, kpos, kseg))
    sharing = None if sub == 1 else [[s * sub + i for s in range(4)] for i in range(sub)]
    ff_all = jnp.stack(ff_got, 1).reshape(-1, 2 * ff_here)
    ff_all = lax.all_gather(ff_all, "head", axis=0, tiled=True, axis_index_groups=sharing)
    ff_all = ff_all.reshape(4, n_plane, share, 2 * ff_here)
    (o, lse), near_cot, far_out = fence(attend(need, qkv, *(kv or (None,)), *q_args), near(cot), far(*near_out))
    o_parts = o.reshape(2, n_blk, own, 2 * HP)
    mine_out = [output_weight, *near_out, join(far_out)]
    o_both, near_cot = fence(pair_up(o_parts[0], swap(o_parts[1], "dp", 1)), near_cot)
    o_got, side_out, near_cot = fence(chips(o_both), across(*mine_out), near_cot)
    all_out = [*mine_out, *side_out]

    def out_project(*values):
        shapes = (jax.ShapeDtypeStruct((own, D), F32), jax.ShapeDtypeStruct((own, D), BF))
        kernel = functools.partial(out_project_kernel, n_blk)
        return simple_call(kernel, shapes, values, "out_project", 2 * own * D * D)

    (x_mid, input_two), side_cot = fence(
        out_project(*o_got, *all_out, x_low, gain_two[None]), across(cot, *near_cot)
    )

    def unpack_ff(value):
        shapes = (jax.ShapeDtypeStruct((D, ff_here), BF),) * 2
        return place_call(unpack_ff_kernel, shapes, ids, value, name="unpack_ff")

    def ff_part(n_mine, n_side, c_mine, c_side):
        return ff_call(n_mine, n_side, c_mine, c_side, gate_w, up_w, down_weight)

    gate_w, up_w = unpack_ff(after(ff_all, input_two))
    side_two = across(input_two)
    near_two, part_0, near_cot, gate_w, up_w = fence(
        near(input_two), ff_part(input_two, side_two[0], cot, side_cot[0]), near_cot, gate_w, up_w
    )
    more_two = across(*near_two)
    far_two, far_cot, part_1, part_2 = fence(
        far(*near_two),
        far(*near_cot),
        ff_part(near_two[0], more_two[0], near_cot[0], side_cot[1]),
        ff_part(near_two[1], more_two[1], near_cot[1], side_cot[2]),
    )
    far_two, far_cot = join(far_two), join(far_cot)
    last_two, last_cot = across(far_two, far_cot)
    side_parts = across(part_0[3], part_1[3], part_2[3])
    part_3, side_parts = fence(ff_part(far_two, last_two, far_cot, last_cot), side_parts)
    parts = [part_0, part_1, part_2, part_3]
    side_parts = [*side_parts, *across(part_3[3])]
    hidden, grad_gu = [p[0] for p in parts], [p[1] for p in parts]
    all_two = [input_two, *near_two, far_two, *side_two, *more_two, last_two]
    all_cot = [cot, *near_cot, far_cot, *side_cot, last_cot]
    local_two = [p[2] + v.astype(F32) for p, v in zip(parts, side_parts)]
    local_0, sent_two = fence(local_two[0], [v.astype(BF) for v in local_two])
    got_two = chips(sent_two)[1:]

    contract = ((0,), (0,))

    def rel_parts(mine):
        return rel_to_abs(mine, True)

    def head_sum(sent):
        return lax.psum_scatter(sent, "head", scatter_dimension=0, tiled=True)

    def owned_rows(chunks):
        if n_head != 4:
            return chunks[0].reshape(-1, chunks[0].shape[-1]).astype(F32)
        shape = jax.ShapeDtypeStruct((4 * chunks[0].shape[0], chunks[0].shape[1]), F32)
        return place_call(place_rows_kernel, shape, ids, *chunks, name="place_rows")

    def owned_columns(chunks, widths):
        if n_head != 4:
            full = rel_to_abs(jnp.moveaxis(chunks[0], 0, 1).reshape((2, n_blk, n_head) + chunks[0].shape[2:]))
            full = full.reshape(n_plane, n_rows, -1).transpose(1, 0, 2).astype(F32)
            ends = [sum(widths[: i + 1]) for i in range(len(widths))]
            return [full[:, :, e - w : e].reshape(n_rows, -1) for e, w in zip(ends, widths)]
        shapes = [jax.ShapeDtypeStruct((n_rows, n_plane * w), F32) for w in widths]
        kernel = functools.partial(place_columns_kernel, widths, len(chunks))
        return place_call(kernel, shapes, ids, *chunks, name="place_columns")

    ff_sent, down_sent = ff_weight_call(all_two, all_cot, grad_gu, hidden, n_head, n_plane)
    got_two, ff_sent, down_sent = fence(got_two, ff_sent, down_sent)
    down_mine = head_sum(down_sent)
    ff_mine = head_sum(ff_sent.reshape(D, 2 * ff_here)).reshape(n_plane, part, 2 * ff_here)

    def branch(*values):
        shapes = (
            jax.ShapeDtypeStruct((own, D), F32),
            jax.ShapeDtypeStruct((own, D), BF),
            jax.ShapeDtypeStruct((2, n_blk, own, 2 * HP), BF),
        )
        kernel = functools.partial(branch_kernel, n_blk)
        return simple_call(kernel, shapes, values, "branch", 2 * own * D * D)

    grad_mid, grad_branch, grad_o = fence(*branch(*all_out, local_0, *got_two, x_mid, cot, gain_two[None]))

    def back_project(transposed, *values):
        shapes = tuple(jax.ShapeDtypeStruct((n_blk, own, D), t) for t in (F32, BF))
        kernel = functools.partial(back_project_kernel, transposed)
        return simple_call(kernel, shapes, values, "back_project", 2 * rows * D * values[-1].size // D)

    do_both, hidden = fence(pair_up(grad_o[0], swap(grad_o[1], "dp", 1)), hidden)
    out_own, out_other = back_project(False, *hidden, down_weight)
    do_got, out_own, out_side, grad_branch = fence(chips(do_both), out_own, swap(out_other, "dp", 1), grad_branch)
    grad_o = jnp.stack(do_got, 1).reshape(rows, 2 * HP)
    line = n_head == 4
    no_step = lambda *v: ()
    step = line_step if line else no_step
    back = attend_back(need, qkv, *(kv or (None,)), *q_args, o, lse, grad_o)
    dqkv, near_branch, out_own, out_side = fence(back, near(grad_branch), out_own, out_side)
    local_out = [out_own[k] + out_side[k].astype(F32) for k in range(n_blk)]
    if sub > 1:
        dkv = lax.psum_scatter(dqkv[1], "head", scatter_dimension=0, tiled=True, axis_index_groups=groups)
        dqkv = [join([dqkv[0], dkv], 1)]
    dqkv = dqkv[0]
    qkv_grad, far_branch, dqkv, ff_mine, local_out, far_sum = fence(
        qkv_weight_call(all_one, dqkv, n_head, n_plane), far(*near_branch), dqkv, ff_mine, local_out, sum_far(local_out)
    )
    qkv_mine = head_sum(qkv_grad.reshape(D, 4 * HD)).reshape(n_plane, part, 4 * HD)
    mine_branch = [grad_branch, *near_branch, join(far_branch)]
    ff_rel = rel_parts(ff_mine)
    (one_own, one_other), side_branch, ff_both, got_out, local_out_0 = fence(
        back_project(True, dqkv, qkv_w),
        across(*mine_branch),
        pair_up(ff_rel[0], swap(ff_rel[1], "dp", 1)),
        sum_near(local_out, *far_sum),
        local_out[0],
    )
    block_out = (x_mid + local_out_0 + sum(g.astype(F32) for g in got_out)).astype(BF)

    def out_weights(*values):
        rows_per = values[1].shape[0]
        lanes = pl.BlockSpec((rows_per, 384), lambda j: (0, j))
        return pl.pallas_call(
            functools.partial(out_weight_kernel, n_plane),
            grid=(D // 384,),
            out_shape=jax.ShapeDtypeStruct((2 * HD, D), BF),
            in_specs=[pl.BlockSpec(values[0].shape, lambda j: (0, 0), pipeline_mode=pl.Buffered(1))] + [lanes] * n_plane,
            out_specs=pl.BlockSpec((2 * HD, 384), lambda j: (0, j)),
            compiler_params=pltpu.CompilerParams(vmem_limit_bytes=48 << 20),
            cost_estimate=small_cost(flops=4 * rows * D * 2 * HP, transcendentals=0, bytes_accessed=9 << 20),
            name="out_weight",
        )(*values)

    one_side = swap(one_other, "dp", 1)
    local_one = [one_own[k] + one_side[k].astype(F32) for k in range(n_blk)]
    ff_got, out_grad, local_0, sent_one, down_mine = fence(
        chips(ff_both),
        out_weights(o, *mine_branch, *side_branch),
        local_one[0],
        [v.astype(BF) for v in local_one],
        down_mine,
    )
    out_mine = head_sum(out_grad)
    late_down = lax.all_gather(down_mine, "head", axis=0)
    ff_rows = jnp.stack(ff_got, 1).reshape(ff_mine.shape)
    ff_0 = step(ff_rows, ff_rows)
    got_one, ff_1, ff_0, qkv_mine, out_mine, block_out = fence(
        chips(sent_one)[1:], step(*ff_0), ff_0, qkv_mine, out_mine, block_out
    )
    normed, factor = normalize(x_low.astype(F32))
    grad_in_one = local_0 + sum(g.astype(F32) for g in got_one)
    grad_input = (grad_mid + norm_back(grad_in_one, gain_one, normed, factor)).astype(BF)
    qkv_rel = rel_parts(qkv_mine)
    qkv_both = pair_up(qkv_rel[0], swap(qkv_rel[1], "dp", 1))
    qkv_rows, ff_2, grad_input, block_out, out_mine = fence(
        chips(qkv_both), step(*ff_1), grad_input, block_out, out_mine
    )
    late = join([jnp.stack(qkv_rows, 1).reshape(-1, 4 * HD), out_mine.reshape(-1, 4 * HD)])
    late = lax.all_gather(late, "head", axis=0)
    grad_input = from_plane(grad_input)
    block_out = from_plane(block_out)
    grad_down = late_down.reshape(-1, D).astype(F32)
    late_qkv = late[:, : n_plane * part].reshape(n_head, n_plane, part, 4 * HD)
    late_out = late[:, n_plane * part :].reshape(n_head, part, D)
    each = lambda v: [v[i] for i in range(4)] if line else [v]
    if line:
        ff_chunks = [ff_2[0], ff_1[0], ff_0[0], ff_rows, ff_0[1], ff_1[1], ff_2[1]]
    else:
        ff_chunks = [lax.all_gather(ff_rows, "head", axis=0)]
    grad_gate_w, grad_up_w = owned_columns(ff_chunks, (ff_here, ff_here))
    grad_query, grad_key, grad_value = owned_columns(each(late_qkv), (2 * HD, HD, HD))
    grad_out = owned_rows(each(late_out))

    def gain_grad(gain, *pairs):
        return sum(jnp.sum(w.astype(F32) * g, -1) for w, g in pairs) / gain.astype(F32)

    grad_gain_one = gain_grad(
        norm_gain_one, (query_weight, grad_query), (key_weight, grad_key), (value_weight, grad_value)
    )
    grad_gain_two = gain_grad(norm_gain_two, (gate_weight, grad_gate_w), (up_weight, grad_up_w))
    return (
        block_out[:, None],
        grad_input[:, None],
        grad_gain_one,
        grad_query,
        grad_key,
        grad_value,
        grad_out,
        grad_gain_two,
        grad_gate_w,
        grad_up_w,
        grad_down,
    )


def solution(mesh):
    tokens = P(None, "dp", ("blk", "head"), None)
    vector = P(("dp", "blk"))
    matrix = P(("dp", "blk"), None)
    return jax.shard_map(
        per_device,
        mesh=mesh,
        in_specs=(
            tokens,
            P(None, "dp", "blk"),
            tokens,
            vector,
            matrix,
            matrix,
            matrix,
            matrix,
            vector,
            matrix,
            matrix,
            matrix,
        ),
        out_specs=(tokens, tokens, vector, matrix, matrix, matrix, matrix, vector, matrix, matrix, matrix),
        check_vma=False,
    )
```

```python
import functools
import math

import jax
import jax.numpy as jnp
from jax import lax
from jax.experimental import pallas as pl
from jax.experimental.pallas import tpu as pltpu
from jax.sharding import PartitionSpec as P

D = 1536
QH = 16
KVH = 8
HD = 96
HP = 128
FF = 4096
EPS = 1e-05
NEG = -1e30
BLK = 256
BF = jnp.bfloat16
F32 = jnp.float32


def small_cost(flops, transcendentals, bytes_accessed):
    part = 64
    return pl.CostEstimate(
        flops=flops // part, transcendentals=transcendentals // part, bytes_accessed=bytes_accessed // part
    )


def dot(left, right, dims=((1,), (0,))):
    return lax.dot_general(left, right, (dims, ((), ())), preferred_element_type=F32)


def normalize(values):
    factor = lax.rsqrt(jnp.mean(values * values, -1, keepdims=True) + EPS)
    return values * factor, factor


def norm_back(grad_norm, gain, normed, factor):
    scaled = grad_norm * gain
    return factor * (scaled - normed * jnp.mean(scaled * normed, -1, keepdims=True))


def rows_of(index):
    return pl.ds(pl.multiple_of(index * BLK, BLK), BLK)


def as_column(row):
    return jnp.broadcast_to(row, (HP, BLK)).T[:, 0:1]


def as_row(col):
    return jnp.broadcast_to(col, (BLK, HP)).T[0:1, :]


def keys_to_columns(kp_ref, ks_ref, pos_sc, seg_sc):
    def one(j, _):
        pos_sc[rows_of(j), :] = as_column(kp_ref[j])
        seg_sc[rows_of(j), :] = as_column(ks_ref[j])
        return 0

    lax.fori_loop(0, kp_ref.shape[0], one, 0)


def attn_fwd_kernel(first, need, q_ref, kv_ref, qp_ref, qs_ref, kp_ref, ks_ref, o_ref, lse_ref, m_sc, l_sc, acc_sc, pos_sc, seg_sc):
    scale = 1.0 / math.sqrt(HD)
    n_q, n_k = q_ref.shape[0] // BLK, kv_ref.shape[0] // BLK
    k_cols, v_cols = slice(first, first + HP), slice(first + HP, first + 2 * HP)
    keys_to_columns(kp_ref, ks_ref, pos_sc, seg_sc)

    def one_query(i, _):
        qr = rows_of(i)
        m_sc[...] = jnp.full_like(m_sc, NEG)
        l_sc[...] = jnp.zeros_like(l_sc)
        acc_sc[...] = jnp.zeros_like(acc_sc)
        qpos, qseg = qp_ref[i], qs_ref[i]

        def one_key(j, _):
            @pl.when(need[i, j] != 0)
            def _():
                kr = rows_of(j)
                ok = (pos_sc[kr, :] <= qpos) & (seg_sc[kr, :] == qseg)
                k, v = kv_ref[kr, k_cols], kv_ref[kr, v_cols]
                state = [(m_sc[g], l_sc[g], acc_sc[g], q_ref[qr, g * HP : (g + 1) * HP]) for g in range(2)]
                scores = [jnp.where(ok, dot(k, q, ((1,), (1,))) * scale, NEG) for _, _, _, q in state]
                new = []
                for (m_old, l_old, acc_old, _), s in zip(state, scores):
                    m_new = jnp.maximum(m_old, jnp.max(s, 0, keepdims=True))
                    p = jnp.where(ok, jnp.exp(s - m_new), 0.0)
                    decay = jnp.exp(m_old - m_new)
                    total = l_old * decay + jnp.sum(p, 0, keepdims=True)
                    new.append((m_new, total, acc_old * decay + dot(v, p.astype(BF), ((0,), (0,)))))
                for g in range(2):
                    m_sc[g], l_sc[g], acc_sc[g] = new[g]

            return 0

        lax.fori_loop(0, n_k, one_key, 0)
        for g in range(2):
            o_ref[qr, g * HP : (g + 1) * HP] = (acc_sc[g] / l_sc[g]).T.astype(BF)
            lse_ref[i, g : g + 1, :] = m_sc[g] + jnp.log(l_sc[g])
        return 0

    lax.fori_loop(0, n_q, one_query, 0)


def attn_bwd_kernel(first, need, q_ref, kv_ref, qp_ref, qs_ref, kp_ref, ks_ref, o_ref, lse_ref, do_ref, *rest):
    dq_ref, dkv_ref = rest[0], rest[-6]
    dq_sc, dk_sc, dv_sc, pos_sc, seg_sc = rest[-5:]
    scale = 1.0 / math.sqrt(HD)
    n_q, n_k = q_ref.shape[0] // BLK, kv_ref.shape[0] // BLK
    k_cols, v_cols = slice(first, first + HP), slice(first + HP, first + 2 * HP)
    dk_sc[...] = jnp.zeros_like(dk_sc)
    dv_sc[...] = jnp.zeros_like(dv_sc)
    keys_to_columns(kp_ref, ks_ref, pos_sc, seg_sc)

    def one_query(i, _):
        qr = rows_of(i)
        dq_sc[...] = jnp.zeros_like(dq_sc)
        qpos, qseg = qp_ref[i], qs_ref[i]
        lse, delta = [], []
        for g in range(2):
            cols = slice(g * HP, (g + 1) * HP)
            lse.append(lse_ref[i, g : g + 1, :])
            prod = do_ref[qr, cols].astype(F32) * o_ref[qr, cols].astype(F32)
            delta.append(as_row(jnp.sum(prod, -1, keepdims=True)))

        def one_key(j, _):
            @pl.when(need[i, j] != 0)
            def _():
                kr = rows_of(j)
                ok = (pos_sc[kr, :] <= qpos) & (seg_sc[kr, :] == qseg)
                k, v = kv_ref[kr, k_cols], kv_ref[kr, v_cols]
                qs = [q_ref[qr, g * HP : (g + 1) * HP] for g in range(2)]
                dos = [do_ref[qr, g * HP : (g + 1) * HP] for g in range(2)]
                scores = [dot(k, q, ((1,), (1,))) * scale for q in qs]
                dps = [dot(v, do, ((1,), (1,))) for do in dos]
                dv, dk = dv_sc[kr, :], dk_sc[kr, :]
                dqs = []
                for g in range(2):
                    p = jnp.where(ok, jnp.exp(scores[g] - lse[g]), 0.0)
                    ds = (p * (dps[g] - delta[g])).astype(BF)
                    dv = dv + dot(p.astype(BF), dos[g])
                    dk = dk + dot(ds, qs[g])
                    dqs.append(dot(ds, k, ((0,), (0,))))
                dv_sc[kr, :], dk_sc[kr, :] = dv, dk
                for g in range(2):
                    dq_sc[g] += dqs[g]

            return 0

        lax.fori_loop(0, n_k, one_key, 0)
        for g in range(2):
            dq_ref[qr, g * HP : (g + 1) * HP] = (dq_sc[g] * scale).astype(BF)
        return 0

    lax.fori_loop(0, n_q, one_query, 0)
    dkv_ref[:, k_cols] = (dk_sc[...] * scale).astype(BF)
    dkv_ref[:, v_cols] = dv_sc[...].astype(BF)


def in_vmem(count):
    return [pl.BlockSpec(memory_space=pltpu.SMEM)] + [pl.BlockSpec(memory_space=pltpu.VMEM)] * count


def attn_cost(n_q, n_k, products):
    return small_cost(
        flops=2 * products * n_q * n_k * 2 * HP, transcendentals=n_q * n_k * 2, bytes_accessed=(n_q + n_k) * HP * 16
    )


def attend(need, q, kv, qpos, qseg, kpos, kseg):
    first, kv = (2 * HP, q) if kv is None else (0, kv)
    n_q, n_k = q.shape[0], kv.shape[0]
    return pl.pallas_call(
        functools.partial(attn_fwd_kernel, first),
        out_shape=(jax.ShapeDtypeStruct((n_q, 2 * HP), BF), jax.ShapeDtypeStruct((n_q // BLK, 2, BLK), F32)),
        in_specs=in_vmem(6),
        out_specs=(pl.BlockSpec(memory_space=pltpu.VMEM),) * 2,
        scratch_shapes=[pltpu.VMEM((2, 1, BLK), F32)] * 2 + [pltpu.VMEM((2, HP, BLK), F32)] + [pltpu.VMEM((n_k, 1), F32)] * 2,
        compiler_params=pltpu.CompilerParams(vmem_limit_bytes=40 << 20),
        cost_estimate=attn_cost(n_q, n_k, 2),
        name="attn_fwd",
    )(need, q, kv, qpos, qseg, kpos, kseg)


def attend_back(need, q, kv, qpos, qseg, kpos, kseg, o, lse, do):
    joint = kv is None
    first, kv = (2 * HP, q) if joint else (0, kv)
    n_q, n_k = q.shape[0], kv.shape[0]
    shapes = [jax.ShapeDtypeStruct((n_q, 4 * HP), BF)] if joint else [jax.ShapeDtypeStruct((n, 2 * HP), BF) for n in (n_q, n_k)]
    return pl.pallas_call(
        functools.partial(attn_bwd_kernel, first),
        out_shape=shapes,
        in_specs=in_vmem(9),
        out_specs=[pl.BlockSpec(memory_space=pltpu.VMEM)] * len(shapes),
        scratch_shapes=[pltpu.VMEM((2, BLK, HP), F32)] + [pltpu.VMEM((n_k, HP), F32)] * 2 + [pltpu.VMEM((n_k, 1), F32)] * 2,
        compiler_params=pltpu.CompilerParams(vmem_limit_bytes=48 << 20),
        cost_estimate=attn_cost(n_q, n_k, 5),
        name="attn_bwd",
    )(need, q, kv, qpos, qseg, kpos, kseg, o, lse, do)


def whole(count):
    return [pl.BlockSpec(memory_space=pltpu.VMEM)] * count


def place_call(kernel, out_shape, ids, *values, name, scratch=()):
    moved = sum(v.size * v.dtype.itemsize for v in values)
    return pl.pallas_call(
        kernel,
        out_shape=out_shape,
        in_specs=[pl.BlockSpec(memory_space=pltpu.SMEM)] + whole(len(values)),
        out_specs=jax.tree.map(lambda _: pl.BlockSpec(memory_space=pltpu.VMEM), out_shape),
        scratch_shapes=scratch,
        compiler_params=pltpu.CompilerParams(vmem_limit_bytes=40 << 20),
        cost_estimate=small_cost(flops=0, transcendentals=0, bytes_accessed=2 * moved),
        name=name,
    )(ids, *values)


def pack_qkv_kernel(ids, q_ref, k_ref, v_ref, small_ref, out_ref):
    rows = q_ref.shape[0]
    zero = jnp.zeros((rows, HP - HD), BF)
    for dev in range(KVH):
        slot = ids[0] ^ dev
        heads = [(q_ref, 2 * dev), (q_ref, 2 * dev + 1), (k_ref, dev), (v_ref, dev)]
        for i, (ref, head) in enumerate(heads):
            piece = ref[:, head * HD : (head + 1) * HD]
            out_ref[slot, :rows, i * HP : (i + 1) * HP] = jnp.concatenate([piece, zero], 1)
        out_ref[slot, rows:, :] = small_ref[...]


def pack_ff_kernel(ids, gate_ref, up_ref, out_ref):
    width = gate_ref.shape[1] // KVH
    for dev in range(KVH):
        slot = ids[0] ^ dev
        for i, ref in enumerate((gate_ref, up_ref)):
            out_ref[slot, :, i * width : (i + 1) * width] = ref[:, dev * width : (dev + 1) * width]


def head_kernel(n_blk, ids, *refs):
    got, x_refs = refs[:n_blk], refs[n_blk : n_blk + 2]
    w_ref, seg_ref, gain_ref, x_ref, c_ref, n_ref, small_sc = refs[n_blk + 2 :]
    n_rows = w_ref.shape[0] // (2 * n_blk)
    for k, ref in enumerate(got):
        for core in range(2):
            at = pl.multiple_of((ids[0] ^ (core * n_blk + k)) * n_rows, 16)
            w_ref[pl.ds(at, n_rows), :] = ref[core, :n_rows, :]
            small_sc[core * n_blk + k] = ref[core, n_rows:, :]
    gains = [[], []]
    for dev in range(2 * n_blk):
        small = small_sc[ids[0] ^ dev]
        seg_ref[dev] = small
        small = small.astype(F32)
        for i in range(2):
            gains[i].append(small[i : i + 1, :n_rows])
    for i in range(2):
        gain_ref[i] = jnp.concatenate(gains[i], 1)
    tok = x_refs[0].shape[0] // 2
    for i, ref in enumerate(x_refs):
        x = ref[:tok, :]
        x_ref[i * tok : (i + 1) * tok, :] = x
        c_ref[i * tok : (i + 1) * tok, :] = ref[tok:, :]
        x = x.astype(F32)
        factor = lax.rsqrt(jnp.mean(x * x, -1, keepdims=True) + EPS)
        n_ref[i * tok : (i + 1) * tok, :] = (x * factor * gain_ref[0]).astype(BF)


def unpack_ff_kernel(ids, in_ref, gate_ref, up_ref):
    n_head, n_slot, part, width = in_ref.shape
    for head in range(n_head):
        for slot in range(n_slot):
            at = pl.ds(pl.multiple_of(((ids[0] ^ slot) * n_head + head) * part, 16), part)
            gate_ref[at, :] = in_ref[head, slot, :, : width // 2]
            up_ref[at, :] = in_ref[head, slot, :, width // 2 :]


def chunk_heads(ids, count):
    if count == 7:
        return [(ids[1] + (i - 3), (ids[1] + (i - 3) >= 0) & (ids[1] + (i - 3) < 4)) for i in range(7)]
    return [(i, None) for i in range(count)]


def place_chunk(ok, body):
    if ok is None:
        body()
    else:
        pl.when(ok)(body)


def place_rows_kernel(ids, *refs):
    out_ref = refs[-1]
    part = refs[0].shape[0]
    for ref, (head, ok) in zip(refs[:-1], chunk_heads(ids, len(refs) - 1)):

        def body():
            out_ref[pl.ds(pl.multiple_of(head * part, 16), part), :] = ref[...].astype(F32)

        place_chunk(ok, body)


def place_columns_kernel(widths, count, ids, *refs):
    chunks, outs = refs[:count], refs[count:]
    n_slot, part = chunks[0].shape[:2]
    for ref, (head, ok) in zip(chunks, chunk_heads(ids, count)):

        def body():
            at = pl.ds(pl.multiple_of(head * part, 16), part)
            first = 0
            for out_ref, width in zip(outs, widths):
                for pair in range(0, n_slot, 2):
                    both = [ref[ids[0] ^ dev][:, first : first + width] for dev in (pair, pair + 1)]
                    out_ref[at, pair * width : (pair + 2) * width] = jnp.concatenate(both, 1).astype(F32)
                first += width

        place_chunk(ok, body)


def last_kernel(ids, in_ref, q_w, k_w, v_w, gain_ref, q_ref, k_ref, v_ref, out_ref, sum_ref):
    n_head = in_ref.shape[0]
    n_rows = q_w.shape[0]
    part = n_rows // n_head
    n_slot = 2 * (q_w.shape[1] // (4 * HD))
    for head in range(n_head):
        at = slice(head * part, (head + 1) * part)
        for pair in range(0, n_slot, 2):
            two = [in_ref[head, pl.ds(pl.multiple_of((ids[0] ^ dev) * part, 16), part), :] for dev in (pair, pair + 1)]
            for ref, first, width in ((q_ref, 0, 2 * HD), (k_ref, 2 * HD, HD), (v_ref, 3 * HD, HD)):
                both = jnp.concatenate([v[:, first : first + width] for v in two], 1)
                ref[at, pair * width : (pair + 2) * width] = both.astype(F32)
        for i in range(D // (4 * HD)):
            rows = slice((n_slot + i) * part, (n_slot + i + 1) * part)
            out_ref[at, i * 4 * HD : (i + 1) * 4 * HD] = in_ref[head, rows, :].astype(F32)
    total = None
    for w, g in ((q_w, q_ref), (k_w, k_ref), (v_w, v_ref)):
        one = jnp.sum(w[...].astype(F32) * g[...], -1, keepdims=True)
        total = one if total is None else total + one
    sum_ref[...] = jnp.broadcast_to(total, (n_rows, 128)).T[0:1, :] / gain_ref[...]


def ff_kernel(n0, n1, c0, c1, gate_ref, up_ref, down_ref, hid_ref, dgu_ref, own_ref, other_ref):
    width = gate_ref.shape[1]
    for i, (n_ref, c_ref) in ((1, (n1, c1)), (0, (n0, c0))):
        n = n_ref[...]
        gate = dot(n, gate_ref[...])
        up = dot(n, up_ref[...])
        grad = dot(c_ref[...], down_ref[...], ((1,), (1,)))
        sigma = jax.nn.sigmoid(gate)
        silu = gate * sigma
        hid_ref[i] = (silu * up).astype(BF)
        grad_gate = (grad * up * sigma * (1.0 + gate * (1.0 - sigma))).astype(BF)
        grad_up = (grad * silu).astype(BF)
        dgu_ref[i, :, :width] = grad_gate
        dgu_ref[i, :, width:] = grad_up
        total = dot(grad_gate, gate_ref[...], ((1,), (1,))) + dot(grad_up, up_ref[...], ((1,), (1,)))
        if i == 0:
            own_ref[...] = total
        else:
            other_ref[...] = total.astype(BF)


def ff_call(n0, n1, c0, c1, gate_w, up_w, down_w):
    rows, width = n0.shape[0], gate_w.shape[1]
    return pl.pallas_call(
        ff_kernel,
        out_shape=(
            jax.ShapeDtypeStruct((2, rows, width), BF),
            jax.ShapeDtypeStruct((2, rows, 2 * width), BF),
            jax.ShapeDtypeStruct((rows, D), F32),
            jax.ShapeDtypeStruct((rows, D), BF),
        ),
        in_specs=whole(7),
        out_specs=tuple(whole(4)),
        compiler_params=pltpu.CompilerParams(vmem_limit_bytes=40 << 20),
        cost_estimate=small_cost(
            flops=2 * 2 * rows * D * width * 5, transcendentals=2 * rows * width, bytes_accessed=12 << 20
        ),
        name="ff",
    )(n0, n1, c0, c1, gate_w, up_w, down_w)


def ff_weight_kernel(n_pairs, *refs):
    n_refs, c_refs = refs[: 2 * n_pairs], refs[2 * n_pairs : 4 * n_pairs]
    dgu_refs, hid_refs = refs[4 * n_pairs : 5 * n_pairs], refs[5 * n_pairs : 6 * n_pairs]
    ff_ref, down_ref = refs[6 * n_pairs :]
    over = ((0,), (0,))
    total_ff = total_down = None
    for i in range(2 * n_pairs):
        core, k = i // n_pairs, i % n_pairs
        one = dot(n_refs[i][...], dgu_refs[k][core], over)
        two = dot(hid_refs[k][core], c_refs[i][...], over)
        total_ff = one if total_ff is None else total_ff + one
        total_down = two if total_down is None else total_down + two
    n_head, n_dev, part, width = ff_ref.shape
    for dev in range(n_dev):
        for head in range(n_head):
            first = (dev * n_head + head) * part
            ff_ref[head, dev] = total_ff[first : first + part].astype(BF)
    down_ref[...] = total_down.astype(BF)


def ff_weight_call(n_list, c_list, dgu_list, hid_list, n_head, n_plane):
    n_pairs = len(dgu_list)
    rows, width2 = n_list[0].shape[0], dgu_list[0].shape[2]
    part = D // n_plane // n_head
    cols = 384
    steps = D // cols
    lanes = pl.BlockSpec((rows, cols), lambda j: (0, j))
    fixed = lambda v: pl.BlockSpec(v.shape, lambda j: (0, 0, 0), pipeline_mode=pl.Buffered(1))
    per_step = n_plane // steps
    return pl.pallas_call(
        functools.partial(ff_weight_kernel, n_pairs),
        grid=(steps,),
        out_shape=(
            jax.ShapeDtypeStruct((n_head, n_plane, part, width2), BF),
            jax.ShapeDtypeStruct((width2 // 2, D), BF),
        ),
        in_specs=[lanes] * (4 * n_pairs) + [fixed(v) for v in dgu_list] + [fixed(v) for v in hid_list],
        out_specs=(
            pl.BlockSpec((n_head, per_step, part, width2), lambda j: (0, j, 0, 0)),
            pl.BlockSpec((width2 // 2, cols), lambda j: (0, j)),
        ),
        compiler_params=pltpu.CompilerParams(vmem_limit_bytes=56 << 20),
        cost_estimate=small_cost(
            flops=2 * 2 * n_pairs * rows * D * width2 * 3 // 2, transcendentals=0, bytes_accessed=24 << 20
        ),
        name="ff_weight",
    )(*n_list, *c_list, *dgu_list, *hid_list)


def simple_call(kernel, out_shape, values, name, flops):
    leaves = jax.tree.leaves(out_shape)
    moved = sum(v.size * v.dtype.itemsize for v in list(values) + leaves)
    return pl.pallas_call(
        kernel,
        out_shape=out_shape,
        in_specs=whole(len(values)),
        out_specs=jax.tree.map(lambda _: pl.BlockSpec(memory_space=pltpu.VMEM), out_shape),
        compiler_params=pltpu.CompilerParams(vmem_limit_bytes=52 << 20),
        cost_estimate=small_cost(flops=flops, transcendentals=0, bytes_accessed=moved),
        name=name,
    )(*values)


def stack_project_kernel(*refs):
    weight, out_ref = refs[-2], refs[-1]
    rows = refs[0].shape[0]
    for i, ref in enumerate(refs[:-2]):
        out_ref[i * rows : (i + 1) * rows, :] = dot(ref[...], weight[...]).astype(BF)


def out_project_kernel(n_blk, *refs):
    o_refs, w_refs = refs[:n_blk], refs[n_blk : 3 * n_blk]
    x_ref, gain_ref, mid_ref, n_ref = refs[3 * n_blk :]
    total = x_ref[...].astype(F32)
    for core in range(2):
        for k in range(n_blk):
            o = o_refs[k][core]
            o = jnp.concatenate([o[:, :HD], o[:, HP : HP + HD]], 1)
            total = total + dot(o, w_refs[core * n_blk + k][...])
    mid_ref[...] = total
    factor = lax.rsqrt(jnp.mean(total * total, -1, keepdims=True) + EPS)
    n_ref[...] = (total * factor * gain_ref[...]).astype(BF)


def branch_kernel(n_blk, *refs):
    w_refs = refs[: 2 * n_blk]
    local_ref, got_refs = refs[2 * n_blk], refs[2 * n_blk + 1 : 3 * n_blk]
    mid_ref, cot_ref, gain_ref, grad_ref, branch_ref, do_ref = refs[3 * n_blk :]
    total = local_ref[...]
    for ref in got_refs:
        total = total + ref[...].astype(F32)
    mid = mid_ref[...]
    factor = lax.rsqrt(jnp.mean(mid * mid, -1, keepdims=True) + EPS)
    grad = cot_ref[...].astype(F32) + norm_back(total, gain_ref[...], mid * factor, factor)
    grad_ref[...] = grad
    branch = grad.astype(BF)
    branch_ref[...] = branch
    zero = jnp.zeros((branch.shape[0], HP - HD), BF)
    for core in range(2):
        for k in range(n_blk):
            do = dot(branch, w_refs[core * n_blk + k][...], ((1,), (1,))).astype(BF)
            do_ref[core, k] = jnp.concatenate([do[:, :HD], zero, do[:, HD:], zero], 1)


def back_project_kernel(transposed, *refs):
    weight, own_ref, other_ref = refs[-3], refs[-2], refs[-1]
    dims = ((1,), (1,)) if transposed else ((1,), (0,))
    n_blk, rows = own_ref.shape[:2]
    for core in (1, 0):
        for k in range(n_blk):
            at = (core * n_blk + k) * rows
            value = refs[0][at : at + rows, :] if len(refs) == 4 else refs[k][core]
            part = dot(value, weight[...], dims)
            if core:
                other_ref[k] = part.astype(BF)
            else:
                own_ref[k] = part


def out_weight_kernel(count, *refs):
    o_ref, b_refs, out_ref = refs[0], refs[1 : 1 + count], refs[-1]
    rows = b_refs[0].shape[0]
    total = None
    for i, ref in enumerate(b_refs):
        one = dot(o_ref[i * rows : (i + 1) * rows, :], ref[...], ((0,), (0,)))
        total = one if total is None else total + one
    out_ref[:HD, :] = total[:HD].astype(BF)
    out_ref[HD:, :] = total[HP : HP + HD].astype(BF)


def qkv_weight_kernel(n_refs_count, *refs):
    n_refs, grad_ref, out_ref = refs[:n_refs_count], refs[-2], refs[-1]
    rows = n_refs[0].shape[0]
    total = None
    for i, ref in enumerate(n_refs):
        one = dot(ref[...], grad_ref[i * rows : (i + 1) * rows, :], ((0,), (0,)))
        total = one if total is None else total + one
    total = jnp.concatenate([total[:, g * HP : g * HP + HD] for g in range(4)], 1)
    n_head, n_dev, part, _ = out_ref.shape
    for dev in range(n_dev):
        for head in range(n_head):
            first = (dev * n_head + head) * part
            out_ref[head, dev] = total[first : first + part].astype(BF)


def qkv_weight_call(n_list, dqkv, n_head, n_plane):
    rows = n_list[0].shape[0]
    part = D // n_plane // n_head
    cols = 384
    steps = D // cols
    return pl.pallas_call(
        functools.partial(qkv_weight_kernel, len(n_list)),
        grid=(steps,),
        out_shape=jax.ShapeDtypeStruct((n_head, n_plane, part, 4 * HD), BF),
        in_specs=[pl.BlockSpec((rows, cols), lambda j: (0, j))] * len(n_list)
        + [pl.BlockSpec(dqkv.shape, lambda j: (0, 0), pipeline_mode=pl.Buffered(1))],
        out_specs=pl.BlockSpec((n_head, n_plane // steps, part, 4 * HD), lambda j: (0, j, 0, 0)),
        compiler_params=pltpu.CompilerParams(vmem_limit_bytes=48 << 20),
        cost_estimate=small_cost(
            flops=2 * len(n_list) * rows * D * 4 * HP * 2, transcendentals=0, bytes_accessed=12 << 20
        ),
        name="qkv_weight",
    )(*n_list, dqkv)


def after(value, *first):
    return lax.optimization_barrier((value,) + first)[0]


def swap(value, axis, mask):
    return lax.ppermute(value, axis, [(i, i ^ mask) for i in range(lax.axis_size(axis))])


class Stages:
    def __init__(self):
        self.last = ()

    def __call__(self, *trees):
        leaves, tree = jax.tree.flatten(trees)
        tied = lax.optimization_barrier(tuple(leaves) + self.last)
        self.last = (tied[0],)
        return jax.tree.unflatten(tree, tied[: len(leaves)])


def near(value):
    return swap(value, "blk", 1), swap(value, "blk", 2)


def far(one, two):
    half = one.shape[0] // 2
    return swap(one[:half], "blk", 2), swap(two[half:], "blk", 1)


def across(*values):
    return tuple(swap(v, "dp", 1) for v in values)


def chips(both):
    return [both[0]] + [swap(both[k], "blk", k) for k in range(1, len(both))]


def pair_up(mine, other):
    return [jnp.stack([mine[k], other[k]]) for k in range(mine.shape[0])]


def add_cores(own, other):
    return own + swap(other, "dp", 1).astype(F32)


def sum_far(parts):
    half = parts[3].shape[0] // 2
    return swap(parts[3][:half].astype(BF), "blk", 1), swap(parts[3][half:].astype(BF), "blk", 2)


def sum_near(parts, low, high):
    half = parts[3].shape[0] // 2
    one = jnp.concatenate([parts[1][:half], parts[1][half:] + high.astype(F32)])
    two = jnp.concatenate([parts[2][:half] + low.astype(F32), parts[2][half:]])
    return swap(one.astype(BF), "blk", 1), swap(two.astype(BF), "blk", 2)


def line_step(left, right):
    up = [(i, i + 1) for i in range(3)]
    return lax.ppermute(left, "head", up), lax.ppermute(right, "head", [(b, a) for a, b in up])


def rel_to_abs(value, reverse=False):
    n_blk = lax.axis_size("blk")
    mine = lax.axis_index("dp") * n_blk + lax.axis_index("blk")
    flat = value.reshape((2 * n_blk,) + value.shape[(1 if reverse else 2) :])
    out = jnp.stack([lax.dynamic_index_in_dim(flat, i ^ mine, 0, keepdims=False) for i in range(2 * n_blk)])
    return out.reshape((2, n_blk) + out.shape[1:]) if reverse else out


def per_device(
    activations,
    segments,
    cotangent,
    norm_gain_one,
    query_weight,
    key_weight,
    value_weight,
    output_weight,
    norm_gain_two,
    gate_weight,
    up_weight,
    down_weight,
):
    n_blk, n_head = lax.axis_size("blk"), lax.axis_size("head")
    n_plane = 2 * n_blk
    assert lax.axis_size("dp") == 2 and activations.shape[0] == 2 and n_plane == KVH
    sub = n_head // 4
    tok = activations.shape[2]
    span = tok * n_head
    own = 2 * tok
    rows = n_plane * own
    my_dp, my_blk, my_head = (lax.axis_index(name) for name in ("dp", "blk", "head"))
    my_seq, my_sub = my_head // sub, my_head % sub

    def routes(k):
        pairs = []
        for core in range(2):
            for head in range(n_head):
                seq_part, sub_part = head // sub, head % sub
                target = 2 * (k ^ (seq_part & 1)) + core
                pairs.append((core * n_head + head, (seq_part >> 1) * n_head + target * sub + sub_part))
        return pairs

    def to_plane(*values):
        parts = []
        for k in range(2):
            piece = [lax.dynamic_index_in_dim(v[:, 0], k ^ (my_seq & 1), 0, keepdims=False) for v in values]
            parts.append(lax.ppermute(jnp.concatenate(piece), ("dp", "head"), routes(k)))
        return parts

    def from_plane(value):
        parts = []
        for k in range(2):
            back = [(b, a) for a, b in routes(k)]
            parts.append(lax.ppermute(value[k * tok : (k + 1) * tok], ("dp", "head"), back))
        odd = (my_seq & 1) == 1
        return jnp.stack([jnp.where(odd, parts[1], parts[0]), jnp.where(odd, parts[0], parts[1])])

    me = my_dp * n_blk + my_blk
    ids = jnp.stack([me, my_head]).astype(jnp.int32)
    n_rows = D // n_plane
    part = n_rows // n_head
    ff_here = FF // n_plane
    width = 4 * HP
    assert span % width == 0
    seg_rows = span // width
    small_rows = -(-(2 + 2 * seg_rows) // 16) * 16
    gain_row = lambda v: jnp.pad(v, (0, width - n_rows))[None]
    small = [gain_row(norm_gain_one), gain_row(norm_gain_two), segments[:, 0].astype(BF).reshape(2 * seg_rows, width)]
    small.append(jnp.zeros((small_rows - 2 - 2 * seg_rows, width), BF))
    small = jnp.concatenate(small)
    fence = Stages()
    join = jnp.concatenate
    share = n_rows // 4

    def pack_qkv(*values):
        shape = jax.ShapeDtypeStruct((n_plane, n_rows + small_rows, 4 * HP), BF)
        packed = place_call(pack_qkv_kernel, shape, ids, *values, name="pack_qkv")
        return packed.reshape((2, n_blk) + packed.shape[1:])

    def pack_ff(gate, up):
        cut = [lax.dynamic_slice_in_dim(w, my_seq * share, share, 0) for w in (gate, up)]
        shape = jax.ShapeDtypeStruct((n_plane, share, 2 * ff_here), BF)
        packed = place_call(pack_ff_kernel, shape, ids, *cut, name="pack_ff")
        return packed.reshape((2, n_blk) + packed.shape[1:])

    near_out = near(output_weight)
    packed, act_low, cot_low, gate_low, up_low = fence(
        pack_qkv(query_weight, key_weight, value_weight, small), activations, cotangent, gate_weight, up_weight
    )
    both, near_out, act_low, cot_low, gate_low, up_low = fence(
        pair_up(packed[0], swap(packed[1], "dp", 1)), near_out, act_low, cot_low, gate_low, up_low
    )
    ff_packed = pack_ff(gate_low, up_low)
    got, x_parts, ff_both = fence(
        chips(both), to_plane(act_low, cot_low), pair_up(ff_packed[0], swap(ff_packed[1], "dp", 1))
    )
    qkv_w, seg_all, gains, x_low, cot, input_one = place_call(
        functools.partial(head_kernel, n_blk),
        (
            jax.ShapeDtypeStruct((D, width), BF),
            jax.ShapeDtypeStruct((n_plane, small_rows, width), BF),
            jax.ShapeDtypeStruct((2, 1, D), F32),
            jax.ShapeDtypeStruct((own, D), BF),
            jax.ShapeDtypeStruct((own, D), BF),
            jax.ShapeDtypeStruct((own, D), BF),
        ),
        ids,
        *got,
        *x_parts,
        name="head",
        scratch=[pltpu.VMEM((n_plane, small_rows, width), BF)],
    )
    gain_one, gain_two = gains[0, 0], gains[1, 0]
    seg_all = seg_all[:, 2 : 2 + 2 * seg_rows].reshape(2, n_blk, 2, span)
    seg_seq = lax.dynamic_index_in_dim(seg_all, my_seq & 1, 0, keepdims=False)
    seg_seq = lax.dynamic_index_in_dim(seg_seq, my_seq >> 1, 1, keepdims=False)
    chunks = seg_seq.astype(jnp.int32).reshape(n_blk * n_head, tok)

    def chunk_ids(sub_index):
        ids = []
        for core in range(2):
            for blk in range(n_blk):
                for k in range(2):
                    seq_part = 2 * (my_dp ^ core) + ((my_seq >> 1) ^ k)
                    ids.append((my_blk ^ blk) * n_head + seq_part * sub + sub_index)
        return ids

    def pos_seg(sub_index):
        ids = chunk_ids(sub_index)
        lane = jnp.arange(tok, dtype=jnp.int32)
        pos = jnp.concatenate([i * tok + lane for i in ids])
        seg = jnp.concatenate([lax.dynamic_index_in_dim(chunks, i, 0, keepdims=False) for i in ids])
        return pos, seg

    qpos, qseg = pos_seg(my_sub)
    if sub == 1:
        kpos, kseg = qpos, qseg
    else:
        every = [pos_seg(i) for i in range(sub)]
        kpos, kseg = (jnp.concatenate([e[i] for e in every]) for i in range(2))
    blocked = lambda v: v.reshape(-1, BLK)
    qb, qsb, kb, ksb = blocked(qpos), blocked(qseg), blocked(kpos), blocked(kseg)
    need = (
        (jnp.min(kb, 1)[None, :] <= jnp.max(qb, 1)[:, None])
        & (jnp.min(ksb, 1)[None, :] <= jnp.max(qsb, 1)[:, None])
        & (jnp.max(ksb, 1)[None, :] >= jnp.min(qsb, 1)[:, None])
    ).astype(jnp.int32)

    input_one, qkv_w, ff_both, cot = fence(input_one, qkv_w, ff_both, cot)
    near_one, side_one, ff_both = fence(near(input_one), across(input_one), ff_both)
    far_one, ff_got, near_one = fence(far(*near_one), chips(ff_both), near_one)
    far_one = join(far_one)
    more_one = across(*near_one)
    mine_one = [input_one, *near_one, far_one]
    all_one = fence(*mine_one, *side_one, *more_one, *across(far_one))

    def project_qkv(*values):
        shape = jax.ShapeDtypeStruct((rows, 4 * HP), BF)
        return simple_call(stack_project_kernel, shape, values, "project_qkv", 2 * rows * D * 4 * HP)

    qkv = project_qkv(*all_one, qkv_w)
    cot, *near_out = lax.optimization_barrier((cot, *near_out, all_one[-1]))[:-1]
    kv = ()
    if sub > 1:
        groups = [[s * sub + i for i in range(sub)] for s in range(4)]
        kv = (lax.all_gather(qkv[:, 2 * HP :], "head", axis=0, tiled=True, axis_index_groups=groups),)
    q_args = tuple(v.astype(F32).reshape(-1, 1, BLK) for v in (qpos, qseg, kpos, kseg))
    sharing = None if sub == 1 else [[s * sub + i for s in range(4)] for i in range(sub)]
    ff_all = jnp.stack(ff_got, 1).reshape(-1, 2 * ff_here)
    ff_all = lax.all_gather(ff_all, "head", axis=0, tiled=True, axis_index_groups=sharing)
    ff_all = ff_all.reshape(4, n_plane, share, 2 * ff_here)
    (o, lse), near_cot, far_out = fence(attend(need, qkv, *(kv or (None,)), *q_args), near(cot), far(*near_out))
    o_parts = o.reshape(2, n_blk, own, 2 * HP)
    mine_out = [output_weight, *near_out, join(far_out)]
    o_both, near_cot = fence(pair_up(o_parts[0], swap(o_parts[1], "dp", 1)), near_cot)
    o_got, side_out, near_cot = fence(chips(o_both), across(*mine_out), near_cot)
    all_out = [*mine_out, *side_out]

    def out_project(*values):
        shapes = (jax.ShapeDtypeStruct((own, D), F32), jax.ShapeDtypeStruct((own, D), BF))
        kernel = functools.partial(out_project_kernel, n_blk)
        return simple_call(kernel, shapes, values, "out_project", 2 * own * D * D)

    (x_mid, input_two), side_cot = fence(
        out_project(*o_got, *all_out, x_low, gain_two[None]), across(cot, *near_cot)
    )

    def unpack_ff(value):
        shapes = (jax.ShapeDtypeStruct((D, ff_here), BF),) * 2
        return place_call(unpack_ff_kernel, shapes, ids, value, name="unpack_ff")

    def ff_part(n_mine, n_side, c_mine, c_side):
        return ff_call(n_mine, n_side, c_mine, c_side, gate_w, up_w, down_weight)

    gate_w, up_w = unpack_ff(after(ff_all, input_two))
    side_two = across(input_two)
    near_two, part_0, near_cot, gate_w, up_w = fence(
        near(input_two), ff_part(input_two, side_two[0], cot, side_cot[0]), near_cot, gate_w, up_w
    )
    more_two = across(*near_two)
    far_two, far_cot, part_1, part_2 = fence(
        far(*near_two),
        far(*near_cot),
        ff_part(near_two[0], more_two[0], near_cot[0], side_cot[1]),
        ff_part(near_two[1], more_two[1], near_cot[1], side_cot[2]),
    )
    far_two, far_cot = join(far_two), join(far_cot)
    last_two, last_cot = across(far_two, far_cot)
    side_parts = across(part_0[3], part_1[3], part_2[3])
    part_3, side_parts = fence(ff_part(far_two, last_two, far_cot, last_cot), side_parts)
    parts = [part_0, part_1, part_2, part_3]
    side_parts = [*side_parts, *across(part_3[3])]
    hidden, grad_gu = [p[0] for p in parts], [p[1] for p in parts]
    all_two = [input_two, *near_two, far_two, *side_two, *more_two, last_two]
    all_cot = [cot, *near_cot, far_cot, *side_cot, last_cot]
    local_two = [p[2] + v.astype(F32) for p, v in zip(parts, side_parts)]
    local_0, sent_two = fence(local_two[0], [v.astype(BF) for v in local_two])
    got_two = chips(sent_two)[1:]

    contract = ((0,), (0,))

    def rel_parts(mine):
        return rel_to_abs(mine, True)

    def head_sum(sent):
        return lax.psum_scatter(sent, "head", scatter_dimension=0, tiled=True)

    def owned_rows(chunks):
        if n_head != 4:
            return chunks[0].reshape(-1, chunks[0].shape[-1]).astype(F32)
        shape = jax.ShapeDtypeStruct((4 * chunks[0].shape[0], chunks[0].shape[1]), F32)
        return place_call(place_rows_kernel, shape, ids, *chunks, name="place_rows")

    def owned_columns(chunks, widths):
        if n_head != 4:
            full = rel_to_abs(jnp.moveaxis(chunks[0], 0, 1).reshape((2, n_blk, n_head) + chunks[0].shape[2:]))
            full = full.reshape(n_plane, n_rows, -1).transpose(1, 0, 2).astype(F32)
            ends = [sum(widths[: i + 1]) for i in range(len(widths))]
            return [full[:, :, e - w : e].reshape(n_rows, -1) for e, w in zip(ends, widths)]
        shapes = [jax.ShapeDtypeStruct((n_rows, n_plane * w), F32) for w in widths]
        kernel = functools.partial(place_columns_kernel, widths, len(chunks))
        return place_call(kernel, shapes, ids, *chunks, name="place_columns")

    ff_sent, down_sent = ff_weight_call(all_two, all_cot, grad_gu, hidden, n_head, n_plane)
    got_two, ff_sent, down_sent = fence(got_two, ff_sent, down_sent)
    down_mine = head_sum(down_sent)
    ff_mine = head_sum(ff_sent.reshape(D, 2 * ff_here)).reshape(n_plane, part, 2 * ff_here)

    def branch(*values):
        shapes = (
            jax.ShapeDtypeStruct((own, D), F32),
            jax.ShapeDtypeStruct((own, D), BF),
            jax.ShapeDtypeStruct((2, n_blk, own, 2 * HP), BF),
        )
        kernel = functools.partial(branch_kernel, n_blk)
        return simple_call(kernel, shapes, values, "branch", 2 * own * D * D)

    grad_mid, grad_branch, grad_o = fence(*branch(*all_out, local_0, *got_two, x_mid, cot, gain_two[None]))

    def back_project(transposed, *values):
        shapes = tuple(jax.ShapeDtypeStruct((n_blk, own, D), t) for t in (F32, BF))
        kernel = functools.partial(back_project_kernel, transposed)
        return simple_call(kernel, shapes, values, "back_project", 2 * rows * D * values[-1].size // D)

    do_both, hidden = fence(pair_up(grad_o[0], swap(grad_o[1], "dp", 1)), hidden)
    out_own, out_other = back_project(False, *hidden, down_weight)
    do_got, out_own, out_side, grad_branch = fence(chips(do_both), out_own, swap(out_other, "dp", 1), grad_branch)
    grad_o = jnp.stack(do_got, 1).reshape(rows, 2 * HP)
    line = n_head == 4
    no_step = lambda *v: ()
    step = line_step if line else no_step
    back = attend_back(need, qkv, *(kv or (None,)), *q_args, o, lse, grad_o)
    dqkv, near_branch, out_own, out_side = fence(back, near(grad_branch), out_own, out_side)
    local_out = [out_own[k] + out_side[k].astype(F32) for k in range(n_blk)]
    if sub > 1:
        dkv = lax.psum_scatter(dqkv[1], "head", scatter_dimension=0, tiled=True, axis_index_groups=groups)
        dqkv = [join([dqkv[0], dkv], 1)]
    dqkv = dqkv[0]
    qkv_grad, far_branch, dqkv, ff_mine, local_out, far_sum = fence(
        qkv_weight_call(all_one, dqkv, n_head, n_plane), far(*near_branch), dqkv, ff_mine, local_out, sum_far(local_out)
    )
    qkv_mine = head_sum(qkv_grad.reshape(D, 4 * HD)).reshape(n_plane, part, 4 * HD)
    mine_branch = [grad_branch, *near_branch, join(far_branch)]
    ff_rel = rel_parts(ff_mine)
    (one_own, one_other), side_branch, ff_both, got_out, local_out_0 = fence(
        back_project(True, dqkv, qkv_w),
        across(*mine_branch),
        pair_up(ff_rel[0], swap(ff_rel[1], "dp", 1)),
        sum_near(local_out, *far_sum),
        local_out[0],
    )
    block_out = (x_mid + local_out_0 + sum(g.astype(F32) for g in got_out)).astype(BF)

    def out_weights(*values):
        rows_per = values[1].shape[0]
        lanes = pl.BlockSpec((rows_per, 384), lambda j: (0, j))
        return pl.pallas_call(
            functools.partial(out_weight_kernel, n_plane),
            grid=(D // 384,),
            out_shape=jax.ShapeDtypeStruct((2 * HD, D), BF),
            in_specs=[pl.BlockSpec(values[0].shape, lambda j: (0, 0), pipeline_mode=pl.Buffered(1))] + [lanes] * n_plane,
            out_specs=pl.BlockSpec((2 * HD, 384), lambda j: (0, j)),
            compiler_params=pltpu.CompilerParams(vmem_limit_bytes=48 << 20),
            cost_estimate=small_cost(flops=4 * rows * D * 2 * HP, transcendentals=0, bytes_accessed=9 << 20),
            name="out_weight",
        )(*values)

    one_side = swap(one_other, "dp", 1)
    local_one = [one_own[k] + one_side[k].astype(F32) for k in range(n_blk)]
    ff_got, out_grad, local_0, sent_one, down_mine = fence(
        chips(ff_both),
        out_weights(o, *mine_branch, *side_branch),
        local_one[0],
        [v.astype(BF) for v in local_one],
        down_mine,
    )
    out_mine = head_sum(out_grad)
    late_down = lax.all_gather(down_mine, "head", axis=0)
    ff_rows = jnp.stack(ff_got, 1).reshape(ff_mine.shape)
    ff_0 = step(ff_rows, ff_rows)
    got_one, ff_1, ff_0, qkv_mine, out_mine, block_out = fence(
        chips(sent_one)[1:], step(*ff_0), ff_0, qkv_mine, out_mine, block_out
    )
    normed, factor = normalize(x_low.astype(F32))
    grad_in_one = local_0 + sum(g.astype(F32) for g in got_one)
    grad_input = (grad_mid + norm_back(grad_in_one, gain_one, normed, factor)).astype(BF)
    qkv_rel = rel_parts(qkv_mine)
    qkv_both = pair_up(qkv_rel[0], swap(qkv_rel[1], "dp", 1))
    qkv_rows, ff_2, grad_input, block_out, out_mine = fence(
        chips(qkv_both), step(*ff_1), grad_input, block_out, out_mine
    )
    out_rows = out_mine.reshape(part, -1, 4 * HD).transpose(1, 0, 2) if line else out_mine
    late = join([jnp.stack(qkv_rows, 1).reshape(-1, 4 * HD), out_rows.reshape(-1, 4 * HD)])
    late = lax.all_gather(late, "head", axis=0)
    grad_input = from_plane(grad_input)
    block_out = from_plane(block_out)
    grad_down = late_down.reshape(-1, D).astype(F32)
    if line:
        ff_chunks = [ff_2[0], ff_1[0], ff_0[0], ff_rows, ff_0[1], ff_1[1], ff_2[1]]
    else:
        ff_chunks = [lax.all_gather(ff_rows, "head", axis=0)]
    grad_gate_w, grad_up_w = owned_columns(ff_chunks, (ff_here, ff_here))
    def gain_grad(gain, *pairs):
        return sum(jnp.sum(w.astype(F32) * g, -1) for w, g in pairs) / gain.astype(F32)

    if line:
        matrices = (query_weight, key_weight, value_weight)
        shapes = [jax.ShapeDtypeStruct(w.shape, F32) for w in (*matrices, output_weight)]
        shapes.append(jax.ShapeDtypeStruct((1, n_rows), F32))
        values = (late, *matrices, norm_gain_one.astype(F32)[None])
        grad_query, grad_key, grad_value, grad_out, grad_gain_one = place_call(last_kernel, shapes, ids, *values, name="last")
        grad_gain_one = grad_gain_one[0]
    else:
        late_qkv = late[:, : n_plane * part].reshape(n_head, n_plane, part, 4 * HD)
        late_out = late[:, n_plane * part :].reshape(n_head, part, D)
        grad_query, grad_key, grad_value = owned_columns([late_qkv], (2 * HD, HD, HD))
        grad_out = owned_rows([late_out])
        grad_gain_one = gain_grad(
            norm_gain_one, (query_weight, grad_query), (key_weight, grad_key), (value_weight, grad_value)
        )
    grad_gain_two = gain_grad(norm_gain_two, (gate_weight, grad_gate_w), (up_weight, grad_up_w))
    return (
        block_out[:, None],
        grad_input[:, None],
        grad_gain_one,
        grad_query,
        grad_key,
        grad_value,
        grad_out,
        grad_gain_two,
        grad_gate_w,
        grad_up_w,
        grad_down,
    )


def solution(mesh):
    tokens = P(None, "dp", ("blk", "head"), None)
    vector = P(("dp", "blk"))
    matrix = P(("dp", "blk"), None)
    return jax.shard_map(
        per_device,
        mesh=mesh,
        in_specs=(
            tokens,
            P(None, "dp", "blk"),
            tokens,
            vector,
            matrix,
            matrix,
            matrix,
            matrix,
            vector,
            matrix,
            matrix,
            matrix,
        ),
        out_specs=(tokens, tokens, vector, matrix, matrix, matrix, matrix, vector, matrix, matrix, matrix),
        check_vma=False,
    )
```

```python
import functools
import math

import jax
import jax.numpy as jnp
from jax import lax
from jax.experimental import pallas as pl
from jax.experimental.pallas import tpu as pltpu
from jax.sharding import PartitionSpec as P

D = 1536
QH = 16
KVH = 8
HD = 96
HP = 128
FF = 4096
EPS = 1e-05
NEG = -1e30
BLK = 256
BF = jnp.bfloat16
F32 = jnp.float32


def small_cost(flops, transcendentals, bytes_accessed):
    part = 64
    return pl.CostEstimate(
        flops=flops // part, transcendentals=transcendentals // part, bytes_accessed=bytes_accessed // part
    )


def dot(left, right, dims=((1,), (0,))):
    return lax.dot_general(left, right, (dims, ((), ())), preferred_element_type=F32)


def normalize(values):
    factor = lax.rsqrt(jnp.mean(values * values, -1, keepdims=True) + EPS)
    return values * factor, factor


def norm_back(grad_norm, gain, normed, factor):
    scaled = grad_norm * gain
    return factor * (scaled - normed * jnp.mean(scaled * normed, -1, keepdims=True))


def rows_of(index):
    return pl.ds(pl.multiple_of(index * BLK, BLK), BLK)


def as_column(row):
    return jnp.broadcast_to(row, (HP, BLK)).T[:, 0:1]


def as_row(col):
    return jnp.broadcast_to(col, (BLK, HP)).T[0:1, :]


def keys_to_columns(kp_ref, ks_ref, pos_sc, seg_sc):
    def one(j, _):
        pos_sc[rows_of(j), :] = as_column(kp_ref[j])
        seg_sc[rows_of(j), :] = as_column(ks_ref[j])
        return 0

    lax.fori_loop(0, kp_ref.shape[0], one, 0)


def attn_fwd_kernel(first, need, q_ref, kv_ref, qp_ref, qs_ref, kp_ref, ks_ref, o_ref, lse_ref, m_sc, l_sc, acc_sc, pos_sc, seg_sc):
    scale = 1.0 / math.sqrt(HD)
    n_q, n_k = q_ref.shape[0] // BLK, kv_ref.shape[0] // BLK
    k_cols, v_cols = slice(first, first + HP), slice(first + HP, first + 2 * HP)
    keys_to_columns(kp_ref, ks_ref, pos_sc, seg_sc)

    def one_query(i, _):
        qr = rows_of(i)
        m_sc[...] = jnp.full_like(m_sc, NEG)
        l_sc[...] = jnp.zeros_like(l_sc)
        acc_sc[...] = jnp.zeros_like(acc_sc)
        qpos, qseg = qp_ref[i], qs_ref[i]

        def one_key(j, _):
            @pl.when(need[i, j] != 0)
            def _():
                kr = rows_of(j)
                ok = (pos_sc[kr, :] <= qpos) & (seg_sc[kr, :] == qseg)
                k, v = kv_ref[kr, k_cols], kv_ref[kr, v_cols]
                state = [(m_sc[g], l_sc[g], acc_sc[g], q_ref[qr, g * HP : (g + 1) * HP]) for g in range(2)]
                scores = [jnp.where(ok, dot(k, q, ((1,), (1,))) * scale, 2.0 * NEG) for _, _, _, q in state]
                new = []
                for (m_old, l_old, acc_old, _), s in zip(state, scores):
                    m_new = jnp.maximum(m_old, jnp.max(s, 0, keepdims=True))
                    p = jnp.exp(s - m_new)
                    decay = jnp.exp(m_old - m_new)
                    total = l_old * decay + jnp.sum(p, 0, keepdims=True)
                    new.append((m_new, total, acc_old * decay + dot(v, p.astype(BF), ((0,), (0,)))))
                for g in range(2):
                    m_sc[g], l_sc[g], acc_sc[g] = new[g]

            return 0

        lax.fori_loop(0, n_k, one_key, 0)
        for g in range(2):
            o_ref[qr, g * HP : (g + 1) * HP] = (acc_sc[g] / l_sc[g]).T.astype(BF)
            lse_ref[i, g : g + 1, :] = m_sc[g] + jnp.log(l_sc[g])
        return 0

    lax.fori_loop(0, n_q, one_query, 0)


def attn_bwd_kernel(first, need, q_ref, kv_ref, qp_ref, qs_ref, kp_ref, ks_ref, o_ref, lse_ref, do_ref, *rest):
    dq_ref, dkv_ref = rest[0], rest[-6]
    dq_sc, dk_sc, dv_sc, pos_sc, seg_sc = rest[-5:]
    scale = 1.0 / math.sqrt(HD)
    n_q, n_k = q_ref.shape[0] // BLK, kv_ref.shape[0] // BLK
    k_cols, v_cols = slice(first, first + HP), slice(first + HP, first + 2 * HP)
    dk_sc[...] = jnp.zeros_like(dk_sc)
    dv_sc[...] = jnp.zeros_like(dv_sc)
    keys_to_columns(kp_ref, ks_ref, pos_sc, seg_sc)

    def one_query(i, _):
        qr = rows_of(i)
        dq_sc[...] = jnp.zeros_like(dq_sc)
        qpos, qseg = qp_ref[i], qs_ref[i]
        lse, delta = [], []
        for g in range(2):
            cols = slice(g * HP, (g + 1) * HP)
            lse.append(lse_ref[i, g : g + 1, :])
            prod = do_ref[qr, cols].astype(F32) * o_ref[qr, cols].astype(F32)
            delta.append(as_row(jnp.sum(prod, -1, keepdims=True)))

        def one_key(j, _):
            @pl.when(need[i, j] != 0)
            def _():
                kr = rows_of(j)
                ok = (pos_sc[kr, :] <= qpos) & (seg_sc[kr, :] == qseg)
                k, v = kv_ref[kr, k_cols], kv_ref[kr, v_cols]
                qs = [q_ref[qr, g * HP : (g + 1) * HP] for g in range(2)]
                dos = [do_ref[qr, g * HP : (g + 1) * HP] for g in range(2)]
                scores = [dot(k, q, ((1,), (1,))) * scale for q in qs]
                dps = [dot(v, do, ((1,), (1,))) for do in dos]
                dv, dk = dv_sc[kr, :], dk_sc[kr, :]
                dqs = []
                for g in range(2):
                    p = jnp.where(ok, jnp.exp(scores[g] - lse[g]), 0.0)
                    ds = (p * (dps[g] - delta[g])).astype(BF)
                    dv = dv + dot(p.astype(BF), dos[g])
                    dk = dk + dot(ds, qs[g])
                    dqs.append(dot(ds, k, ((0,), (0,))))
                dv_sc[kr, :], dk_sc[kr, :] = dv, dk
                for g in range(2):
                    dq_sc[g] += dqs[g]

            return 0

        lax.fori_loop(0, n_k, one_key, 0)
        for g in range(2):
            dq_ref[qr, g * HP : (g + 1) * HP] = (dq_sc[g] * scale).astype(BF)
        return 0

    lax.fori_loop(0, n_q, one_query, 0)
    dkv_ref[:, k_cols] = (dk_sc[...] * scale).astype(BF)
    dkv_ref[:, v_cols] = dv_sc[...].astype(BF)


def in_vmem(count):
    return [pl.BlockSpec(memory_space=pltpu.SMEM)] + [pl.BlockSpec(memory_space=pltpu.VMEM)] * count


def attn_cost(n_q, n_k, products):
    return small_cost(
        flops=2 * products * n_q * n_k * 2 * HP, transcendentals=n_q * n_k * 2, bytes_accessed=(n_q + n_k) * HP * 16
    )


def attend(need, q, kv, qpos, qseg, kpos, kseg):
    first, kv = (2 * HP, q) if kv is None else (0, kv)
    n_q, n_k = q.shape[0], kv.shape[0]
    return pl.pallas_call(
        functools.partial(attn_fwd_kernel, first),
        out_shape=(jax.ShapeDtypeStruct((n_q, 2 * HP), BF), jax.ShapeDtypeStruct((n_q // BLK, 2, BLK), F32)),
        in_specs=in_vmem(6),
        out_specs=(pl.BlockSpec(memory_space=pltpu.VMEM),) * 2,
        scratch_shapes=[pltpu.VMEM((2, 1, BLK), F32)] * 2 + [pltpu.VMEM((2, HP, BLK), F32)] + [pltpu.VMEM((n_k, 1), F32)] * 2,
        compiler_params=pltpu.CompilerParams(vmem_limit_bytes=40 << 20),
        cost_estimate=attn_cost(n_q, n_k, 2),
        name="attn_fwd",
    )(need, q, kv, qpos, qseg, kpos, kseg)


def attend_back(need, q, kv, qpos, qseg, kpos, kseg, o, lse, do):
    joint = kv is None
    first, kv = (2 * HP, q) if joint else (0, kv)
    n_q, n_k = q.shape[0], kv.shape[0]
    shapes = [jax.ShapeDtypeStruct((n_q, 4 * HP), BF)] if joint else [jax.ShapeDtypeStruct((n, 2 * HP), BF) for n in (n_q, n_k)]
    return pl.pallas_call(
        functools.partial(attn_bwd_kernel, first),
        out_shape=shapes,
        in_specs=in_vmem(9),
        out_specs=[pl.BlockSpec(memory_space=pltpu.VMEM)] * len(shapes),
        scratch_shapes=[pltpu.VMEM((2, BLK, HP), F32)] + [pltpu.VMEM((n_k, HP), F32)] * 2 + [pltpu.VMEM((n_k, 1), F32)] * 2,
        compiler_params=pltpu.CompilerParams(vmem_limit_bytes=48 << 20),
        cost_estimate=attn_cost(n_q, n_k, 5),
        name="attn_bwd",
    )(need, q, kv, qpos, qseg, kpos, kseg, o, lse, do)


def whole(count):
    return [pl.BlockSpec(memory_space=pltpu.VMEM)] * count


def place_call(kernel, out_shape, ids, *values, name, scratch=()):
    moved = sum(v.size * v.dtype.itemsize for v in values)
    return pl.pallas_call(
        kernel,
        out_shape=out_shape,
        in_specs=[pl.BlockSpec(memory_space=pltpu.SMEM)] + whole(len(values)),
        out_specs=jax.tree.map(lambda _: pl.BlockSpec(memory_space=pltpu.VMEM), out_shape),
        scratch_shapes=scratch,
        compiler_params=pltpu.CompilerParams(vmem_limit_bytes=40 << 20),
        cost_estimate=small_cost(flops=0, transcendentals=0, bytes_accessed=2 * moved),
        name=name,
    )(ids, *values)


def pack_qkv_kernel(ids, q_ref, k_ref, v_ref, small_ref, out_ref):
    rows = q_ref.shape[0]
    zero = jnp.zeros((rows, HP - HD), BF)
    for dev in range(KVH):
        slot = ids[0] ^ dev
        heads = [(q_ref, 2 * dev), (q_ref, 2 * dev + 1), (k_ref, dev), (v_ref, dev)]
        for i, (ref, head) in enumerate(heads):
            piece = ref[:, head * HD : (head + 1) * HD]
            out_ref[slot, :rows, i * HP : (i + 1) * HP] = jnp.concatenate([piece, zero], 1)
        out_ref[slot, rows:, :] = small_ref[...]


def pack_ff_kernel(ids, gate_ref, up_ref, out_ref):
    width = gate_ref.shape[1] // KVH
    for dev in range(KVH):
        slot = ids[0] ^ dev
        for i, ref in enumerate((gate_ref, up_ref)):
            out_ref[slot, :, i * width : (i + 1) * width] = ref[:, dev * width : (dev + 1) * width]


def head_kernel(n_blk, ids, *refs):
    got, x_refs = refs[:n_blk], refs[n_blk : n_blk + 2]
    w_ref, seg_ref, gain_ref, x_ref, c_ref, n_ref, small_sc = refs[n_blk + 2 :]
    n_rows = w_ref.shape[0] // (2 * n_blk)
    for k, ref in enumerate(got):
        for core in range(2):
            at = pl.multiple_of((ids[0] ^ (core * n_blk + k)) * n_rows, 16)
            w_ref[pl.ds(at, n_rows), :] = ref[core, :n_rows, :]
            small_sc[core * n_blk + k] = ref[core, n_rows:, :]
    gains = [[], []]
    for dev in range(2 * n_blk):
        small = small_sc[ids[0] ^ dev]
        seg_ref[dev] = small
        small = small.astype(F32)
        for i in range(2):
            gains[i].append(small[i : i + 1, :n_rows])
    for i in range(2):
        gain_ref[i] = jnp.concatenate(gains[i], 1)
    tok = x_refs[0].shape[0] // 2
    for i, ref in enumerate(x_refs):
        x = ref[:tok, :]
        x_ref[i * tok : (i + 1) * tok, :] = x
        c_ref[i * tok : (i + 1) * tok, :] = ref[tok:, :]
        x = x.astype(F32)
        factor = lax.rsqrt(jnp.mean(x * x, -1, keepdims=True) + EPS)
        n_ref[i * tok : (i + 1) * tok, :] = (x * factor * gain_ref[0]).astype(BF)


def unpack_ff_kernel(ids, in_ref, gate_ref, up_ref):
    n_head, n_slot, part, width = in_ref.shape
    for head in range(n_head):
        for slot in range(n_slot):
            at = pl.ds(pl.multiple_of(((ids[0] ^ slot) * n_head + head) * part, 16), part)
            gate_ref[at, :] = in_ref[head, slot, :, : width // 2]
            up_ref[at, :] = in_ref[head, slot, :, width // 2 :]


def chunk_heads(ids, count):
    if count == 7:
        return [(ids[1] + (i - 3), (ids[1] + (i - 3) >= 0) & (ids[1] + (i - 3) < 4)) for i in range(7)]
    return [(i, None) for i in range(count)]


def place_chunk(ok, body):
    if ok is None:
        body()
    else:
        pl.when(ok)(body)


def place_rows_kernel(ids, *refs):
    out_ref = refs[-1]
    part = refs[0].shape[0]
    for ref, (head, ok) in zip(refs[:-1], chunk_heads(ids, len(refs) - 1)):

        def body():
            out_ref[pl.ds(pl.multiple_of(head * part, 16), part), :] = ref[...].astype(F32)

        place_chunk(ok, body)


def place_columns_kernel(widths, count, ids, *refs):
    chunks, outs = refs[:count], refs[count:]
    n_slot, part = chunks[0].shape[:2]
    for ref, (head, ok) in zip(chunks, chunk_heads(ids, count)):

        def body():
            at = pl.ds(pl.multiple_of(head * part, 16), part)
            first = 0
            for out_ref, width in zip(outs, widths):
                for pair in range(0, n_slot, 2):
                    both = [ref[ids[0] ^ dev][:, first : first + width] for dev in (pair, pair + 1)]
                    out_ref[at, pair * width : (pair + 2) * width] = jnp.concatenate(both, 1).astype(F32)
                first += width

        place_chunk(ok, body)


def last_kernel(ids, in_ref, q_w, k_w, v_w, gain_ref, q_ref, k_ref, v_ref, out_ref, sum_ref):
    n_head = in_ref.shape[0]
    n_rows = q_w.shape[0]
    part = n_rows // n_head
    n_slot = 2 * (q_w.shape[1] // (4 * HD))
    for head in range(n_head):
        at = slice(head * part, (head + 1) * part)
        for pair in range(0, n_slot, 2):
            two = [in_ref[head, pl.ds(pl.multiple_of((ids[0] ^ dev) * part, 16), part), :] for dev in (pair, pair + 1)]
            for ref, first, width in ((q_ref, 0, 2 * HD), (k_ref, 2 * HD, HD), (v_ref, 3 * HD, HD)):
                both = jnp.concatenate([v[:, first : first + width] for v in two], 1)
                ref[at, pair * width : (pair + 2) * width] = both.astype(F32)
        for i in range(D // (4 * HD)):
            rows = slice((n_slot + i) * part, (n_slot + i + 1) * part)
            out_ref[at, i * 4 * HD : (i + 1) * 4 * HD] = in_ref[head, rows, :].astype(F32)
    total = None
    for w, g in ((q_w, q_ref), (k_w, k_ref), (v_w, v_ref)):
        one = jnp.sum(w[...].astype(F32) * g[...], -1, keepdims=True)
        total = one if total is None else total + one
    sum_ref[...] = jnp.broadcast_to(total, (n_rows, 128)).T[0:1, :] / gain_ref[...]


def ff_kernel(n0, n1, c0, c1, gate_ref, up_ref, down_ref, hid_ref, dgu_ref, own_ref, other_ref):
    width = gate_ref.shape[1]
    for i, (n_ref, c_ref) in ((1, (n1, c1)), (0, (n0, c0))):
        n = n_ref[...]
        gate = dot(n, gate_ref[...])
        up = dot(n, up_ref[...])
        grad = dot(c_ref[...], down_ref[...], ((1,), (1,)))
        sigma = jax.nn.sigmoid(gate)
        silu = gate * sigma
        hid_ref[i] = (silu * up).astype(BF)
        grad_gate = (grad * up * sigma * (1.0 + gate * (1.0 - sigma))).astype(BF)
        grad_up = (grad * silu).astype(BF)
        dgu_ref[i, :, :width] = grad_gate
        dgu_ref[i, :, width:] = grad_up
        total = dot(grad_gate, gate_ref[...], ((1,), (1,))) + dot(grad_up, up_ref[...], ((1,), (1,)))
        if i == 0:
            own_ref[...] = total
        else:
            other_ref[...] = total.astype(BF)


def ff_call(n0, n1, c0, c1, gate_w, up_w, down_w):
    rows, width = n0.shape[0], gate_w.shape[1]
    return pl.pallas_call(
        ff_kernel,
        out_shape=(
            jax.ShapeDtypeStruct((2, rows, width), BF),
            jax.ShapeDtypeStruct((2, rows, 2 * width), BF),
            jax.ShapeDtypeStruct((rows, D), F32),
            jax.ShapeDtypeStruct((rows, D), BF),
        ),
        in_specs=whole(7),
        out_specs=tuple(whole(4)),
        compiler_params=pltpu.CompilerParams(vmem_limit_bytes=40 << 20),
        cost_estimate=small_cost(
            flops=2 * 2 * rows * D * width * 5, transcendentals=2 * rows * width, bytes_accessed=12 << 20
        ),
        name="ff",
    )(n0, n1, c0, c1, gate_w, up_w, down_w)


def ff_weight_kernel(n_pairs, *refs):
    n_refs, c_refs = refs[: 2 * n_pairs], refs[2 * n_pairs : 4 * n_pairs]
    dgu_refs, hid_refs = refs[4 * n_pairs : 5 * n_pairs], refs[5 * n_pairs : 6 * n_pairs]
    ff_ref, down_ref = refs[6 * n_pairs :]
    over = ((0,), (0,))
    total_ff = total_down = None
    for i in range(2 * n_pairs):
        core, k = i // n_pairs, i % n_pairs
        one = dot(n_refs[i][...], dgu_refs[k][core], over)
        two = dot(hid_refs[k][core], c_refs[i][...], over)
        total_ff = one if total_ff is None else total_ff + one
        total_down = two if total_down is None else total_down + two
    n_head, n_dev, part, width = ff_ref.shape
    for dev in range(n_dev):
        for head in range(n_head):
            first = (dev * n_head + head) * part
            ff_ref[head, dev] = total_ff[first : first + part].astype(BF)
    down_ref[...] = total_down.astype(BF)


def ff_weight_call(n_list, c_list, dgu_list, hid_list, n_head, n_plane):
    n_pairs = len(dgu_list)
    rows, width2 = n_list[0].shape[0], dgu_list[0].shape[2]
    part = D // n_plane // n_head
    cols = 384
    steps = D // cols
    lanes = pl.BlockSpec((rows, cols), lambda j: (0, j))
    fixed = lambda v: pl.BlockSpec(v.shape, lambda j: (0, 0, 0), pipeline_mode=pl.Buffered(1))
    per_step = n_plane // steps
    return pl.pallas_call(
        functools.partial(ff_weight_kernel, n_pairs),
        grid=(steps,),
        out_shape=(
            jax.ShapeDtypeStruct((n_head, n_plane, part, width2), BF),
            jax.ShapeDtypeStruct((width2 // 2, D), BF),
        ),
        in_specs=[lanes] * (4 * n_pairs) + [fixed(v) for v in dgu_list] + [fixed(v) for v in hid_list],
        out_specs=(
            pl.BlockSpec((n_head, per_step, part, width2), lambda j: (0, j, 0, 0)),
            pl.BlockSpec((width2 // 2, cols), lambda j: (0, j)),
        ),
        compiler_params=pltpu.CompilerParams(vmem_limit_bytes=56 << 20),
        cost_estimate=small_cost(
            flops=2 * 2 * n_pairs * rows * D * width2 * 3 // 2, transcendentals=0, bytes_accessed=24 << 20
        ),
        name="ff_weight",
    )(*n_list, *c_list, *dgu_list, *hid_list)


def simple_call(kernel, out_shape, values, name, flops):
    leaves = jax.tree.leaves(out_shape)
    moved = sum(v.size * v.dtype.itemsize for v in list(values) + leaves)
    return pl.pallas_call(
        kernel,
        out_shape=out_shape,
        in_specs=whole(len(values)),
        out_specs=jax.tree.map(lambda _: pl.BlockSpec(memory_space=pltpu.VMEM), out_shape),
        compiler_params=pltpu.CompilerParams(vmem_limit_bytes=52 << 20),
        cost_estimate=small_cost(flops=flops, transcendentals=0, bytes_accessed=moved),
        name=name,
    )(*values)


def stack_project_kernel(*refs):
    weight, out_ref = refs[-2], refs[-1]
    rows = refs[0].shape[0]
    for i, ref in enumerate(refs[:-2]):
        out_ref[i * rows : (i + 1) * rows, :] = dot(ref[...], weight[...]).astype(BF)


def out_project_kernel(n_blk, *refs):
    o_refs, w_refs = refs[:n_blk], refs[n_blk : 3 * n_blk]
    x_ref, gain_ref, mid_ref, n_ref = refs[3 * n_blk :]
    total = x_ref[...].astype(F32)
    for core in range(2):
        for k in range(n_blk):
            o = o_refs[k][core]
            o = jnp.concatenate([o[:, :HD], o[:, HP : HP + HD]], 1)
            total = total + dot(o, w_refs[core * n_blk + k][...])
    mid_ref[...] = total
    factor = lax.rsqrt(jnp.mean(total * total, -1, keepdims=True) + EPS)
    n_ref[...] = (total * factor * gain_ref[...]).astype(BF)


def branch_kernel(n_blk, *refs):
    w_refs = refs[: 2 * n_blk]
    local_ref, got_refs = refs[2 * n_blk], refs[2 * n_blk + 1 : 3 * n_blk]
    mid_ref, cot_ref, gain_ref, grad_ref, branch_ref, do_ref = refs[3 * n_blk :]
    total = local_ref[...]
    for ref in got_refs:
        total = total + ref[...].astype(F32)
    mid = mid_ref[...]
    factor = lax.rsqrt(jnp.mean(mid * mid, -1, keepdims=True) + EPS)
    grad = cot_ref[...].astype(F32) + norm_back(total, gain_ref[...], mid * factor, factor)
    grad_ref[...] = grad
    branch = grad.astype(BF)
    branch_ref[...] = branch
    zero = jnp.zeros((branch.shape[0], HP - HD), BF)
    for core in range(2):
        for k in range(n_blk):
            do = dot(branch, w_refs[core * n_blk + k][...], ((1,), (1,))).astype(BF)
            do_ref[core, k] = jnp.concatenate([do[:, :HD], zero, do[:, HD:], zero], 1)


def back_project_kernel(transposed, *refs):
    weight, own_ref, other_ref = refs[-3], refs[-2], refs[-1]
    dims = ((1,), (1,)) if transposed else ((1,), (0,))
    n_blk, rows = own_ref.shape[:2]
    for core in (1, 0):
        for k in range(n_blk):
            at = (core * n_blk + k) * rows
            value = refs[0][at : at + rows, :] if len(refs) == 4 else refs[k][core]
            part = dot(value, weight[...], dims)
            if core:
                other_ref[k] = part.astype(BF)
            else:
                own_ref[k] = part


def out_weight_kernel(count, *refs):
    o_ref, b_refs, out_ref = refs[0], refs[1 : 1 + count], refs[-1]
    rows = b_refs[0].shape[0]
    total = None
    for i, ref in enumerate(b_refs):
        one = dot(o_ref[i * rows : (i + 1) * rows, :], ref[...], ((0,), (0,)))
        total = one if total is None else total + one
    out_ref[:HD, :] = total[:HD].astype(BF)
    out_ref[HD:, :] = total[HP : HP + HD].astype(BF)


def qkv_weight_kernel(n_refs_count, *refs):
    n_refs, grad_ref, out_ref = refs[:n_refs_count], refs[-2], refs[-1]
    rows = n_refs[0].shape[0]
    total = None
    for i, ref in enumerate(n_refs):
        one = dot(ref[...], grad_ref[i * rows : (i + 1) * rows, :], ((0,), (0,)))
        total = one if total is None else total + one
    total = jnp.concatenate([total[:, g * HP : g * HP + HD] for g in range(4)], 1)
    n_head, n_dev, part, _ = out_ref.shape
    for dev in range(n_dev):
        for head in range(n_head):
            first = (dev * n_head + head) * part
            out_ref[head, dev] = total[first : first + part].astype(BF)


def qkv_weight_call(n_list, dqkv, n_head, n_plane):
    rows = n_list[0].shape[0]
    part = D // n_plane // n_head
    cols = 384
    steps = D // cols
    return pl.pallas_call(
        functools.partial(qkv_weight_kernel, len(n_list)),
        grid=(steps,),
        out_shape=jax.ShapeDtypeStruct((n_head, n_plane, part, 4 * HD), BF),
        in_specs=[pl.BlockSpec((rows, cols), lambda j: (0, j))] * len(n_list)
        + [pl.BlockSpec(dqkv.shape, lambda j: (0, 0), pipeline_mode=pl.Buffered(1))],
        out_specs=pl.BlockSpec((n_head, n_plane // steps, part, 4 * HD), lambda j: (0, j, 0, 0)),
        compiler_params=pltpu.CompilerParams(vmem_limit_bytes=48 << 20),
        cost_estimate=small_cost(
            flops=2 * len(n_list) * rows * D * 4 * HP * 2, transcendentals=0, bytes_accessed=12 << 20
        ),
        name="qkv_weight",
    )(*n_list, dqkv)


def after(value, *first):
    return lax.optimization_barrier((value,) + first)[0]


def swap(value, axis, mask):
    return lax.ppermute(value, axis, [(i, i ^ mask) for i in range(lax.axis_size(axis))])


class Stages:
    def __init__(self):
        self.last = ()

    def __call__(self, *trees):
        leaves, tree = jax.tree.flatten(trees)
        tied = lax.optimization_barrier(tuple(leaves) + self.last)
        self.last = (tied[0],)
        return jax.tree.unflatten(tree, tied[: len(leaves)])


def near(value):
    return swap(value, "blk", 1), swap(value, "blk", 2)


def halves(one, two):
    half = one.shape[0] // 2
    return one[:half], two[half:]


def far_halves(low, high):
    return swap(low, "blk", 2), swap(high, "blk", 1)


def far(one, two):
    return far_halves(*halves(one, two))


def across(*values):
    return tuple(swap(v, "dp", 1) for v in values)


def chips(both):
    return [both[0]] + [swap(both[k], "blk", k) for k in range(1, len(both))]


def pair_up(mine, other):
    return [jnp.stack([mine[k], other[k]]) for k in range(mine.shape[0])]


def add_cores(own, other):
    return own + swap(other, "dp", 1).astype(F32)


def sum_far(parts):
    half = parts[3].shape[0] // 2
    return swap(parts[3][:half].astype(BF), "blk", 1), swap(parts[3][half:].astype(BF), "blk", 2)


def sum_near(parts, low, high):
    half = parts[3].shape[0] // 2
    one = jnp.concatenate([parts[1][:half], parts[1][half:] + high.astype(F32)])
    two = jnp.concatenate([parts[2][:half] + low.astype(F32), parts[2][half:]])
    return swap(one.astype(BF), "blk", 1), swap(two.astype(BF), "blk", 2)


def line_step(left, right):
    up = [(i, i + 1) for i in range(3)]
    return lax.ppermute(left, "head", up), lax.ppermute(right, "head", [(b, a) for a, b in up])


def rel_to_abs(value, reverse=False):
    n_blk = lax.axis_size("blk")
    mine = lax.axis_index("dp") * n_blk + lax.axis_index("blk")
    flat = value.reshape((2 * n_blk,) + value.shape[(1 if reverse else 2) :])
    out = jnp.stack([lax.dynamic_index_in_dim(flat, i ^ mine, 0, keepdims=False) for i in range(2 * n_blk)])
    return out.reshape((2, n_blk) + out.shape[1:]) if reverse else out


def per_device(
    activations,
    segments,
    cotangent,
    norm_gain_one,
    query_weight,
    key_weight,
    value_weight,
    output_weight,
    norm_gain_two,
    gate_weight,
    up_weight,
    down_weight,
):
    n_blk, n_head = lax.axis_size("blk"), lax.axis_size("head")
    n_plane = 2 * n_blk
    assert lax.axis_size("dp") == 2 and activations.shape[0] == 2 and n_plane == KVH
    sub = n_head // 4
    tok = activations.shape[2]
    span = tok * n_head
    own = 2 * tok
    rows = n_plane * own
    my_dp, my_blk, my_head = (lax.axis_index(name) for name in ("dp", "blk", "head"))
    my_seq, my_sub = my_head // sub, my_head % sub

    def routes(k):
        pairs = []
        for core in range(2):
            for head in range(n_head):
                seq_part, sub_part = head // sub, head % sub
                target = 2 * (k ^ (seq_part & 1)) + core
                pairs.append((core * n_head + head, (seq_part >> 1) * n_head + target * sub + sub_part))
        return pairs

    def to_plane(*values):
        parts = []
        for k in range(2):
            piece = [lax.dynamic_index_in_dim(v[:, 0], k ^ (my_seq & 1), 0, keepdims=False) for v in values]
            parts.append(lax.ppermute(jnp.concatenate(piece), ("dp", "head"), routes(k)))
        return parts

    def from_plane(value):
        parts = []
        for k in range(2):
            back = [(b, a) for a, b in routes(k)]
            parts.append(lax.ppermute(value[k * tok : (k + 1) * tok], ("dp", "head"), back))
        odd = (my_seq & 1) == 1
        return jnp.stack([jnp.where(odd, parts[1], parts[0]), jnp.where(odd, parts[0], parts[1])])

    me = my_dp * n_blk + my_blk
    ids = jnp.stack([me, my_head]).astype(jnp.int32)
    n_rows = D // n_plane
    part = n_rows // n_head
    ff_here = FF // n_plane
    width = 4 * HP
    assert span % width == 0
    seg_rows = span // width
    small_rows = -(-(2 + 2 * seg_rows) // 16) * 16
    gain_row = lambda v: jnp.pad(v, (0, width - n_rows))[None]
    small = [gain_row(norm_gain_one), gain_row(norm_gain_two), segments[:, 0].astype(BF).reshape(2 * seg_rows, width)]
    small.append(jnp.zeros((small_rows - 2 - 2 * seg_rows, width), BF))
    small = jnp.concatenate(small)
    fence = Stages()
    join = jnp.concatenate
    share = n_rows // 4

    def pack_qkv(*values):
        shape = jax.ShapeDtypeStruct((n_plane, n_rows + small_rows, 4 * HP), BF)
        packed = place_call(pack_qkv_kernel, shape, ids, *values, name="pack_qkv")
        return packed.reshape((2, n_blk) + packed.shape[1:])

    def pack_ff(gate, up):
        cut = [lax.dynamic_slice_in_dim(w, my_seq * share, share, 0) for w in (gate, up)]
        shape = jax.ShapeDtypeStruct((n_plane, share, 2 * ff_here), BF)
        packed = place_call(pack_ff_kernel, shape, ids, *cut, name="pack_ff")
        return packed.reshape((2, n_blk) + packed.shape[1:])

    near_out = near(output_weight)
    packed, act_low, cot_low, gate_low, up_low = fence(
        pack_qkv(query_weight, key_weight, value_weight, small), activations, cotangent, gate_weight, up_weight
    )
    both, near_out, act_low, cot_low, gate_low, up_low = fence(
        pair_up(packed[0], swap(packed[1], "dp", 1)), near_out, act_low, cot_low, gate_low, up_low
    )
    ff_packed = pack_ff(gate_low, up_low)
    got, x_parts, ff_both = fence(
        chips(both), to_plane(act_low, cot_low), pair_up(ff_packed[0], swap(ff_packed[1], "dp", 1))
    )
    qkv_w, seg_all, gains, x_low, cot, input_one = place_call(
        functools.partial(head_kernel, n_blk),
        (
            jax.ShapeDtypeStruct((D, width), BF),
            jax.ShapeDtypeStruct((n_plane, small_rows, width), BF),
            jax.ShapeDtypeStruct((2, 1, D), F32),
            jax.ShapeDtypeStruct((own, D), BF),
            jax.ShapeDtypeStruct((own, D), BF),
            jax.ShapeDtypeStruct((own, D), BF),
        ),
        ids,
        *got,
        *x_parts,
        name="head",
        scratch=[pltpu.VMEM((n_plane, small_rows, width), BF)],
    )
    gain_one, gain_two = gains[0, 0], gains[1, 0]
    seg_all = seg_all[:, 2 : 2 + 2 * seg_rows].reshape(2, n_blk, 2, span)
    seg_seq = lax.dynamic_index_in_dim(seg_all, my_seq & 1, 0, keepdims=False)
    seg_seq = lax.dynamic_index_in_dim(seg_seq, my_seq >> 1, 1, keepdims=False)
    chunks = seg_seq.astype(jnp.int32).reshape(n_blk * n_head, tok)

    def chunk_ids(sub_index):
        ids = []
        for core in range(2):
            for blk in range(n_blk):
                for k in range(2):
                    seq_part = 2 * (my_dp ^ core) + ((my_seq >> 1) ^ k)
                    ids.append((my_blk ^ blk) * n_head + seq_part * sub + sub_index)
        return ids

    def pos_seg(sub_index):
        ids = chunk_ids(sub_index)
        lane = jnp.arange(tok, dtype=jnp.int32)
        pos = jnp.concatenate([i * tok + lane for i in ids])
        seg = jnp.concatenate([lax.dynamic_index_in_dim(chunks, i, 0, keepdims=False) for i in ids])
        return pos, seg

    qpos, qseg = pos_seg(my_sub)
    if sub == 1:
        kpos, kseg = qpos, qseg
    else:
        every = [pos_seg(i) for i in range(sub)]
        kpos, kseg = (jnp.concatenate([e[i] for e in every]) for i in range(2))
    blocked = lambda v: v.reshape(-1, BLK)
    qb, qsb, kb, ksb = blocked(qpos), blocked(qseg), blocked(kpos), blocked(kseg)
    need = (
        (jnp.min(kb, 1)[None, :] <= jnp.max(qb, 1)[:, None])
        & (jnp.min(ksb, 1)[None, :] <= jnp.max(qsb, 1)[:, None])
        & (jnp.max(ksb, 1)[None, :] >= jnp.min(qsb, 1)[:, None])
    ).astype(jnp.int32)

    input_one, qkv_w, ff_both, cot = fence(input_one, qkv_w, ff_both, cot)
    near_one, side_one, ff_both = fence(near(input_one), across(input_one), ff_both)
    far_one, ff_got, near_one = fence(far(*near_one), chips(ff_both), near_one)
    far_one = join(far_one)
    more_one = across(*near_one)
    mine_one = [input_one, *near_one, far_one]
    all_one = fence(*mine_one, *side_one, *more_one, *across(far_one))

    def project_qkv(*values):
        shape = jax.ShapeDtypeStruct((rows, 4 * HP), BF)
        return simple_call(stack_project_kernel, shape, values, "project_qkv", 2 * rows * D * 4 * HP)

    qkv = project_qkv(*all_one, qkv_w)
    cot, *near_out = lax.optimization_barrier((cot, *near_out, all_one[-1]))[:-1]
    kv = ()
    if sub > 1:
        groups = [[s * sub + i for i in range(sub)] for s in range(4)]
        kv = (lax.all_gather(qkv[:, 2 * HP :], "head", axis=0, tiled=True, axis_index_groups=groups),)
    q_args = tuple(v.astype(F32).reshape(-1, 1, BLK) for v in (qpos, qseg, kpos, kseg))
    sharing = None if sub == 1 else [[s * sub + i for s in range(4)] for i in range(sub)]
    ff_all = jnp.stack(ff_got, 1).reshape(-1, 2 * ff_here)
    ff_all = lax.all_gather(ff_all, "head", axis=0, tiled=True, axis_index_groups=sharing)
    ff_all = ff_all.reshape(4, n_plane, share, 2 * ff_here)
    (o, lse), near_cot, far_out = fence(attend(need, qkv, *(kv or (None,)), *q_args), near(cot), far(*near_out))
    o_parts = o.reshape(2, n_blk, own, 2 * HP)
    mine_out = [output_weight, *near_out, join(far_out)]
    o_both, near_cot = fence(pair_up(o_parts[0], swap(o_parts[1], "dp", 1)), near_cot)
    o_got, side_out, near_cot, cut_cot = fence(chips(o_both), across(*mine_out), near_cot, halves(*near_cot))
    all_out = [*mine_out, *side_out]

    def out_project(*values):
        shapes = (jax.ShapeDtypeStruct((own, D), F32), jax.ShapeDtypeStruct((own, D), BF))
        kernel = functools.partial(out_project_kernel, n_blk)
        return simple_call(kernel, shapes, values, "out_project", 2 * own * D * D)

    (x_mid, input_two), side_cot = fence(
        out_project(*o_got, *all_out, x_low, gain_two[None]), across(cot, *near_cot)
    )

    def unpack_ff(value):
        shapes = (jax.ShapeDtypeStruct((D, ff_here), BF),) * 2
        return place_call(unpack_ff_kernel, shapes, ids, value, name="unpack_ff")

    def ff_part(n_mine, n_side, c_mine, c_side):
        return ff_call(n_mine, n_side, c_mine, c_side, gate_w, up_w, down_weight)

    gate_w, up_w = unpack_ff(after(ff_all, input_two))
    side_two = across(input_two)
    near_two, part_0, near_cot, cut_cot, gate_w, up_w = fence(
        near(input_two), ff_part(input_two, side_two[0], cot, side_cot[0]), near_cot, cut_cot, gate_w, up_w
    )
    more_two = across(*near_two)
    far_two, far_cot, part_1, part_2 = fence(
        far(*near_two),
        far_halves(*cut_cot),
        ff_part(near_two[0], more_two[0], near_cot[0], side_cot[1]),
        ff_part(near_two[1], more_two[1], near_cot[1], side_cot[2]),
    )
    far_two, far_cot = join(far_two), join(far_cot)
    last_two, last_cot = across(far_two, far_cot)
    side_parts = across(part_0[3], part_1[3], part_2[3])
    part_3, side_parts = fence(ff_part(far_two, last_two, far_cot, last_cot), side_parts)
    parts = [part_0, part_1, part_2, part_3]
    side_parts = [*side_parts, *across(part_3[3])]
    hidden, grad_gu = [p[0] for p in parts], [p[1] for p in parts]
    all_two = [input_two, *near_two, far_two, *side_two, *more_two, last_two]
    all_cot = [cot, *near_cot, far_cot, *side_cot, last_cot]
    local_two = [p[2] + v.astype(F32) for p, v in zip(parts, side_parts)]
    local_0, sent_two = fence(local_two[0], [v.astype(BF) for v in local_two])
    got_two = chips(sent_two)[1:]

    contract = ((0,), (0,))

    def rel_parts(mine):
        return rel_to_abs(mine, True)

    def head_sum(sent):
        return lax.psum_scatter(sent, "head", scatter_dimension=0, tiled=True)

    def owned_rows(chunks):
        if n_head != 4:
            return chunks[0].reshape(-1, chunks[0].shape[-1]).astype(F32)
        shape = jax.ShapeDtypeStruct((4 * chunks[0].shape[0], chunks[0].shape[1]), F32)
        return place_call(place_rows_kernel, shape, ids, *chunks, name="place_rows")

    def owned_columns(chunks, widths):
        if n_head != 4:
            full = rel_to_abs(jnp.moveaxis(chunks[0], 0, 1).reshape((2, n_blk, n_head) + chunks[0].shape[2:]))
            full = full.reshape(n_plane, n_rows, -1).transpose(1, 0, 2).astype(F32)
            ends = [sum(widths[: i + 1]) for i in range(len(widths))]
            return [full[:, :, e - w : e].reshape(n_rows, -1) for e, w in zip(ends, widths)]
        shapes = [jax.ShapeDtypeStruct((n_rows, n_plane * w), F32) for w in widths]
        kernel = functools.partial(place_columns_kernel, widths, len(chunks))
        return place_call(kernel, shapes, ids, *chunks, name="place_columns")

    ff_sent, down_sent = ff_weight_call(all_two, all_cot, grad_gu, hidden, n_head, n_plane)
    got_two, ff_sent, down_sent = fence(got_two, ff_sent, down_sent)
    down_mine = head_sum(down_sent)
    ff_mine = head_sum(ff_sent.reshape(D, 2 * ff_here)).reshape(n_plane, part, 2 * ff_here)

    def branch(*values):
        shapes = (
            jax.ShapeDtypeStruct((own, D), F32),
            jax.ShapeDtypeStruct((own, D), BF),
            jax.ShapeDtypeStruct((2, n_blk, own, 2 * HP), BF),
        )
        kernel = functools.partial(branch_kernel, n_blk)
        return simple_call(kernel, shapes, values, "branch", 2 * own * D * D)

    grad_mid, grad_branch, grad_o = fence(*branch(*all_out, local_0, *got_two, x_mid, cot, gain_two[None]))

    def back_project(transposed, *values):
        shapes = tuple(jax.ShapeDtypeStruct((n_blk, own, D), t) for t in (F32, BF))
        kernel = functools.partial(back_project_kernel, transposed)
        return simple_call(kernel, shapes, values, "back_project", 2 * rows * D * values[-1].size // D)

    do_both, hidden = fence(pair_up(grad_o[0], swap(grad_o[1], "dp", 1)), hidden)
    out_own, out_other = back_project(False, *hidden, down_weight)
    do_got, out_own, out_side, grad_branch = fence(chips(do_both), out_own, swap(out_other, "dp", 1), grad_branch)
    grad_o = jnp.stack(do_got, 1).reshape(rows, 2 * HP)
    line = n_head == 4
    no_step = lambda *v: ()
    step = line_step if line else no_step
    back = attend_back(need, qkv, *(kv or (None,)), *q_args, o, lse, grad_o)
    dqkv, near_branch, out_own, out_side = fence(back, near(grad_branch), out_own, out_side)
    local_out = [out_own[k] + out_side[k].astype(F32) for k in range(n_blk)]
    if sub > 1:
        dkv = lax.psum_scatter(dqkv[1], "head", scatter_dimension=0, tiled=True, axis_index_groups=groups)
        dqkv = [join([dqkv[0], dkv], 1)]
    dqkv = dqkv[0]
    qkv_grad, far_branch, dqkv, ff_mine, local_out, far_sum = fence(
        qkv_weight_call(all_one, dqkv, n_head, n_plane), far(*near_branch), dqkv, ff_mine, local_out, sum_far(local_out)
    )
    qkv_mine = head_sum(qkv_grad.reshape(D, 4 * HD)).reshape(n_plane, part, 4 * HD)
    mine_branch = [grad_branch, *near_branch, join(far_branch)]
    ff_rel = rel_parts(ff_mine)
    (one_own, one_other), side_branch, ff_both, got_out, local_out_0 = fence(
        back_project(True, dqkv, qkv_w),
        across(*mine_branch),
        pair_up(ff_rel[0], swap(ff_rel[1], "dp", 1)),
        sum_near(local_out, *far_sum),
        local_out[0],
    )
    block_out = (x_mid + local_out_0 + sum(g.astype(F32) for g in got_out)).astype(BF)

    def out_weights(*values):
        rows_per = values[1].shape[0]
        lanes = pl.BlockSpec((rows_per, 384), lambda j: (0, j))
        return pl.pallas_call(
            functools.partial(out_weight_kernel, n_plane),
            grid=(D // 384,),
            out_shape=jax.ShapeDtypeStruct((2 * HD, D), BF),
            in_specs=[pl.BlockSpec(values[0].shape, lambda j: (0, 0), pipeline_mode=pl.Buffered(1))] + [lanes] * n_plane,
            out_specs=pl.BlockSpec((2 * HD, 384), lambda j: (0, j)),
            compiler_params=pltpu.CompilerParams(vmem_limit_bytes=48 << 20),
            cost_estimate=small_cost(flops=4 * rows * D * 2 * HP, transcendentals=0, bytes_accessed=9 << 20),
            name="out_weight",
        )(*values)

    one_side = swap(one_other, "dp", 1)
    local_one = [one_own[k] + one_side[k].astype(F32) for k in range(n_blk)]
    ff_got, out_grad, local_0, sent_one, down_mine = fence(
        chips(ff_both),
        out_weights(o, *mine_branch, *side_branch),
        local_one[0],
        [v.astype(BF) for v in local_one],
        down_mine,
    )
    out_mine = head_sum(out_grad)
    late_down = lax.all_gather(down_mine, "head", axis=0)
    ff_rows = jnp.stack(ff_got, 1).reshape(ff_mine.shape)
    ff_0 = step(ff_rows, ff_rows)
    got_one, ff_1, ff_0, qkv_mine, out_mine, block_out = fence(
        chips(sent_one)[1:], step(*ff_0), ff_0, qkv_mine, out_mine, block_out
    )
    normed, factor = normalize(x_low.astype(F32))
    grad_in_one = local_0 + sum(g.astype(F32) for g in got_one)
    grad_input = (grad_mid + norm_back(grad_in_one, gain_one, normed, factor)).astype(BF)
    qkv_rel = rel_parts(qkv_mine)
    qkv_both = pair_up(qkv_rel[0], swap(qkv_rel[1], "dp", 1))
    qkv_rows = chips(qkv_both)
    ff_2, grad_input, block_out = fence(step(*ff_1), grad_input, block_out)
    out_rows = out_mine.reshape(part, -1, 4 * HD).transpose(1, 0, 2) if line else out_mine
    late = join([jnp.stack(qkv_rows, 1).reshape(-1, 4 * HD), out_rows.reshape(-1, 4 * HD)])
    late = lax.all_gather(late, "head", axis=0)
    grad_input = from_plane(grad_input)
    block_out = from_plane(block_out)
    grad_down = late_down.reshape(-1, D).astype(F32)
    if line:
        ff_chunks = [ff_2[0], ff_1[0], ff_0[0], ff_rows, ff_0[1], ff_1[1], ff_2[1]]
    else:
        ff_chunks = [lax.all_gather(ff_rows, "head", axis=0)]
    grad_gate_w, grad_up_w = owned_columns(ff_chunks, (ff_here, ff_here))
    def gain_grad(gain, *pairs):
        return sum(jnp.sum(w.astype(F32) * g, -1) for w, g in pairs) / gain.astype(F32)

    if line:
        matrices = (query_weight, key_weight, value_weight)
        shapes = [jax.ShapeDtypeStruct(w.shape, F32) for w in (*matrices, output_weight)]
        shapes.append(jax.ShapeDtypeStruct((1, n_rows), F32))
        values = (late, *matrices, norm_gain_one.astype(F32)[None])
        grad_query, grad_key, grad_value, grad_out, grad_gain_one = place_call(last_kernel, shapes, ids, *values, name="last")
        grad_gain_one = grad_gain_one[0]
    else:
        late_qkv = late[:, : n_plane * part].reshape(n_head, n_plane, part, 4 * HD)
        late_out = late[:, n_plane * part :].reshape(n_head, part, D)
        grad_query, grad_key, grad_value = owned_columns([late_qkv], (2 * HD, HD, HD))
        grad_out = owned_rows([late_out])
        grad_gain_one = gain_grad(
            norm_gain_one, (query_weight, grad_query), (key_weight, grad_key), (value_weight, grad_value)
        )
    grad_gain_two = gain_grad(norm_gain_two, (gate_weight, grad_gate_w), (up_weight, grad_up_w))
    return (
        block_out[:, None],
        grad_input[:, None],
        grad_gain_one,
        grad_query,
        grad_key,
        grad_value,
        grad_out,
        grad_gain_two,
        grad_gate_w,
        grad_up_w,
        grad_down,
    )


def solution(mesh):
    tokens = P(None, "dp", ("blk", "head"), None)
    vector = P(("dp", "blk"))
    matrix = P(("dp", "blk"), None)
    return jax.shard_map(
        per_device,
        mesh=mesh,
        in_specs=(
            tokens,
            P(None, "dp", "blk"),
            tokens,
            vector,
            matrix,
            matrix,
            matrix,
            matrix,
            vector,
            matrix,
            matrix,
            matrix,
        ),
        out_specs=(tokens, tokens, vector, matrix, matrix, matrix, matrix, vector, matrix, matrix, matrix),
        check_vma=False,
    )
```

```python
import functools
import math

import jax
import jax.numpy as jnp
from jax import lax
from jax.experimental import pallas as pl
from jax.experimental.pallas import tpu as pltpu
from jax.sharding import PartitionSpec as P

D = 1536
QH = 16
KVH = 8
HD = 96
HP = 128
FF = 4096
EPS = 1e-05
NEG = -1e30
BLK = 256
BF = jnp.bfloat16
F32 = jnp.float32


def small_cost(flops, transcendentals, bytes_accessed):
    part = 64
    return pl.CostEstimate(
        flops=flops // part, transcendentals=transcendentals // part, bytes_accessed=bytes_accessed // part
    )


def dot(left, right, dims=((1,), (0,))):
    return lax.dot_general(left, right, (dims, ((), ())), preferred_element_type=F32)


def normalize(values):
    factor = lax.rsqrt(jnp.mean(values * values, -1, keepdims=True) + EPS)
    return values * factor, factor


def norm_back(grad_norm, gain, normed, factor):
    scaled = grad_norm * gain
    return factor * (scaled - normed * jnp.mean(scaled * normed, -1, keepdims=True))


def rows_of(index):
    return pl.ds(pl.multiple_of(index * BLK, BLK), BLK)


def as_column(row):
    return jnp.broadcast_to(row, (HP, BLK)).T[:, 0:1]


def as_row(col):
    return jnp.broadcast_to(col, (BLK, HP)).T[0:1, :]


def keys_to_columns(kp_ref, ks_ref, pos_sc, seg_sc):
    def one(j, _):
        pos_sc[rows_of(j), :] = as_column(kp_ref[j])
        seg_sc[rows_of(j), :] = as_column(ks_ref[j])
        return 0

    lax.fori_loop(0, kp_ref.shape[0], one, 0)


def attn_fwd_kernel(first, need, q_ref, kv_ref, qp_ref, qs_ref, kp_ref, ks_ref, o_ref, lse_ref, m_sc, l_sc, acc_sc, pos_sc, seg_sc):
    scale = 1.0 / math.sqrt(HD)
    n_q, n_k = q_ref.shape[0] // BLK, kv_ref.shape[0] // BLK
    k_cols, v_cols = slice(first, first + HP), slice(first + HP, first + 2 * HP)
    keys_to_columns(kp_ref, ks_ref, pos_sc, seg_sc)

    def one_query(i, _):
        qr = rows_of(i)
        m_sc[...] = jnp.full_like(m_sc, NEG)
        l_sc[...] = jnp.zeros_like(l_sc)
        acc_sc[...] = jnp.zeros_like(acc_sc)
        qpos, qseg = qp_ref[i], qs_ref[i]

        def one_key(j, _):
            @pl.when(need[i, j] != 0)
            def _():
                kr = rows_of(j)
                ok = (pos_sc[kr, :] <= qpos) & (seg_sc[kr, :] == qseg)
                k, v = kv_ref[kr, k_cols], kv_ref[kr, v_cols]
                state = [(m_sc[g], l_sc[g], acc_sc[g], q_ref[qr, g * HP : (g + 1) * HP]) for g in range(2)]
                scores = [jnp.where(ok, dot(k, q, ((1,), (1,))) * scale, 2.0 * NEG) for _, _, _, q in state]
                new = []
                for (m_old, l_old, acc_old, _), s in zip(state, scores):
                    m_new = jnp.maximum(m_old, jnp.max(s, 0, keepdims=True))
                    p = jnp.exp(s - m_new)
                    decay = jnp.exp(m_old - m_new)
                    total = l_old * decay + jnp.sum(p, 0, keepdims=True)
                    new.append((m_new, total, acc_old * decay + dot(v, p.astype(BF), ((0,), (0,)))))
                for g in range(2):
                    m_sc[g], l_sc[g], acc_sc[g] = new[g]

            return 0

        lax.fori_loop(0, n_k, one_key, 0)
        for g in range(2):
            o_ref[qr, g * HP : (g + 1) * HP] = (acc_sc[g] / l_sc[g]).T.astype(BF)
            lse_ref[i, g : g + 1, :] = m_sc[g] + jnp.log(l_sc[g])
        return 0

    lax.fori_loop(0, n_q, one_query, 0)


def attn_bwd_kernel(first, need, q_ref, kv_ref, qp_ref, qs_ref, kp_ref, ks_ref, o_ref, lse_ref, do_ref, *rest):
    dq_ref, dkv_ref = rest[0], rest[-6]
    dq_sc, dk_sc, dv_sc, pos_sc, seg_sc = rest[-5:]
    scale = 1.0 / math.sqrt(HD)
    n_q, n_k = q_ref.shape[0] // BLK, kv_ref.shape[0] // BLK
    k_cols, v_cols = slice(first, first + HP), slice(first + HP, first + 2 * HP)
    dk_sc[...] = jnp.zeros_like(dk_sc)
    dv_sc[...] = jnp.zeros_like(dv_sc)
    keys_to_columns(kp_ref, ks_ref, pos_sc, seg_sc)

    def one_query(i, _):
        qr = rows_of(i)
        dq_sc[...] = jnp.zeros_like(dq_sc)
        qpos, qseg = qp_ref[i], qs_ref[i]
        lse, delta = [], []
        for g in range(2):
            cols = slice(g * HP, (g + 1) * HP)
            lse.append(lse_ref[i, g : g + 1, :])
            prod = do_ref[qr, cols].astype(F32) * o_ref[qr, cols].astype(F32)
            delta.append(as_row(jnp.sum(prod, -1, keepdims=True)))

        def one_key(j, _):
            @pl.when(need[i, j] != 0)
            def _():
                kr = rows_of(j)
                ok = (pos_sc[kr, :] <= qpos) & (seg_sc[kr, :] == qseg)
                k, v = kv_ref[kr, k_cols], kv_ref[kr, v_cols]
                qs = [q_ref[qr, g * HP : (g + 1) * HP] for g in range(2)]
                dos = [do_ref[qr, g * HP : (g + 1) * HP] for g in range(2)]
                scores = [dot(k, q, ((1,), (1,))) * scale for q in qs]
                dps = [dot(v, do, ((1,), (1,))) for do in dos]
                dv, dk = dv_sc[kr, :], dk_sc[kr, :]
                dqs = []
                for g in range(2):
                    p = jnp.where(ok, jnp.exp(scores[g] - lse[g]), 0.0)
                    ds = (p * (dps[g] - delta[g])).astype(BF)
                    dv = dv + dot(p.astype(BF), dos[g])
                    dk = dk + dot(ds, qs[g])
                    dqs.append(dot(ds, k, ((0,), (0,))))
                dv_sc[kr, :], dk_sc[kr, :] = dv, dk
                for g in range(2):
                    dq_sc[g] += dqs[g]

            return 0

        lax.fori_loop(0, n_k, one_key, 0)
        for g in range(2):
            dq_ref[qr, g * HP : (g + 1) * HP] = (dq_sc[g] * scale).astype(BF)
        return 0

    lax.fori_loop(0, n_q, one_query, 0)
    dkv_ref[:, k_cols] = (dk_sc[...] * scale).astype(BF)
    dkv_ref[:, v_cols] = dv_sc[...].astype(BF)


def in_vmem(count):
    return [pl.BlockSpec(memory_space=pltpu.SMEM)] + [pl.BlockSpec(memory_space=pltpu.VMEM)] * count


def attn_cost(n_q, n_k, products):
    return small_cost(
        flops=2 * products * n_q * n_k * 2 * HP, transcendentals=n_q * n_k * 2, bytes_accessed=(n_q + n_k) * HP * 16
    )


def attend(need, q, kv, qpos, qseg, kpos, kseg):
    first, kv = (2 * HP, q) if kv is None else (0, kv)
    n_q, n_k = q.shape[0], kv.shape[0]
    return pl.pallas_call(
        functools.partial(attn_fwd_kernel, first),
        out_shape=(jax.ShapeDtypeStruct((n_q, 2 * HP), BF), jax.ShapeDtypeStruct((n_q // BLK, 2, BLK), F32)),
        in_specs=in_vmem(6),
        out_specs=(pl.BlockSpec(memory_space=pltpu.VMEM),) * 2,
        scratch_shapes=[pltpu.VMEM((2, 1, BLK), F32)] * 2 + [pltpu.VMEM((2, HP, BLK), F32)] + [pltpu.VMEM((n_k, 1), F32)] * 2,
        compiler_params=pltpu.CompilerParams(vmem_limit_bytes=40 << 20),
        cost_estimate=attn_cost(n_q, n_k, 2),
        name="attn_fwd",
    )(need, q, kv, qpos, qseg, kpos, kseg)


def attend_back(need, q, kv, qpos, qseg, kpos, kseg, o, lse, do):
    joint = kv is None
    first, kv = (2 * HP, q) if joint else (0, kv)
    n_q, n_k = q.shape[0], kv.shape[0]
    shapes = [jax.ShapeDtypeStruct((n_q, 4 * HP), BF)] if joint else [jax.ShapeDtypeStruct((n, 2 * HP), BF) for n in (n_q, n_k)]
    return pl.pallas_call(
        functools.partial(attn_bwd_kernel, first),
        out_shape=shapes,
        in_specs=in_vmem(9),
        out_specs=[pl.BlockSpec(memory_space=pltpu.VMEM)] * len(shapes),
        scratch_shapes=[pltpu.VMEM((2, BLK, HP), F32)] + [pltpu.VMEM((n_k, HP), F32)] * 2 + [pltpu.VMEM((n_k, 1), F32)] * 2,
        compiler_params=pltpu.CompilerParams(vmem_limit_bytes=48 << 20),
        cost_estimate=attn_cost(n_q, n_k, 5),
        name="attn_bwd",
    )(need, q, kv, qpos, qseg, kpos, kseg, o, lse, do)


def whole(count):
    return [pl.BlockSpec(memory_space=pltpu.VMEM)] * count


def place_call(kernel, out_shape, ids, *values, name, scratch=()):
    moved = sum(v.size * v.dtype.itemsize for v in values)
    return pl.pallas_call(
        kernel,
        out_shape=out_shape,
        in_specs=[pl.BlockSpec(memory_space=pltpu.SMEM)] + whole(len(values)),
        out_specs=jax.tree.map(lambda _: pl.BlockSpec(memory_space=pltpu.VMEM), out_shape),
        scratch_shapes=scratch,
        compiler_params=pltpu.CompilerParams(vmem_limit_bytes=40 << 20),
        cost_estimate=small_cost(flops=0, transcendentals=0, bytes_accessed=2 * moved),
        name=name,
    )(ids, *values)


def pack_qkv_kernel(ids, q_ref, k_ref, v_ref, small_ref, out_ref):
    rows = q_ref.shape[0]
    for dev in range(KVH):
        slot = ids[0] ^ dev
        pieces = [q_ref[:, 2 * dev * HD : 2 * (dev + 1) * HD]]
        pieces += [ref[:, dev * HD : (dev + 1) * HD] for ref in (k_ref, v_ref)]
        out_ref[slot, :rows, :] = jnp.concatenate(pieces, 1)
        out_ref[slot, rows:, :] = small_ref[...]


def pack_ff_kernel(ids, gate_ref, up_ref, out_ref):
    width = gate_ref.shape[1] // KVH
    for dev in range(KVH):
        slot = ids[0] ^ dev
        for i, ref in enumerate((gate_ref, up_ref)):
            out_ref[slot, :, i * width : (i + 1) * width] = ref[:, dev * width : (dev + 1) * width]


def head_kernel(n_blk, ids, *refs):
    got, x_refs = refs[:n_blk], refs[n_blk : n_blk + 2]
    w_ref, seg_ref, gain_ref, x_ref, c_ref, n_ref, small_sc = refs[n_blk + 2 :]
    n_rows = w_ref.shape[0] // (2 * n_blk)
    zero = jnp.zeros((n_rows, HP - HD), BF)
    for k, ref in enumerate(got):
        for core in range(2):
            at = pl.multiple_of((ids[0] ^ (core * n_blk + k)) * n_rows, 16)
            heads = [ref[core, :n_rows, i * HD : (i + 1) * HD] for i in range(4)]
            w_ref[pl.ds(at, n_rows), :] = jnp.concatenate([v for head in heads for v in (head, zero)], 1)
            small_sc[core * n_blk + k] = ref[core, n_rows:, :]
    gains = [[], []]
    for dev in range(2 * n_blk):
        small = small_sc[ids[0] ^ dev]
        seg_ref[dev] = small
        small = small.astype(F32)
        for i in range(2):
            gains[i].append(small[i : i + 1, :n_rows])
    for i in range(2):
        gain_ref[i] = jnp.concatenate(gains[i], 1)
    tok = x_refs[0].shape[0] // 2
    for i, ref in enumerate(x_refs):
        x = ref[:tok, :]
        x_ref[i * tok : (i + 1) * tok, :] = x
        c_ref[i * tok : (i + 1) * tok, :] = ref[tok:, :]
        x = x.astype(F32)
        factor = lax.rsqrt(jnp.mean(x * x, -1, keepdims=True) + EPS)
        n_ref[i * tok : (i + 1) * tok, :] = (x * factor * gain_ref[0]).astype(BF)


def unpack_ff_kernel(ids, in_ref, gate_ref, up_ref):
    n_head, n_slot, part, width = in_ref.shape
    for head in range(n_head):
        for slot in range(n_slot):
            at = pl.ds(pl.multiple_of(((ids[0] ^ slot) * n_head + head) * part, 16), part)
            gate_ref[at, :] = in_ref[head, slot, :, : width // 2]
            up_ref[at, :] = in_ref[head, slot, :, width // 2 :]


def chunk_heads(ids, count):
    if count == 7:
        return [(ids[1] + (i - 3), (ids[1] + (i - 3) >= 0) & (ids[1] + (i - 3) < 4)) for i in range(7)]
    return [(i, None) for i in range(count)]


def place_chunk(ok, body):
    if ok is None:
        body()
    else:
        pl.when(ok)(body)


def place_rows_kernel(ids, *refs):
    out_ref = refs[-1]
    part = refs[0].shape[0]
    for ref, (head, ok) in zip(refs[:-1], chunk_heads(ids, len(refs) - 1)):

        def body():
            out_ref[pl.ds(pl.multiple_of(head * part, 16), part), :] = ref[...].astype(F32)

        place_chunk(ok, body)


def place_columns_kernel(widths, count, ids, *refs):
    chunks, outs = refs[:count], refs[count:]
    n_slot, part = chunks[0].shape[:2]
    for ref, (head, ok) in zip(chunks, chunk_heads(ids, count)):

        def body():
            at = pl.ds(pl.multiple_of(head * part, 16), part)
            first = 0
            for out_ref, width in zip(outs, widths):
                for pair in range(0, n_slot, 2):
                    both = [ref[ids[0] ^ dev][:, first : first + width] for dev in (pair, pair + 1)]
                    out_ref[at, pair * width : (pair + 2) * width] = jnp.concatenate(both, 1).astype(F32)
                first += width

        place_chunk(ok, body)


def last_kernel(ids, in_ref, q_w, k_w, v_w, gain_ref, q_ref, k_ref, v_ref, out_ref, sum_ref):
    n_head = in_ref.shape[0]
    n_rows = q_w.shape[0]
    part = n_rows // n_head
    n_slot = 2 * (q_w.shape[1] // (4 * HD))
    for head in range(n_head):
        at = slice(head * part, (head + 1) * part)
        for pair in range(0, n_slot, 2):
            two = [in_ref[head, pl.ds(pl.multiple_of((ids[0] ^ dev) * part, 16), part), :] for dev in (pair, pair + 1)]
            for ref, first, width in ((q_ref, 0, 2 * HD), (k_ref, 2 * HD, HD), (v_ref, 3 * HD, HD)):
                both = jnp.concatenate([v[:, first : first + width] for v in two], 1)
                ref[at, pair * width : (pair + 2) * width] = both.astype(F32)
        for i in range(D // (4 * HD)):
            rows = slice((n_slot + i) * part, (n_slot + i + 1) * part)
            out_ref[at, i * 4 * HD : (i + 1) * 4 * HD] = in_ref[head, rows, :].astype(F32)
    total = None
    for w, g in ((q_w, q_ref), (k_w, k_ref), (v_w, v_ref)):
        one = jnp.sum(w[...].astype(F32) * g[...], -1, keepdims=True)
        total = one if total is None else total + one
    sum_ref[...] = jnp.broadcast_to(total, (n_rows, 128)).T[0:1, :] / gain_ref[...]


def ff_kernel(n0, n1, c0, c1, gate_ref, up_ref, down_ref, hid_ref, dgu_ref, own_ref, other_ref):
    width = gate_ref.shape[1]
    for i, (n_ref, c_ref) in ((1, (n1, c1)), (0, (n0, c0))):
        n = n_ref[...]
        gate = dot(n, gate_ref[...])
        up = dot(n, up_ref[...])
        grad = dot(c_ref[...], down_ref[...], ((1,), (1,)))
        sigma = jax.nn.sigmoid(gate)
        silu = gate * sigma
        hid_ref[i] = (silu * up).astype(BF)
        grad_gate = (grad * up * sigma * (1.0 + gate * (1.0 - sigma))).astype(BF)
        grad_up = (grad * silu).astype(BF)
        dgu_ref[i, :, :width] = grad_gate
        dgu_ref[i, :, width:] = grad_up
        total = dot(grad_gate, gate_ref[...], ((1,), (1,))) + dot(grad_up, up_ref[...], ((1,), (1,)))
        if i == 0:
            own_ref[...] = total
        else:
            other_ref[...] = total.astype(BF)


def ff_call(n0, n1, c0, c1, gate_w, up_w, down_w):
    rows, width = n0.shape[0], gate_w.shape[1]
    return pl.pallas_call(
        ff_kernel,
        out_shape=(
            jax.ShapeDtypeStruct((2, rows, width), BF),
            jax.ShapeDtypeStruct((2, rows, 2 * width), BF),
            jax.ShapeDtypeStruct((rows, D), F32),
            jax.ShapeDtypeStruct((rows, D), BF),
        ),
        in_specs=whole(7),
        out_specs=tuple(whole(4)),
        compiler_params=pltpu.CompilerParams(vmem_limit_bytes=40 << 20),
        cost_estimate=small_cost(
            flops=2 * 2 * rows * D * width * 5, transcendentals=2 * rows * width, bytes_accessed=12 << 20
        ),
        name="ff",
    )(n0, n1, c0, c1, gate_w, up_w, down_w)


def ff_weight_kernel(n_pairs, *refs):
    n_refs, c_refs = refs[: 2 * n_pairs], refs[2 * n_pairs : 4 * n_pairs]
    dgu_refs, hid_refs = refs[4 * n_pairs : 5 * n_pairs], refs[5 * n_pairs : 6 * n_pairs]
    ff_ref, down_ref = refs[6 * n_pairs :]
    over = ((0,), (0,))
    total_ff = total_down = None
    for i in range(2 * n_pairs):
        core, k = i // n_pairs, i % n_pairs
        one = dot(n_refs[i][...], dgu_refs[k][core], over)
        two = dot(hid_refs[k][core], c_refs[i][...], over)
        total_ff = one if total_ff is None else total_ff + one
        total_down = two if total_down is None else total_down + two
    n_head, n_dev, part, width = ff_ref.shape
    for dev in range(n_dev):
        for head in range(n_head):
            first = (dev * n_head + head) * part
            ff_ref[head, dev] = total_ff[first : first + part].astype(BF)
    down_ref[...] = total_down.astype(BF)


def ff_weight_call(n_list, c_list, dgu_list, hid_list, n_head, n_plane):
    n_pairs = len(dgu_list)
    rows, width2 = n_list[0].shape[0], dgu_list[0].shape[2]
    part = D // n_plane // n_head
    cols = 384
    steps = D // cols
    lanes = pl.BlockSpec((rows, cols), lambda j: (0, j))
    fixed = lambda v: pl.BlockSpec(v.shape, lambda j: (0, 0, 0), pipeline_mode=pl.Buffered(1))
    per_step = n_plane // steps
    return pl.pallas_call(
        functools.partial(ff_weight_kernel, n_pairs),
        grid=(steps,),
        out_shape=(
            jax.ShapeDtypeStruct((n_head, n_plane, part, width2), BF),
            jax.ShapeDtypeStruct((width2 // 2, D), BF),
        ),
        in_specs=[lanes] * (4 * n_pairs) + [fixed(v) for v in dgu_list] + [fixed(v) for v in hid_list],
        out_specs=(
            pl.BlockSpec((n_head, per_step, part, width2), lambda j: (0, j, 0, 0)),
            pl.BlockSpec((width2 // 2, cols), lambda j: (0, j)),
        ),
        compiler_params=pltpu.CompilerParams(vmem_limit_bytes=56 << 20),
        cost_estimate=small_cost(
            flops=2 * 2 * n_pairs * rows * D * width2 * 3 // 2, transcendentals=0, bytes_accessed=24 << 20
        ),
        name="ff_weight",
    )(*n_list, *c_list, *dgu_list, *hid_list)


def simple_call(kernel, out_shape, values, name, flops):
    leaves = jax.tree.leaves(out_shape)
    moved = sum(v.size * v.dtype.itemsize for v in list(values) + leaves)
    return pl.pallas_call(
        kernel,
        out_shape=out_shape,
        in_specs=whole(len(values)),
        out_specs=jax.tree.map(lambda _: pl.BlockSpec(memory_space=pltpu.VMEM), out_shape),
        compiler_params=pltpu.CompilerParams(vmem_limit_bytes=52 << 20),
        cost_estimate=small_cost(flops=flops, transcendentals=0, bytes_accessed=moved),
        name=name,
    )(*values)


def stack_project_kernel(*refs):
    weight, out_ref = refs[-2], refs[-1]
    rows = refs[0].shape[0]
    for i, ref in enumerate(refs[:-2]):
        out_ref[i * rows : (i + 1) * rows, :] = dot(ref[...], weight[...]).astype(BF)


def out_project_kernel(n_blk, *refs):
    o_refs, w_refs = refs[:n_blk], refs[n_blk : 3 * n_blk]
    x_ref, gain_ref, mid_ref, n_ref = refs[3 * n_blk :]
    total = x_ref[...].astype(F32)
    for core in range(2):
        for k in range(n_blk):
            o = o_refs[k][core]
            o = jnp.concatenate([o[:, :HD], o[:, HP : HP + HD]], 1)
            total = total + dot(o, w_refs[core * n_blk + k][...])
    mid_ref[...] = total
    factor = lax.rsqrt(jnp.mean(total * total, -1, keepdims=True) + EPS)
    n_ref[...] = (total * factor * gain_ref[...]).astype(BF)


def branch_kernel(n_blk, *refs):
    w_refs = refs[: 2 * n_blk]
    local_ref, got_refs = refs[2 * n_blk], refs[2 * n_blk + 1 : 3 * n_blk]
    mid_ref, cot_ref, gain_ref, grad_ref, branch_ref, do_ref = refs[3 * n_blk :]
    total = local_ref[...]
    for ref in got_refs:
        total = total + ref[...].astype(F32)
    mid = mid_ref[...]
    factor = lax.rsqrt(jnp.mean(mid * mid, -1, keepdims=True) + EPS)
    grad = cot_ref[...].astype(F32) + norm_back(total, gain_ref[...], mid * factor, factor)
    grad_ref[...] = grad
    branch = grad.astype(BF)
    branch_ref[...] = branch
    zero = jnp.zeros((branch.shape[0], HP - HD), BF)
    for core in range(2):
        for k in range(n_blk):
            do = dot(branch, w_refs[core * n_blk + k][...], ((1,), (1,))).astype(BF)
            do_ref[core, k] = jnp.concatenate([do[:, :HD], zero, do[:, HD:], zero], 1)


def back_project_kernel(transposed, *refs):
    weight, own_ref, other_ref = refs[-3], refs[-2], refs[-1]
    dims = ((1,), (1,)) if transposed else ((1,), (0,))
    n_blk, rows = own_ref.shape[:2]
    for core in (1, 0):
        for k in range(n_blk):
            at = (core * n_blk + k) * rows
            value = refs[0][at : at + rows, :] if len(refs) == 4 else refs[k][core]
            part = dot(value, weight[...], dims)
            if core:
                other_ref[k] = part.astype(BF)
            else:
                own_ref[k] = part


def out_weight_kernel(count, *refs):
    o_ref, b_refs, out_ref = refs[0], refs[1 : 1 + count], refs[-1]
    rows = b_refs[0].shape[0]
    total = None
    for i, ref in enumerate(b_refs):
        one = dot(o_ref[i * rows : (i + 1) * rows, :], ref[...], ((0,), (0,)))
        total = one if total is None else total + one
    out_ref[:HD, :] = total[:HD].astype(BF)
    out_ref[HD:, :] = total[HP : HP + HD].astype(BF)


def qkv_weight_kernel(n_refs_count, *refs):
    n_refs, grad_ref, out_ref = refs[:n_refs_count], refs[-2], refs[-1]
    rows = n_refs[0].shape[0]
    total = None
    for i, ref in enumerate(n_refs):
        one = dot(ref[...], grad_ref[i * rows : (i + 1) * rows, :], ((0,), (0,)))
        total = one if total is None else total + one
    total = jnp.concatenate([total[:, g * HP : g * HP + HD] for g in range(4)], 1)
    n_head, n_dev, part, _ = out_ref.shape
    for dev in range(n_dev):
        for head in range(n_head):
            first = (dev * n_head + head) * part
            out_ref[head, dev] = total[first : first + part].astype(BF)


def qkv_weight_call(n_list, dqkv, n_head, n_plane):
    rows = n_list[0].shape[0]
    part = D // n_plane // n_head
    cols = 384
    steps = D // cols
    return pl.pallas_call(
        functools.partial(qkv_weight_kernel, len(n_list)),
        grid=(steps,),
        out_shape=jax.ShapeDtypeStruct((n_head, n_plane, part, 4 * HD), BF),
        in_specs=[pl.BlockSpec((rows, cols), lambda j: (0, j))] * len(n_list)
        + [pl.BlockSpec(dqkv.shape, lambda j: (0, 0), pipeline_mode=pl.Buffered(1))],
        out_specs=pl.BlockSpec((n_head, n_plane // steps, part, 4 * HD), lambda j: (0, j, 0, 0)),
        compiler_params=pltpu.CompilerParams(vmem_limit_bytes=48 << 20),
        cost_estimate=small_cost(
            flops=2 * len(n_list) * rows * D * 4 * HP * 2, transcendentals=0, bytes_accessed=12 << 20
        ),
        name="qkv_weight",
    )(*n_list, dqkv)


def after(value, *first):
    return lax.optimization_barrier((value,) + first)[0]


def swap(value, axis, mask):
    return lax.ppermute(value, axis, [(i, i ^ mask) for i in range(lax.axis_size(axis))])


class Stages:
    def __init__(self):
        self.last = ()

    def __call__(self, *trees):
        leaves, tree = jax.tree.flatten(trees)
        tied = lax.optimization_barrier(tuple(leaves) + self.last)
        self.last = (tied[0],)
        return jax.tree.unflatten(tree, tied[: len(leaves)])


def near(value):
    return swap(value, "blk", 1), swap(value, "blk", 2)


def halves(one, two):
    half = one.shape[0] // 2
    return one[:half], two[half:]


def far_halves(low, high):
    return swap(low, "blk", 2), swap(high, "blk", 1)


def far(one, two):
    return far_halves(*halves(one, two))


def across(*values):
    return tuple(swap(v, "dp", 1) for v in values)


def chips(both):
    return [both[0]] + [swap(both[k], "blk", k) for k in range(1, len(both))]


def pair_up(mine, other):
    return [jnp.stack([mine[k], other[k]]) for k in range(mine.shape[0])]


def add_cores(own, other):
    return own + swap(other, "dp", 1).astype(F32)


def sum_far(parts):
    half = parts[3].shape[0] // 2
    return swap(parts[3][:half].astype(BF), "blk", 1), swap(parts[3][half:].astype(BF), "blk", 2)


def sum_near(parts, low, high):
    half = parts[3].shape[0] // 2
    one = jnp.concatenate([parts[1][:half], parts[1][half:] + high.astype(F32)])
    two = jnp.concatenate([parts[2][:half] + low.astype(F32), parts[2][half:]])
    return swap(one.astype(BF), "blk", 1), swap(two.astype(BF), "blk", 2)


def line_step(left, right):
    up = [(i, i + 1) for i in range(3)]
    return lax.ppermute(left, "head", up), lax.ppermute(right, "head", [(b, a) for a, b in up])


def rel_to_abs(value, reverse=False):
    n_blk = lax.axis_size("blk")
    mine = lax.axis_index("dp") * n_blk + lax.axis_index("blk")
    flat = value.reshape((2 * n_blk,) + value.shape[(1 if reverse else 2) :])
    out = jnp.stack([lax.dynamic_index_in_dim(flat, i ^ mine, 0, keepdims=False) for i in range(2 * n_blk)])
    return out.reshape((2, n_blk) + out.shape[1:]) if reverse else out


def per_device(
    activations,
    segments,
    cotangent,
    norm_gain_one,
    query_weight,
    key_weight,
    value_weight,
    output_weight,
    norm_gain_two,
    gate_weight,
    up_weight,
    down_weight,
):
    n_blk, n_head = lax.axis_size("blk"), lax.axis_size("head")
    n_plane = 2 * n_blk
    assert lax.axis_size("dp") == 2 and activations.shape[0] == 2 and n_plane == KVH
    sub = n_head // 4
    tok = activations.shape[2]
    span = tok * n_head
    own = 2 * tok
    rows = n_plane * own
    my_dp, my_blk, my_head = (lax.axis_index(name) for name in ("dp", "blk", "head"))
    my_seq, my_sub = my_head // sub, my_head % sub

    def routes(k):
        pairs = []
        for core in range(2):
            for head in range(n_head):
                seq_part, sub_part = head // sub, head % sub
                target = 2 * (k ^ (seq_part & 1)) + core
                pairs.append((core * n_head + head, (seq_part >> 1) * n_head + target * sub + sub_part))
        return pairs

    def to_plane(*values):
        parts = []
        for k in range(2):
            piece = [lax.dynamic_index_in_dim(v[:, 0], k ^ (my_seq & 1), 0, keepdims=False) for v in values]
            parts.append(lax.ppermute(jnp.concatenate(piece), ("dp", "head"), routes(k)))
        return parts

    def from_plane(value):
        parts = []
        for k in range(2):
            back = [(b, a) for a, b in routes(k)]
            parts.append(lax.ppermute(value[k * tok : (k + 1) * tok], ("dp", "head"), back))
        odd = (my_seq & 1) == 1
        return jnp.stack([jnp.where(odd, parts[1], parts[0]), jnp.where(odd, parts[0], parts[1])])

    me = my_dp * n_blk + my_blk
    ids = jnp.stack([me, my_head]).astype(jnp.int32)
    n_rows = D // n_plane
    part = n_rows // n_head
    ff_here = FF // n_plane
    width = 4 * HD
    seg_rows = -(-2 * span // width)
    small_rows = -(-(2 + seg_rows) // 16) * 16
    gain_row = lambda v: jnp.pad(v, (0, width - n_rows))
    small = [gain_row(norm_gain_one), gain_row(norm_gain_two), segments[:, 0].reshape(-1).astype(BF)]
    small = jnp.concatenate(small)
    small = jnp.pad(small, (0, small_rows * width - small.shape[0])).reshape(small_rows, width)
    fence = Stages()
    join = jnp.concatenate
    share = n_rows // 4

    def pack_qkv(*values):
        shape = jax.ShapeDtypeStruct((n_plane, n_rows + small_rows, width), BF)
        packed = place_call(pack_qkv_kernel, shape, ids, *values, name="pack_qkv")
        return packed.reshape((2, n_blk) + packed.shape[1:])

    def pack_ff(gate, up):
        cut = [lax.dynamic_slice_in_dim(w, my_seq * share, share, 0) for w in (gate, up)]
        shape = jax.ShapeDtypeStruct((n_plane, share, 2 * ff_here), BF)
        packed = place_call(pack_ff_kernel, shape, ids, *cut, name="pack_ff")
        return packed.reshape((2, n_blk) + packed.shape[1:])

    near_out = near(output_weight)
    packed, act_low, cot_low, gate_low, up_low = fence(
        pack_qkv(query_weight, key_weight, value_weight, small), activations, cotangent, gate_weight, up_weight
    )
    both, near_out, act_low, cot_low, gate_low, up_low = fence(
        pair_up(packed[0], swap(packed[1], "dp", 1)), near_out, act_low, cot_low, gate_low, up_low
    )
    ff_packed = pack_ff(gate_low, up_low)
    got, x_parts, ff_both = fence(
        chips(both), to_plane(act_low, cot_low), pair_up(ff_packed[0], swap(ff_packed[1], "dp", 1))
    )
    qkv_w, seg_all, gains, x_low, cot, input_one = place_call(
        functools.partial(head_kernel, n_blk),
        (
            jax.ShapeDtypeStruct((D, 4 * HP), BF),
            jax.ShapeDtypeStruct((n_plane, small_rows, width), BF),
            jax.ShapeDtypeStruct((2, 1, D), F32),
            jax.ShapeDtypeStruct((own, D), BF),
            jax.ShapeDtypeStruct((own, D), BF),
            jax.ShapeDtypeStruct((own, D), BF),
        ),
        ids,
        *got,
        *x_parts,
        name="head",
        scratch=[pltpu.VMEM((n_plane, small_rows, width), BF)],
    )
    gain_one, gain_two = gains[0, 0], gains[1, 0]
    seg_all = seg_all[:, 2 : 2 + seg_rows].reshape(n_plane, -1)[:, : 2 * span].reshape(2, n_blk, 2, span)
    seg_seq = lax.dynamic_index_in_dim(seg_all, my_seq & 1, 0, keepdims=False)
    seg_seq = lax.dynamic_index_in_dim(seg_seq, my_seq >> 1, 1, keepdims=False)
    chunks = seg_seq.astype(jnp.int32).reshape(n_blk * n_head, tok)

    def chunk_ids(sub_index):
        ids = []
        for core in range(2):
            for blk in range(n_blk):
                for k in range(2):
                    seq_part = 2 * (my_dp ^ core) + ((my_seq >> 1) ^ k)
                    ids.append((my_blk ^ blk) * n_head + seq_part * sub + sub_index)
        return ids

    def pos_seg(sub_index):
        ids = chunk_ids(sub_index)
        lane = jnp.arange(tok, dtype=jnp.int32)
        pos = jnp.concatenate([i * tok + lane for i in ids])
        seg = jnp.concatenate([lax.dynamic_index_in_dim(chunks, i, 0, keepdims=False) for i in ids])
        return pos, seg

    qpos, qseg = pos_seg(my_sub)
    if sub == 1:
        kpos, kseg = qpos, qseg
    else:
        every = [pos_seg(i) for i in range(sub)]
        kpos, kseg = (jnp.concatenate([e[i] for e in every]) for i in range(2))
    blocked = lambda v: v.reshape(-1, BLK)
    qb, qsb, kb, ksb = blocked(qpos), blocked(qseg), blocked(kpos), blocked(kseg)
    need = (
        (jnp.min(kb, 1)[None, :] <= jnp.max(qb, 1)[:, None])
        & (jnp.min(ksb, 1)[None, :] <= jnp.max(qsb, 1)[:, None])
        & (jnp.max(ksb, 1)[None, :] >= jnp.min(qsb, 1)[:, None])
    ).astype(jnp.int32)

    input_one, qkv_w, ff_both, cot = fence(input_one, qkv_w, ff_both, cot)
    near_one, side_one, ff_both = fence(near(input_one), across(input_one), ff_both)
    far_one, ff_got, near_one = fence(far(*near_one), chips(ff_both), near_one)
    far_one = join(far_one)
    more_one = across(*near_one)
    mine_one = [input_one, *near_one, far_one]
    all_one = fence(*mine_one, *side_one, *more_one, *across(far_one))

    def project_qkv(*values):
        shape = jax.ShapeDtypeStruct((rows, 4 * HP), BF)
        return simple_call(stack_project_kernel, shape, values, "project_qkv", 2 * rows * D * 4 * HP)

    qkv = project_qkv(*all_one, qkv_w)
    cot, *near_out = lax.optimization_barrier((cot, *near_out, all_one[-1]))[:-1]
    kv = ()
    if sub > 1:
        groups = [[s * sub + i for i in range(sub)] for s in range(4)]
        kv = (lax.all_gather(qkv[:, 2 * HP :], "head", axis=0, tiled=True, axis_index_groups=groups),)
    q_args = tuple(v.astype(F32).reshape(-1, 1, BLK) for v in (qpos, qseg, kpos, kseg))
    sharing = None if sub == 1 else [[s * sub + i for s in range(4)] for i in range(sub)]
    ff_all = jnp.stack(ff_got, 1).reshape(-1, 2 * ff_here)
    ff_all = lax.all_gather(ff_all, "head", axis=0, tiled=True, axis_index_groups=sharing)
    ff_all = ff_all.reshape(4, n_plane, share, 2 * ff_here)
    (o, lse), near_cot, far_out = fence(attend(need, qkv, *(kv or (None,)), *q_args), near(cot), far(*near_out))
    o_parts = o.reshape(2, n_blk, own, 2 * HP)
    mine_out = [output_weight, *near_out, join(far_out)]
    o_both, near_cot = fence(pair_up(o_parts[0], swap(o_parts[1], "dp", 1)), near_cot)
    o_got, side_out, near_cot, cut_cot = fence(chips(o_both), across(*mine_out), near_cot, halves(*near_cot))
    all_out = [*mine_out, *side_out]

    def out_project(*values):
        shapes = (jax.ShapeDtypeStruct((own, D), F32), jax.ShapeDtypeStruct((own, D), BF))
        kernel = functools.partial(out_project_kernel, n_blk)
        return simple_call(kernel, shapes, values, "out_project", 2 * own * D * D)

    (x_mid, input_two), side_cot = fence(
        out_project(*o_got, *all_out, x_low, gain_two[None]), across(cot, *near_cot)
    )

    def unpack_ff(value):
        shapes = (jax.ShapeDtypeStruct((D, ff_here), BF),) * 2
        return place_call(unpack_ff_kernel, shapes, ids, value, name="unpack_ff")

    def ff_part(n_mine, n_side, c_mine, c_side):
        return ff_call(n_mine, n_side, c_mine, c_side, gate_w, up_w, down_weight)

    gate_w, up_w = unpack_ff(after(ff_all, input_two))
    side_two = across(input_two)
    near_two, part_0, near_cot, cut_cot, gate_w, up_w = fence(
        near(input_two), ff_part(input_two, side_two[0], cot, side_cot[0]), near_cot, cut_cot, gate_w, up_w
    )
    more_two = across(*near_two)
    far_two, far_cot, part_1, part_2 = fence(
        far(*near_two),
        far_halves(*cut_cot),
        ff_part(near_two[0], more_two[0], near_cot[0], side_cot[1]),
        ff_part(near_two[1], more_two[1], near_cot[1], side_cot[2]),
    )
    far_two, far_cot = join(far_two), join(far_cot)
    last_two, last_cot = across(far_two, far_cot)
    side_parts = across(part_0[3], part_1[3], part_2[3])
    part_3, side_parts = fence(ff_part(far_two, last_two, far_cot, last_cot), side_parts)
    parts = [part_0, part_1, part_2, part_3]
    side_parts = [*side_parts, *across(part_3[3])]
    hidden, grad_gu = [p[0] for p in parts], [p[1] for p in parts]
    all_two = [input_two, *near_two, far_two, *side_two, *more_two, last_two]
    all_cot = [cot, *near_cot, far_cot, *side_cot, last_cot]
    local_two = [p[2] + v.astype(F32) for p, v in zip(parts, side_parts)]
    local_0, sent_two = fence(local_two[0], [v.astype(BF) for v in local_two])
    got_two = chips(sent_two)[1:]

    contract = ((0,), (0,))

    def rel_parts(mine):
        return rel_to_abs(mine, True)

    def head_sum(sent):
        return lax.psum_scatter(sent, "head", scatter_dimension=0, tiled=True)

    def owned_rows(chunks):
        if n_head != 4:
            return chunks[0].reshape(-1, chunks[0].shape[-1]).astype(F32)
        shape = jax.ShapeDtypeStruct((4 * chunks[0].shape[0], chunks[0].shape[1]), F32)
        return place_call(place_rows_kernel, shape, ids, *chunks, name="place_rows")

    def owned_columns(chunks, widths):
        if n_head != 4:
            full = rel_to_abs(jnp.moveaxis(chunks[0], 0, 1).reshape((2, n_blk, n_head) + chunks[0].shape[2:]))
            full = full.reshape(n_plane, n_rows, -1).transpose(1, 0, 2).astype(F32)
            ends = [sum(widths[: i + 1]) for i in range(len(widths))]
            return [full[:, :, e - w : e].reshape(n_rows, -1) for e, w in zip(ends, widths)]
        shapes = [jax.ShapeDtypeStruct((n_rows, n_plane * w), F32) for w in widths]
        kernel = functools.partial(place_columns_kernel, widths, len(chunks))
        return place_call(kernel, shapes, ids, *chunks, name="place_columns")

    ff_sent, down_sent = ff_weight_call(all_two, all_cot, grad_gu, hidden, n_head, n_plane)
    got_two, ff_sent, down_sent = fence(got_two, ff_sent, down_sent)
    down_mine = head_sum(down_sent)
    ff_mine = head_sum(ff_sent.reshape(D, 2 * ff_here)).reshape(n_plane, part, 2 * ff_here)

    def branch(*values):
        shapes = (
            jax.ShapeDtypeStruct((own, D), F32),
            jax.ShapeDtypeStruct((own, D), BF),
            jax.ShapeDtypeStruct((2, n_blk, own, 2 * HP), BF),
        )
        kernel = functools.partial(branch_kernel, n_blk)
        return simple_call(kernel, shapes, values, "branch", 2 * own * D * D)

    grad_mid, grad_branch, grad_o = fence(*branch(*all_out, local_0, *got_two, x_mid, cot, gain_two[None]))

    def back_project(transposed, *values):
        shapes = tuple(jax.ShapeDtypeStruct((n_blk, own, D), t) for t in (F32, BF))
        kernel = functools.partial(back_project_kernel, transposed)
        return simple_call(kernel, shapes, values, "back_project", 2 * rows * D * values[-1].size // D)

    do_both, hidden = fence(pair_up(grad_o[0], swap(grad_o[1], "dp", 1)), hidden)
    out_own, out_other = back_project(False, *hidden, down_weight)
    do_got, out_own, out_side, grad_branch = fence(chips(do_both), out_own, swap(out_other, "dp", 1), grad_branch)
    grad_o = jnp.stack(do_got, 1).reshape(rows, 2 * HP)
    line = n_head == 4
    no_step = lambda *v: ()
    step = line_step if line else no_step
    back = attend_back(need, qkv, *(kv or (None,)), *q_args, o, lse, grad_o)
    dqkv, near_branch, out_own, out_side = fence(back, near(grad_branch), out_own, out_side)
    local_out = [out_own[k] + out_side[k].astype(F32) for k in range(n_blk)]
    if sub > 1:
        dkv = lax.psum_scatter(dqkv[1], "head", scatter_dimension=0, tiled=True, axis_index_groups=groups)
        dqkv = [join([dqkv[0], dkv], 1)]
    dqkv = dqkv[0]
    qkv_grad, far_branch, dqkv, ff_mine, local_out, far_sum = fence(
        qkv_weight_call(all_one, dqkv, n_head, n_plane), far(*near_branch), dqkv, ff_mine, local_out, sum_far(local_out)
    )
    qkv_mine = head_sum(qkv_grad.reshape(D, 4 * HD)).reshape(n_plane, part, 4 * HD)
    mine_branch = [grad_branch, *near_branch, join(far_branch)]
    ff_rel = rel_parts(ff_mine)
    (one_own, one_other), side_branch, ff_both, got_out, local_out_0 = fence(
        back_project(True, dqkv, qkv_w),
        across(*mine_branch),
        pair_up(ff_rel[0], swap(ff_rel[1], "dp", 1)),
        sum_near(local_out, *far_sum),
        local_out[0],
    )
    block_out = (x_mid + local_out_0 + sum(g.astype(F32) for g in got_out)).astype(BF)

    def out_weights(*values):
        rows_per = values[1].shape[0]
        lanes = pl.BlockSpec((rows_per, 384), lambda j: (0, j))
        return pl.pallas_call(
            functools.partial(out_weight_kernel, n_plane),
            grid=(D // 384,),
            out_shape=jax.ShapeDtypeStruct((2 * HD, D), BF),
            in_specs=[pl.BlockSpec(values[0].shape, lambda j: (0, 0), pipeline_mode=pl.Buffered(1))] + [lanes] * n_plane,
            out_specs=pl.BlockSpec((2 * HD, 384), lambda j: (0, j)),
            compiler_params=pltpu.CompilerParams(vmem_limit_bytes=48 << 20),
            cost_estimate=small_cost(flops=4 * rows * D * 2 * HP, transcendentals=0, bytes_accessed=9 << 20),
            name="out_weight",
        )(*values)

    one_side = swap(one_other, "dp", 1)
    local_one = [one_own[k] + one_side[k].astype(F32) for k in range(n_blk)]
    ff_got, out_grad, local_0, sent_one, down_mine = fence(
        chips(ff_both),
        out_weights(o, *mine_branch, *side_branch),
        local_one[0],
        [v.astype(BF) for v in local_one],
        down_mine,
    )
    out_mine = head_sum(out_grad)
    late_down = lax.all_gather(down_mine, "head", axis=0)
    ff_rows = jnp.stack(ff_got, 1).reshape(ff_mine.shape)
    ff_0 = step(ff_rows, ff_rows)
    got_one, ff_1, ff_0, qkv_mine, out_mine, block_out = fence(
        chips(sent_one)[1:], step(*ff_0), ff_0, qkv_mine, out_mine, block_out
    )
    normed, factor = normalize(x_low.astype(F32))
    grad_in_one = local_0 + sum(g.astype(F32) for g in got_one)
    grad_input = (grad_mid + norm_back(grad_in_one, gain_one, normed, factor)).astype(BF)
    qkv_rel = rel_parts(qkv_mine)
    qkv_both = pair_up(qkv_rel[0], swap(qkv_rel[1], "dp", 1))
    qkv_rows = chips(qkv_both)
    ff_2, grad_input, block_out = fence(step(*ff_1), grad_input, block_out)
    out_rows = out_mine.reshape(part, -1, 4 * HD).transpose(1, 0, 2) if line else out_mine
    late = join([jnp.stack(qkv_rows, 1).reshape(-1, 4 * HD), out_rows.reshape(-1, 4 * HD)])
    late = lax.all_gather(late, "head", axis=0)
    grad_input = from_plane(grad_input)
    block_out = from_plane(block_out)
    grad_down = late_down.reshape(-1, D).astype(F32)
    if line:
        ff_chunks = [ff_2[0], ff_1[0], ff_0[0], ff_rows, ff_0[1], ff_1[1], ff_2[1]]
    else:
        ff_chunks = [lax.all_gather(ff_rows, "head", axis=0)]
    grad_gate_w, grad_up_w = owned_columns(ff_chunks, (ff_here, ff_here))
    def gain_grad(gain, *pairs):
        return sum(jnp.sum(w.astype(F32) * g, -1) for w, g in pairs) / gain.astype(F32)

    if line:
        matrices = (query_weight, key_weight, value_weight)
        shapes = [jax.ShapeDtypeStruct(w.shape, F32) for w in (*matrices, output_weight)]
        shapes.append(jax.ShapeDtypeStruct((1, n_rows), F32))
        values = (late, *matrices, norm_gain_one.astype(F32)[None])
        grad_query, grad_key, grad_value, grad_out, grad_gain_one = place_call(last_kernel, shapes, ids, *values, name="last")
        grad_gain_one = grad_gain_one[0]
    else:
        late_qkv = late[:, : n_plane * part].reshape(n_head, n_plane, part, 4 * HD)
        late_out = late[:, n_plane * part :].reshape(n_head, part, D)
        grad_query, grad_key, grad_value = owned_columns([late_qkv], (2 * HD, HD, HD))
        grad_out = owned_rows([late_out])
        grad_gain_one = gain_grad(
            norm_gain_one, (query_weight, grad_query), (key_weight, grad_key), (value_weight, grad_value)
        )
    grad_gain_two = gain_grad(norm_gain_two, (gate_weight, grad_gate_w), (up_weight, grad_up_w))
    return (
        block_out[:, None],
        grad_input[:, None],
        grad_gain_one,
        grad_query,
        grad_key,
        grad_value,
        grad_out,
        grad_gain_two,
        grad_gate_w,
        grad_up_w,
        grad_down,
    )


def solution(mesh):
    tokens = P(None, "dp", ("blk", "head"), None)
    vector = P(("dp", "blk"))
    matrix = P(("dp", "blk"), None)
    return jax.shard_map(
        per_device,
        mesh=mesh,
        in_specs=(
            tokens,
            P(None, "dp", "blk"),
            tokens,
            vector,
            matrix,
            matrix,
            matrix,
            matrix,
            vector,
            matrix,
            matrix,
            matrix,
        ),
        out_specs=(tokens, tokens, vector, matrix, matrix, matrix, matrix, vector, matrix, matrix, matrix),
        check_vma=False,
    )
```
